32 devices in a mesh: dp: 8 (over z, x), mp: 4 (over y, core).
Axes of the slice: x: 2, y: 2, z: 4, core: 2. Of those that a mesh axis runs over, the one named last changes fastest.
Arguments:
- images: bfloat16 [128, 196, 512], P('dp'), may hold values from -6 to 6
- cotangent: bfloat16 [128, 196, 512], P('dp'), may hold values from -6 to 6
- qkv_weight: float32 [1536, 512], P(('mp', 'dp')), may hold values from -0.25 to 0.25
- proj_weight: float32 [512, 512], P(('mp', 'dp')), may hold values from -0.5 to 0.5
- expand_weight: float32 [2048, 512], P(('mp', 'dp')), may hold values from -0.25 to 0.25
- contract_weight: float32 [2048, 512], P(('mp', 'dp')), may hold values from -0.125 to 0.125
- qkv_moment: float32 [1536, 512], P(('mp', 'dp')), may hold values from -256 to 256
- proj_moment: float32 [512, 512], P(('mp', 'dp')), may hold values from -256 to 256
- expand_moment: float32 [2048, 512], P(('mp', 'dp')), may hold values from -192 to 192
- contract_moment: float32 [2048, 512], P(('mp', 'dp')), may hold values from -384 to 384
- vectors: float32 [6, 512], replicated, may hold values from -1.2 to 2.2
- qv_bias: float32 [2, 512], P(None, 'mp'), may hold values from -3 to 3
- expand_bias: float32 [2048], P('mp'), may hold values from -3 to 3
- rel_table: float32 [169, 16], P(None, 'mp'), may hold values from -3 to 334
- vectors_first: float32 [6, 512], replicated, may hold values from -80 to 80
- vectors_second: float32 [6, 512], replicated, may hold values from 7.5264 to 30.1056
- qv_first: float32 [2, 512], P(None, 'mp'), may hold values from -40 to 40
- qv_second: float32 [2, 512], P(None, 'mp'), may hold values from 2.5088 to 10.0352
- expand_bias_first: float32 [2048], P('mp'), may hold values from -20 to 20
- expand_bias_second: float32 [2048], P('mp'), may hold values from 0.75264 to 2.5088
- table_first: float32 [169, 16], P(None, 'mp'), may hold values from -6 to 6
- table_second: float32 [169, 16], P(None, 'mp'), may hold values from 0.0075264 to 0.0301056
- region_ids: int32 [14, 14], replicated, may hold values from 0 to 3
- pos_index: int32 [49, 49], replicated, may hold values from 0 to 168
- image_counts: int32 [8], P('dp'), may hold values from 1 to 16, as said below
Outputs:
- block_out: bfloat16 [128, 196, 512], P('dp')
- input_grad: bfloat16 [128, 196, 512], P('dp')
- qkv_grad: float32 [1536, 512], P(('mp', 'dp'))
- proj_grad: float32 [512, 512], P(('mp', 'dp'))
- expand_grad: float32 [2048, 512], P(('mp', 'dp'))
- contract_grad: float32 [2048, 512], P(('mp', 'dp'))
- vectors_grad: float32 [6, 512], replicated
- qv_grad: float32 [2, 512], P(None, 'mp')
- expand_bias_grad: float32 [2048], P('mp')
- table_grad: float32 [169, 16], P(None, 'mp')
- qkv_step: float32 [1536, 512], P(('mp', 'dp'))
- proj_step: float32 [512, 512], P(('mp', 'dp'))
- expand_step: float32 [2048, 512], P(('mp', 'dp'))
- contract_step: float32 [2048, 512], P(('mp', 'dp'))
- qkv_moment_new: float32 [1536, 512], P(('mp', 'dp'))
- proj_moment_new: float32 [512, 512], P(('mp', 'dp'))
- expand_moment_new: float32 [2048, 512], P(('mp', 'dp'))
- contract_moment_new: float32 [2048, 512], P(('mp', 'dp'))
- vectors_step: float32 [6, 512], replicated
- qv_step: float32 [2, 512], P(None, 'mp')
- expand_bias_step: float32 [2048], P('mp')
- table_step: float32 [169, 16], P(None, 'mp')
- vectors_first_new: float32 [6, 512], replicated
- vectors_second_new: float32 [6, 512], replicated
- qv_first_new: float32 [2, 512], P(None, 'mp')
- qv_second_new: float32 [2, 512], P(None, 'mp')
- expand_bias_first_new: float32 [2048], P('mp')
- expand_bias_second_new: float32 [2048], P('mp')
- table_first_new: float32 [169, 16], P(None, 'mp')
- table_second_new: float32 [169, 16], P(None, 'mp')
The draws below stay inside these ranges and needn't reach their ends.
Inputs may be any that keep to these rules, and one draw needn't show every extreme that they name: `image_counts`: some index of dp has all 16 images live.
All inputs are finite; a program needn't handle non-finite values.
Results may differ from the reference program's by a relative error of at most 0.018.
The reference program's roundings to bfloat16 on the way count: a program that leaves them out, or rounds other values in their place, can miss the bound.
Values may be sent and summed in bfloat16 or wider, within the bound.
A program may use at most 192 MiB of HBM per device.

```python
import math
import jax
import jax.numpy as jnp
from jax import lax

C = 512
HEADS = 16
HD = 32
FF = 2048
WIN = 7
SIDE = 14
SHIFT = 3
NS_ITERS = 5
IMG_DEV = 16
WTOK = 49
TABLE = 169
IMAGES = 128
TOKENS = 25088


def draw_vectors(key, part):
    base = jnp.clip(0.35 * jax.random.normal(key, (6, C), jnp.float32), -1.2, 1.2)
    offsets = jnp.array([1.0, 0.0, 1.0, 0.0, 0.0, 0.0], jnp.float32)[:, None]
    return base + offsets


def draw_rel_table(key, part):
    key_base = jax.random.fold_in(key, 0)
    return jnp.clip(jax.random.normal(key_base, (TABLE, HEADS), jnp.float32), -3.0, 3.0)


def draw_image_counts(key, part):
    key_counts, key_chosen = jax.random.split(key)
    devices_dp = IMAGES // IMG_DEV
    counts = jax.random.randint(key_counts, (devices_dp,), 1, IMG_DEV + 1)
    chosen = jax.random.randint(key_chosen, (), 0, devices_dp)
    return jnp.where(jnp.arange(devices_dp) == chosen, IMG_DEV, counts).astype(jnp.int32)


def plant(entries, own_key, low, top_value):
    longest = entries.shape.index(max(entries.shape))
    spots = []
    for shift in (0, 1):
        where = [jax.random.randint(jax.random.fold_in(own_key, axis), (), 0, length) for axis, length in enumerate(entries.shape)]
        where[longest] = (where[longest] + shift) % entries.shape[longest]
        spots.append(tuple(where))
    return entries.at[spots[0]].set(low).at[spots[1]].set(top_value)


def level_of(stream_key, shape, cuts, least, largest):
    loudness, own = 1.0, jax.random.fold_in(stream_key, 6)
    for position, blocks in cuts:
        draws = jnp.exp(jax.random.uniform(jax.random.fold_in(own, position), (blocks,), jnp.float32, least / len(cuts), largest / len(cuts)))
        loudness = loudness * jnp.repeat(draws, shape[position] // blocks).reshape([-1 if axis == position else 1 for axis in range(len(shape))])
    return loudness


def gaussian(rng, dims, width, most, cuts=(), kind=jnp.bfloat16):
    factor_of = level_of(rng, dims, cuts, -0.22, 0.18) if cuts else 1.0
    entries = jax.random.normal(rng, dims, jnp.float32) * width * factor_of
    return jnp.minimum(jnp.maximum(entries, -most), most).astype(kind)


def setup_inputs(seed: int = 0) -> dict:
    splits = jax.random.split(jax.random.key(seed), 26)
    return {
        "images": gaussian(splits[0], (IMAGES, SIDE * SIDE, C), 1.0, 6.0, ((0, 8),)),
        "cotangent": gaussian(splits[1], (IMAGES, SIDE * SIDE, C), 1.0, 6.0, ((0, 8),)),
        "qkv_weight": gaussian(splits[2], (3 * C, C), C ** -0.5, 0.25, ((0, 32),), jnp.float32),
        "proj_weight": gaussian(splits[3], (C, C), (C // 4) ** -0.5, 0.5, ((0, 32),), jnp.float32),
        "expand_weight": gaussian(splits[4], (FF, C), C ** -0.5, 0.25, ((0, 32),), jnp.float32),
        "contract_weight": gaussian(splits[5], (FF, C), FF ** -0.5, 0.125, ((0, 32),), jnp.float32),
        "qkv_moment": gaussian(splits[6], (3 * C, C), (0.25 * TOKENS ** 0.5), 256.0, ((0, 32),), jnp.float32),
        "proj_moment": gaussian(splits[7], (C, C), (0.25 * TOKENS ** 0.5), 256.0, ((0, 32),), jnp.float32),
        "expand_moment": gaussian(splits[8], (FF, C), (0.2 * TOKENS ** 0.5), 192.0, ((0, 32),), jnp.float32),
        "contract_moment": gaussian(splits[9], (FF, C), (0.4 * TOKENS ** 0.5), 384.0, ((0, 32),), jnp.float32),
        "vectors": draw_vectors(jax.random.fold_in(splits[25], 71), 0),
        "qv_bias": gaussian(splits[11], (2, C), 0.5, 3.0, ((1, 4),), jnp.float32),
        "expand_bias": gaussian(splits[12], (FF,), 0.5, 3.0, ((0, 4),), jnp.float32),
        "rel_table": draw_rel_table(jax.random.fold_in(splits[25], 71), 0),
        "vectors_first": gaussian(splits[14], (6, C), (0.08 * TOKENS ** 0.5), 80.0, (), jnp.float32),
        "vectors_second": jnp.clip(jnp.exp(jax.random.uniform(splits[15], (6, C), jnp.float32, math.log(7.5264), math.log(30.1056))), 7.5264, 30.1056),
        "qv_first": gaussian(splits[16], (2, C), (0.04 * TOKENS ** 0.5), 40.0, ((1, 4),), jnp.float32),
        "qv_second": jnp.clip(jnp.exp(math.log(10.0352) - 1.3862944 * jax.random.uniform(splits[17], (2, C), jnp.float32) ** level_of(splits[17], (2, C), ((1, 4),), -0.2, 0.2)), 2.5088, 10.0352),
        "expand_bias_first": gaussian(splits[18], (FF,), (0.02 * TOKENS ** 0.5), 20.0, ((0, 4),), jnp.float32),
        "expand_bias_second": jnp.clip(jnp.exp(math.log(2.5088) - 1.2039728 * jax.random.uniform(splits[19], (FF,), jnp.float32) ** level_of(splits[19], (FF,), ((0, 4),), -0.2, 0.2)), 0.75264, 2.5088),
        "table_first": gaussian(splits[20], (TABLE, HEADS), (0.003 * TOKENS ** 0.5), 6.0, ((1, 4),), jnp.float32),
        "table_second": jnp.clip(jnp.exp(math.log(0.0301056) - 1.3862944 * jax.random.uniform(splits[21], (TABLE, HEADS), jnp.float32) ** level_of(splits[21], (TABLE, HEADS), ((1, 4),), -0.2, 0.2)), 0.0075264, 0.0301056),
        "region_ids": plant(jax.random.randint(splits[22], (SIDE, SIDE), 0, 4), jax.random.fold_in(splits[22], 1), 0, 3).astype(jnp.int32),
        "pos_index": plant(jax.random.randint(splits[23], (WTOK, WTOK), 0, TABLE), jax.random.fold_in(splits[23], 1), 0, TABLE - 1).astype(jnp.int32),
        "image_counts": draw_image_counts(jax.random.fold_in(splits[25], 71), 0),
    }


@jax.custom_vjp
def low(v):
    return lax.optimization_barrier(v.astype(jnp.bfloat16)).astype(jnp.float32)

@jax.custom_vjp
def low_back(v):
    return v

def low_keep(v):
    return (low(v), None)

def low_pass(kept, grad):
    return (grad,)

def back_keep(v):
    return (v, None)

def back_low(kept, grad):
    return (low(grad),)
low.defvjp(low_keep, low_pass)
low_back.defvjp(back_keep, back_low)
norm_eps = 1e-05
ns_eps = 1e-07
coef_a = 3.4445
coef_b = -4.775
coef_c = 2.0315
muon_rate = 0.3
muon_decay = 0.1
muon_beta = 0.95
adam_rate = 0.1
adam_one = 0.9
adam_two = 0.999
adam_eps = 1e-08
adam_step = 4
mask_value = -100.0
highest = lax.Precision.HIGHEST

def matmul(left_side, right_side):
    return jnp.matmul(left_side, right_side, precision=highest)

def layer_norm(values, gain, offset):
    mean_value = lax.optimization_barrier(jnp.mean(values, axis=-1, keepdims=True))
    centered = values - mean_value
    variance = lax.optimization_barrier(jnp.mean(centered * centered, axis=-1, keepdims=True))
    return centered * lax.rsqrt(variance + norm_eps) * gain + offset

def gelu_value(values):
    return 0.5 * values * (1.0 + lax.erf(values * (1.0 / math.sqrt(2.0))))

def to_windows(field_values):
    image_total = field_values.shape[0]
    channels = field_values.shape[-1]
    blocks = SIDE // WIN
    grid_values = field_values.reshape(image_total, SIDE, SIDE, channels)
    grid_values = jnp.roll(grid_values, (-SHIFT, -SHIFT), axis=(1, 2))
    grid_values = grid_values.reshape(image_total, blocks, WIN, blocks, WIN, channels)
    grid_values = grid_values.transpose(0, 1, 3, 2, 4, 5)
    return grid_values.reshape(image_total * blocks * blocks, WIN * WIN, channels)

def from_windows(window_values, image_total):
    channels = window_values.shape[-1]
    blocks = SIDE // WIN
    grid_values = window_values.reshape(image_total, blocks, blocks, WIN, WIN, channels)
    grid_values = grid_values.transpose(0, 1, 3, 2, 4, 5).reshape(image_total, SIDE, SIDE, channels)
    grid_values = jnp.roll(grid_values, (SHIFT, SHIFT), axis=(1, 2))
    return grid_values.reshape(image_total, SIDE * SIDE, channels)

def window_layer(tokens, qkv_weight, proj_weight, expand_weight, contract_weight, vectors, qv_bias, expand_bias, rel_table, pos_index, window_mask):
    image_total = tokens.shape[0]
    span = WIN * WIN
    window_count = image_total * (SIDE // WIN) ** 2
    first_in = low(layer_norm(tokens, vectors[0], vectors[1]))
    window_in = to_windows(first_in).reshape(window_count * span, C)
    joint_bias = jnp.stack([qv_bias[0].reshape(HEADS, HD), jnp.zeros((HEADS, HD), jnp.float32), qv_bias[1].reshape(HEADS, HD)], axis=1).reshape(3 * C)
    qkv_all = low(low_back(matmul(window_in, low(qkv_weight).T) + joint_bias)).reshape(window_count, span, HEADS, 3, HD)
    queries = qkv_all[:, :, :, 0]
    keys_part = qkv_all[:, :, :, 1]
    values_part = qkv_all[:, :, :, 2]
    raw_scores = jnp.einsum('wihd,wjhd->whij', queries, keys_part, precision=highest) * (1.0 / math.sqrt(HD))
    pos_bias = rel_table[pos_index].transpose(2, 0, 1)
    scores = raw_scores.reshape(image_total, window_count // image_total, HEADS, span, span)
    scores = scores + pos_bias[None, None] + window_mask[None, :, None]
    scores = low_back(scores.reshape(window_count, HEADS, span, span))
    row_top = lax.optimization_barrier(jnp.max(scores, axis=-1, keepdims=True))
    exponent = jnp.exp(scores - row_top)
    attention = low(exponent / lax.optimization_barrier(jnp.sum(exponent, axis=-1, keepdims=True)))
    attended = jnp.einsum('whij,wjhd->wihd', attention, values_part, precision=highest)
    attended = low(low_back(attended)).reshape(window_count * span, C)
    projected = low_back(matmul(attended, low(proj_weight)))
    middle = tokens + (from_windows(projected.reshape(window_count, span, C), image_total) + vectors[4])
    second_in = low(layer_norm(middle, vectors[2], vectors[3])).reshape(image_total * SIDE * SIDE, C)
    hidden = low_back(matmul(second_in, low(expand_weight).T) + expand_bias)
    acted = low(gelu_value(hidden))
    mlp_out = low_back(matmul(acted, low(contract_weight)))
    return middle + (mlp_out.reshape(image_total, SIDE * SIDE, C) + vectors[5])

def orthogonalize(matrix):
    norm_value = jnp.sqrt(jnp.sum(matrix * matrix))
    iterate = matrix / (norm_value + ns_eps)
    for iteration in range(NS_ITERS):
        gram = matmul(iterate.T, iterate)
        poly = coef_b * gram + coef_c * matmul(gram, gram)
        iterate = coef_a * iterate + matmul(iterate, poly)
    return iterate

def adam_update(grad_sum, first_moment, second_moment):
    first_new = adam_one * first_moment + (1.0 - adam_one) * grad_sum
    second_new = adam_two * second_moment + (1.0 - adam_two) * grad_sum * grad_sum
    first_hat = first_new / (1.0 - adam_one ** adam_step)
    second_hat = second_new / (1.0 - adam_two ** adam_step)
    return (-adam_rate * first_hat / (jnp.sqrt(second_hat) + adam_eps), first_new, second_new)

def reference(images, cotangent, qkv_weight, proj_weight, expand_weight, contract_weight, qkv_moment, proj_moment, expand_moment, contract_moment, vectors, qv_bias, expand_bias, rel_table, vectors_first, vectors_second, qv_first, qv_second, expand_bias_first, expand_bias_second, table_first, table_second, region_ids, pos_index, image_counts):
    window_regions = to_windows(region_ids.reshape(1, SIDE * SIDE, 1))[:, :, 0]
    window_mask = jnp.where(window_regions[:, :, None] != window_regions[:, None, :], mask_value, 0.0).astype(jnp.float32)
    groups = IMAGES // IMG_DEV
    live = jnp.arange(IMG_DEV, dtype=jnp.int32)[None, :] < image_counts[:, None]
    params = (qkv_weight, proj_weight, expand_weight, contract_weight, vectors, qv_bias, expand_bias, rel_table)

    def closed_layer(tokens, weight_one, weight_two, weight_three, weight_four, vector_rows, bias_qv, bias_expand, table_rows):
        return window_layer(tokens, weight_one, weight_two, weight_three, weight_four, vector_rows, bias_qv, bias_expand, table_rows, pos_index, window_mask)

    def group_step(totals, group_data):
        image_group, cot_group, live_group = group_data
        outputs, pullback = jax.vjp(closed_layer, image_group.astype(jnp.float32), *params)
        live_float = live_group.astype(jnp.float32)[:, None, None]
        grads = pullback(cot_group.astype(jnp.float32) * live_float)
        new_totals = tuple((total + grad_part for total, grad_part in zip(totals, grads[1:])))
        block_low = jnp.where(live_group[:, None, None], outputs, 0.0).astype(jnp.bfloat16)
        return (new_totals, (block_low, grads[0].astype(jnp.bfloat16)))
    initial = tuple((jnp.zeros_like(parameter) for parameter in params))
    stacked = (images.reshape(groups, IMG_DEV, SIDE * SIDE, C), cotangent.reshape(groups, IMG_DEV, SIDE * SIDE, C), live)
    totals, (block_parts, input_parts) = lax.scan(group_step, initial, stacked)
    block_out = block_parts.reshape(IMAGES, SIDE * SIDE, C)
    input_grad = input_parts.reshape(IMAGES, SIDE * SIDE, C)
    qkv_grad, proj_grad, expand_grad, contract_grad, vectors_grad, qv_grad, expand_bias_grad, table_grad = totals
    factors = (math.sqrt(3.0), 1.0, math.sqrt(max(1.0, FF / C)), 1.0)
    matrices = (qkv_weight, proj_weight, expand_weight, contract_weight)
    moments = (qkv_moment, proj_moment, expand_moment, contract_moment)
    matrix_grads = (qkv_grad, proj_grad, expand_grad, contract_grad)
    new_steps = []
    new_moments = []
    for weight, moment, grad_part, factor in zip(matrices, moments, matrix_grads, factors):
        buffer_new = muon_beta * moment + grad_part
        nesterov = grad_part + muon_beta * buffer_new
        ortho = orthogonalize(nesterov)
        new_steps.append(-muon_rate * (muon_decay * weight + factor * ortho))
        new_moments.append(buffer_new)
    vectors_step, vectors_first_new, vectors_second_new = adam_update(vectors_grad, vectors_first, vectors_second)
    qv_step, qv_first_new, qv_second_new = adam_update(qv_grad, qv_first, qv_second)
    expand_bias_step, expand_bias_first_new, expand_bias_second_new = adam_update(expand_bias_grad, expand_bias_first, expand_bias_second)
    table_step, table_first_new, table_second_new = adam_update(table_grad, table_first, table_second)
    return (block_out, input_grad, qkv_grad, proj_grad, expand_grad, contract_grad, vectors_grad, qv_grad, expand_bias_grad, table_grad, new_steps[0], new_steps[1], new_steps[2], new_steps[3], new_moments[0], new_moments[1], new_moments[2], new_moments[3], vectors_step, qv_step, expand_bias_step, table_step, vectors_first_new, vectors_second_new, qv_first_new, qv_second_new, expand_bias_first_new, expand_bias_second_new, table_first_new, table_second_new)
```

```python
import math

import jax
import jax.numpy as jnp
from jax import lax
from jax.sharding import PartitionSpec as P

C = 512
HD = 32
FF = 2048
WIN = 7
SIDE = 14
SHIFT = 3
NS_ITERS = 5
IMG_DEV = 16
TABLE = 169


norm_eps = 1e-05
ns_eps = 1e-07
coef_a = 3.4445
coef_b = -4.775
coef_c = 2.0315
muon_rate = 0.3
muon_decay = 0.1
muon_beta = 0.95
adam_rate = 0.1
adam_one = 0.9
adam_two = 0.999
adam_eps = 1e-08
adam_step = 4
mask_value = -100.0
highest = lax.Precision.HIGHEST
contract_rows = (((0,), (0,)), ((), ()))
contract_cols = (((1,), (1,)), ((), ()))


def to_windows(field_values):
    image_total = field_values.shape[0]
    channels = field_values.shape[-1]
    blocks = SIDE // WIN
    grid_values = field_values.reshape(image_total, SIDE, SIDE, channels)
    grid_values = jnp.roll(grid_values, (-SHIFT, -SHIFT), axis=(1, 2))
    grid_values = grid_values.reshape(image_total, blocks, WIN, blocks, WIN, channels)
    grid_values = grid_values.transpose(0, 1, 3, 2, 4, 5)
    return grid_values.reshape(image_total * blocks * blocks, WIN * WIN, channels)


def from_windows(window_values, image_total):
    channels = window_values.shape[-1]
    blocks = SIDE // WIN
    grid_values = window_values.reshape(image_total, blocks, blocks, WIN, WIN, channels)
    grid_values = grid_values.transpose(0, 1, 3, 2, 4, 5).reshape(image_total, SIDE, SIDE, channels)
    grid_values = jnp.roll(grid_values, (SHIFT, SHIFT), axis=(1, 2))
    return grid_values.reshape(image_total, SIDE * SIDE, channels)


def normalize(values):
    mean_value = jnp.mean(values, axis=-1, keepdims=True)
    centered = values - mean_value
    variance = jnp.mean(centered * centered, axis=-1, keepdims=True)
    inv_scale = lax.rsqrt(variance + norm_eps)
    return (centered * inv_scale, inv_scale)


def normalize_back(grad_norm, normed, inv_scale, gain):
    scaled = grad_norm * gain
    return inv_scale * (
        scaled
        - jnp.mean(scaled, axis=-1, keepdims=True)
        - normed * jnp.mean(scaled * normed, axis=-1, keepdims=True)
    )


def gelu_value(values):
    return 0.5 * values * (1.0 + lax.erf(values * (1.0 / math.sqrt(2.0))))


def gelu_slope(values):
    return 0.5 * (1.0 + lax.erf(values * (1.0 / math.sqrt(2.0)))) + values * jnp.exp(
        -0.5 * values * values
    ) * (1.0 / math.sqrt(2.0 * math.pi))


def split_low(values):
    high = lax.reduce_precision(values, exponent_bits=8, mantissa_bits=7)
    return high.astype(jnp.bfloat16), (values - high).astype(jnp.bfloat16)


def dot_three(left, right):
    left_high, left_rest = left
    right_high, right_rest = right
    wide = dict(preferred_element_type=jnp.float32)
    return (
        jnp.dot(left_rest, right_high, **wide)
        + jnp.dot(left_high, right_rest, **wide)
        + jnp.dot(left_high, right_high, **wide)
    )


def newton_schulz(gram):
    width = gram.shape[0]
    eye = jnp.eye(width, dtype=jnp.float32)
    norm_value = jnp.sqrt(jnp.sum(gram * eye)) + ns_eps
    gram = gram / (norm_value * norm_value)
    total = None
    for iteration in range(NS_ITERS):
        parts = split_low(gram)
        square = dot_three(parts, parts)
        poly = coef_a * eye + (coef_b * gram + coef_c * square)
        poly_parts = split_low(poly)
        total = poly if total is None else dot_three(split_low(total), poly_parts)
        if iteration + 1 < NS_ITERS:
            half = dot_three(parts, poly_parts)
            gram = dot_three(split_low(half), poly_parts)
    return total / norm_value


def adam_update(grad_sum, first_moment, second_moment):
    first_new = adam_one * first_moment + (1.0 - adam_one) * grad_sum
    second_new = adam_two * second_moment + (1.0 - adam_two) * grad_sum * grad_sum
    first_hat = first_new / (1.0 - adam_one**adam_step)
    second_hat = second_new / (1.0 - adam_two**adam_step)
    return (-adam_rate * first_hat / (jnp.sqrt(second_hat) + adam_eps), first_new, second_new)


def layer_pass(
    image_block,
    cot_block,
    live_block,
    gathered,
    vectors,
    qv_bias,
    expand_bias,
    pos_bias,
    window_mask,
    onehot,
):
    qkv_local, proj_local, expand_local, contract_local = gathered
    image_total = image_block.shape[0]
    heads_here = pos_bias.shape[0]
    wide = heads_here * HD
    span = WIN * WIN
    window_count = image_total * (SIDE // WIN) ** 2
    token_count = image_total * SIDE * SIDE
    score_scale = 1.0 / math.sqrt(HD)
    tokens_in = image_block.astype(jnp.float32)
    normed_one, inv_one = normalize(tokens_in)
    first_in = (normed_one * vectors[0] + vectors[1]).astype(jnp.bfloat16)
    window_in = to_windows(first_in).reshape(window_count * span, C)
    zero_bias = jnp.zeros((heads_here, HD), jnp.float32)
    joint_bias = jnp.stack(
        [qv_bias[0].reshape(heads_here, HD), zero_bias, qv_bias[1].reshape(heads_here, HD)], axis=1
    ).reshape(3 * wide)
    projected_qkv = lax.dot_general(
        window_in, qkv_local, contract_cols, preferred_element_type=jnp.float32
    )
    qkv_low = (
        (projected_qkv + joint_bias)
        .astype(jnp.bfloat16)
        .reshape(window_count, span, heads_here, 3, HD)
    )
    queries = qkv_low[:, :, :, 0]
    keys_part = qkv_low[:, :, :, 1]
    values_part = qkv_low[:, :, :, 2]

    def score_block():
        raw_scores = (
            jnp.einsum("wihd,wjhd->whij", queries, keys_part, preferred_element_type=jnp.float32)
            * score_scale
        )
        raw_scores = raw_scores.reshape(
            image_total, window_count // image_total, heads_here, span, span
        )
        raw_scores = raw_scores + pos_bias[None, None] + window_mask[None, :, None]
        return raw_scores.reshape(window_count, heads_here, span, span)

    scores = score_block()
    row_top = jnp.max(scores, axis=-1, keepdims=True)
    exponent = jnp.exp(scores - row_top)
    row_total = jnp.sum(exponent, axis=-1, keepdims=True)
    attention = exponent / row_total
    log_total = row_top + jnp.log(row_total)
    attended = jnp.einsum(
        "whij,wjhd->wihd",
        attention.astype(jnp.bfloat16),
        values_part,
        preferred_element_type=jnp.float32,
    )
    attended = attended.astype(jnp.bfloat16).reshape(window_count * span, wide)
    proj_part = jnp.dot(attended, proj_local, preferred_element_type=jnp.float32)
    projected = proj_part
    middle = tokens_in + (
        from_windows(projected.reshape(window_count, span, C), image_total) + vectors[4]
    )
    normed_two, inv_two = normalize(middle)
    second_in = (normed_two * vectors[2] + vectors[3]).astype(jnp.bfloat16).reshape(token_count, C)
    hidden = (
        lax.dot_general(second_in, expand_local, contract_cols, preferred_element_type=jnp.float32)
        + expand_bias
    )
    acted = gelu_value(hidden).astype(jnp.bfloat16)
    mlp_part = jnp.dot(acted, contract_local, preferred_element_type=jnp.float32)
    mlp_out = mlp_part
    block_out = middle + (mlp_out.reshape(image_total, SIDE * SIDE, C) + vectors[5])
    block_low = jnp.where(live_block[:, None, None], block_out, 0.0).astype(jnp.bfloat16)
    grad_out = cot_block.astype(jnp.float32) * live_block.astype(jnp.float32)[:, None, None]
    out_low = grad_out.astype(jnp.bfloat16).reshape(token_count, C)
    contract_grad = lax.dot_general(
        acted, out_low, contract_rows, preferred_element_type=jnp.float32
    )
    acted_grad = lax.dot_general(
        out_low, contract_local, contract_cols, preferred_element_type=jnp.float32
    )
    hidden_grad = (acted_grad * gelu_slope(hidden)).astype(jnp.bfloat16)
    expand_bias_grad = jnp.sum(hidden_grad.astype(jnp.float32), axis=0)
    expand_grad = lax.dot_general(
        hidden_grad, second_in, contract_rows, preferred_element_type=jnp.float32
    )
    second_part = jnp.dot(hidden_grad, expand_local, preferred_element_type=jnp.float32)
    second_grad = second_part.reshape(image_total, SIDE * SIDE, C)
    middle_grad = grad_out + normalize_back(second_grad, normed_two, inv_two, vectors[2])
    attn_low = to_windows(middle_grad.astype(jnp.bfloat16)).reshape(window_count * span, C)
    proj_grad = lax.dot_general(
        attended, attn_low, contract_rows, preferred_element_type=jnp.float32
    )
    attended_grad = lax.dot_general(
        attn_low, proj_local, contract_cols, preferred_element_type=jnp.float32
    )
    attended_grad = attended_grad.astype(jnp.bfloat16).reshape(window_count, span, heads_here, HD)
    attention_again = jnp.exp(score_block() - log_total)
    value_grad = jnp.einsum(
        "whij,wihd->wjhd",
        attention_again.astype(jnp.bfloat16),
        attended_grad,
        preferred_element_type=jnp.float32,
    )
    probs_grad = jnp.einsum(
        "wihd,wjhd->whij", attended_grad, values_part, preferred_element_type=jnp.float32
    )
    row_term = jnp.sum(attention_again * probs_grad, axis=-1, keepdims=True)
    score_grad = (attention_again * (probs_grad - row_term)).astype(jnp.bfloat16)
    query_grad = (
        jnp.einsum("whij,wjhd->wihd", score_grad, keys_part, preferred_element_type=jnp.float32)
        * score_scale
    )
    key_grad = (
        jnp.einsum("whij,wihd->wjhd", score_grad, queries, preferred_element_type=jnp.float32)
        * score_scale
    )
    bias_heads = (
        jnp.sum(score_grad.astype(jnp.float32), axis=0)
        .transpose(1, 2, 0)
        .reshape(span * span, heads_here)
    )
    table_grad = jnp.dot(onehot.T, bias_heads, precision=highest)
    qkv_back = (
        jnp.stack([query_grad, key_grad, value_grad], axis=3)
        .astype(jnp.bfloat16)
        .reshape(window_count * span, 3 * wide)
    )
    kind_sums = jnp.sum(qkv_back.astype(jnp.float32), axis=0).reshape(heads_here, 3, HD)
    qv_grad = jnp.stack([kind_sums[:, 0].reshape(wide), kind_sums[:, 2].reshape(wide)], axis=0)
    qkv_grad = lax.dot_general(
        qkv_back, window_in, contract_rows, preferred_element_type=jnp.float32
    )
    first_part = jnp.dot(qkv_back, qkv_local, preferred_element_type=jnp.float32)
    first_windows = first_part
    first_grad = from_windows(first_windows.reshape(window_count, span, C), image_total)
    input_grad = middle_grad + normalize_back(first_grad, normed_one, inv_one, vectors[0])
    vectors_grad = jnp.stack(
        [
            jnp.sum(first_grad * normed_one, axis=(0, 1)),
            jnp.sum(first_grad, axis=(0, 1)),
            jnp.sum(second_grad * normed_two, axis=(0, 1)),
            jnp.sum(second_grad, axis=(0, 1)),
            jnp.sum(middle_grad, axis=(0, 1)),
            jnp.sum(grad_out, axis=(0, 1)),
        ],
        axis=0,
    )
    big_grads = (qkv_grad, proj_grad, expand_grad, contract_grad)
    small_grads = (vectors_grad, qv_grad, expand_bias_grad, table_grad)
    return (block_low, input_grad.astype(jnp.bfloat16), big_grads, small_grads)


def shards(
    images,
    cotangent,
    qkv_weight,
    proj_weight,
    expand_weight,
    contract_weight,
    qkv_moment,
    proj_moment,
    expand_moment,
    contract_moment,
    vectors,
    qv_bias,
    expand_bias,
    rel_table,
    vectors_first,
    vectors_second,
    qv_first,
    qv_second,
    expand_bias_first,
    expand_bias_second,
    table_first,
    table_second,
    region_ids,
    pos_index,
    image_counts,
):
    everyone = ("mp", "dp")
    span = WIN * WIN
    mp_size, dp_size = lax.axis_size("mp"), lax.axis_size("dp")
    mp_index, dp_index = lax.axis_index("mp"), lax.axis_index("dp")
    devices = mp_size * dp_size
    per_device = IMG_DEV // mp_size
    first_image = mp_index * per_device
    live_all = first_image + jnp.arange(per_device, dtype=jnp.int32) < image_counts[0]
    own_images = lax.dynamic_slice_in_dim(images, first_image, per_device, 0)
    own_cotangent = lax.dynamic_slice_in_dim(cotangent, first_image, per_device, 0)
    qv_full = lax.all_gather(qv_bias, "mp", axis=1, tiled=True)
    expand_full = lax.all_gather(expand_bias, "mp", axis=0, tiled=True)
    table_full = lax.all_gather(rel_table, "mp", axis=1, tiled=True)
    onehot = (
        pos_index.reshape(span * span)[:, None] == jnp.arange(TABLE, dtype=jnp.int32)[None, :]
    ).astype(jnp.float32)
    heads_here = table_full.shape[1]
    pos_bias = (
        jnp.dot(onehot, table_full, precision=highest)
        .reshape(span, span, heads_here)
        .transpose(2, 0, 1)
    )
    window_regions = to_windows(region_ids.reshape(1, SIDE * SIDE, 1))[:, :, 0]
    window_mask = jnp.where(
        window_regions[:, :, None] != window_regions[:, None, :], mask_value, 0.0
    ).astype(jnp.float32)
    weights_all = (qkv_weight, proj_weight, expand_weight, contract_weight)
    moments = (qkv_moment, proj_moment, expand_moment, contract_moment)
    rows = [weight.shape[0] for weight in weights_all]
    starts = [sum(rows[:which]) for which in range(4)]
    total_rows = sum(rows)

    def cut(stacked):
        return [stacked[:, start : start + count] for start, count in zip(starts, rows)]

    own_low = jnp.concatenate(weights_all, axis=0).astype(jnp.bfloat16)
    gathered = [
        part.reshape(-1, C) for part in cut(lax.all_gather(own_low, everyone, axis=0, tiled=False))
    ]
    block_low, input_low, big_local, small_local = layer_pass(
        own_images,
        own_cotangent,
        live_all,
        gathered,
        vectors,
        qv_full,
        expand_full,
        pos_bias,
        window_mask,
        onehot,
    )
    block_out = lax.all_gather(block_low, "mp", axis=0, tiled=True)
    input_grad = lax.all_gather(input_low, "mp", axis=0, tiled=True)
    stacked_grads = jnp.concatenate(
        [grad.reshape(devices, count, C) for grad, count in zip(big_local, rows)], axis=1
    ).astype(jnp.bfloat16)
    own_grads = lax.psum_scatter(
        stacked_grads.reshape(devices * total_rows, C), everyone, scatter_dimension=0, tiled=True
    ).astype(jnp.float32)
    own_moments = jnp.concatenate(moments, axis=0)
    own_buffers = muon_beta * own_moments + own_grads
    own_nesterov = own_grads + muon_beta * own_buffers
    iterate_all = lax.all_gather(
        own_nesterov.astype(jnp.bfloat16), everyone, axis=0, tiled=False
    )
    grams = jnp.stack(
        [
            lax.dot_general(
                part.reshape(-1, C),
                part.reshape(-1, C),
                contract_rows,
                preferred_element_type=jnp.float32,
            )
            for part in cut(iterate_all)
        ]
    )
    own_gram = lax.dynamic_index_in_dim(grams, mp_index, 0, keepdims=False)
    ortho_map = newton_schulz(own_gram)
    most = max(rows)
    start_here = jnp.array(starts, jnp.int32)[mp_index]
    by_group = iterate_all.reshape(mp_size, dp_size, total_rows, C)
    picked = lax.dynamic_slice(
        by_group,
        (jnp.int32(0), dp_index.astype(jnp.int32), start_here, jnp.int32(0)),
        (mp_size, 1, most, C),
    ).reshape(mp_size * most, C)
    map_parts = split_low(ortho_map)
    products = jnp.dot(picked, map_parts[0], preferred_element_type=jnp.float32) + jnp.dot(
        picked, map_parts[1], preferred_element_type=jnp.float32
    )
    exchanged = lax.all_to_all(products.reshape(mp_size, most, C), "mp", 0, 0, tiled=False)
    ortho = [exchanged[which, :count] for which, count in enumerate(rows)]
    shares = [own_grads[start : start + count] for start, count in zip(starts, rows)]
    buffers = [own_buffers[start : start + count] for start, count in zip(starts, rows)]
    small_full = lax.psum(small_local, everyone)

    def own_columns(full, width):
        return lax.dynamic_slice_in_dim(full, mp_index * width, width, full.ndim - 1)

    small_sums = (
        small_full[0],
        own_columns(small_full[1], qv_bias.shape[1]),
        own_columns(small_full[2], expand_bias.shape[0]),
        own_columns(small_full[3], rel_table.shape[1]),
    )
    factors = (math.sqrt(3.0), 1.0, math.sqrt(max(1.0, FF / C)), 1.0)
    new_steps = tuple(
        (
            -muon_rate * (muon_decay * weight + factor * ortho_part)
            for weight, ortho_part, factor in zip(weights_all, ortho, factors)
        )
    )
    vectors_step, vectors_first_new, vectors_second_new = adam_update(
        small_sums[0], vectors_first, vectors_second
    )
    qv_step, qv_first_new, qv_second_new = adam_update(small_sums[1], qv_first, qv_second)
    expand_bias_step, expand_bias_first_new, expand_bias_second_new = adam_update(
        small_sums[2], expand_bias_first, expand_bias_second
    )
    table_step, table_first_new, table_second_new = adam_update(
        small_sums[3], table_first, table_second
    )
    return (
        block_out,
        input_grad,
        shares[0],
        shares[1],
        shares[2],
        shares[3],
        small_sums[0],
        small_sums[1],
        small_sums[2],
        small_sums[3],
        new_steps[0],
        new_steps[1],
        new_steps[2],
        new_steps[3],
        buffers[0],
        buffers[1],
        buffers[2],
        buffers[3],
        vectors_step,
        qv_step,
        expand_bias_step,
        table_step,
        vectors_first_new,
        vectors_second_new,
        qv_first_new,
        qv_second_new,
        expand_bias_first_new,
        expand_bias_second_new,
        table_first_new,
        table_second_new,
    )


def solution(mesh):
    return jax.shard_map(
        shards,
        mesh=mesh,
        in_specs=(
            P("dp", None, None),
            P("dp", None, None),
            P(("mp", "dp"), None),
            P(("mp", "dp"), None),
            P(("mp", "dp"), None),
            P(("mp", "dp"), None),
            P(("mp", "dp"), None),
            P(("mp", "dp"), None),
            P(("mp", "dp"), None),
            P(("mp", "dp"), None),
            P(),
            P(None, "mp"),
            P("mp"),
            P(None, "mp"),
            P(),
            P(),
            P(None, "mp"),
            P(None, "mp"),
            P("mp"),
            P("mp"),
            P(None, "mp"),
            P(None, "mp"),
            P(),
            P(),
            P("dp"),
        ),
        out_specs=(
            P("dp", None, None),
            P("dp", None, None),
            P(("mp", "dp"), None),
            P(("mp", "dp"), None),
            P(("mp", "dp"), None),
            P(("mp", "dp"), None),
            P(),
            P(None, "mp"),
            P("mp"),
            P(None, "mp"),
            P(("mp", "dp"), None),
            P(("mp", "dp"), None),
            P(("mp", "dp"), None),
            P(("mp", "dp"), None),
            P(("mp", "dp"), None),
            P(("mp", "dp"), None),
            P(("mp", "dp"), None),
            P(("mp", "dp"), None),
            P(),
            P(None, "mp"),
            P("mp"),
            P(None, "mp"),
            P(),
            P(),
            P(None, "mp"),
            P(None, "mp"),
            P("mp"),
            P("mp"),
            P(None, "mp"),
            P(None, "mp"),
        ),
        check_vma=False,
    )
```

```python
import functools
import math

import jax
import jax.numpy as jnp
import numpy as np
from jax import lax
from jax.experimental import pallas as pl
from jax.experimental.pallas import tpu as pltpu
from jax.sharding import PartitionSpec as P

C = 512
HEADS = 16
HD = 32
FF = 2048
WIN = 7
SIDE = 14
SHIFT = 3
SPAN = WIN * WIN
TOK = SIDE * SIDE
NS_ITERS = 5
IMG_DEV = 16
TABLE = 169
PAIR = 112
ROWS = 2 * PAIR
GROUP = 4

norm_eps = 1e-05
ns_eps = 1e-07
coef_a = 3.4445
coef_b = -4.775
coef_c = 2.0315
muon_rate = 0.3
muon_decay = 0.1
muon_beta = 0.95
adam_rate = 0.1
adam_one = 0.9
adam_two = 0.999
adam_eps = 1e-08
adam_step = 4
mask_value = -100.0
away = -1e30
wide = jnp.float32
low = jnp.bfloat16
highest = lax.Precision.HIGHEST


def to_windows(field_values):
    image_total = field_values.shape[0]
    channels = field_values.shape[-1]
    blocks = SIDE // WIN
    grid_values = field_values.reshape(image_total, SIDE, SIDE, channels)
    grid_values = jnp.roll(grid_values, (-SHIFT, -SHIFT), axis=(1, 2))
    grid_values = grid_values.reshape(image_total, blocks, WIN, blocks, WIN, channels)
    grid_values = grid_values.transpose(0, 1, 3, 2, 4, 5)
    return grid_values.reshape(image_total * blocks * blocks, WIN * WIN, channels)


def window_order():
    order = np.full((ROWS,), -1, np.int64)
    for window in range(4):
        top, left = window // 2, window % 2
        for token in range(SPAN):
            row = (top * WIN + token // WIN + SHIFT) % SIDE
            column = (left * WIN + token % WIN + SHIFT) % SIDE
            order[(window // 2) * PAIR + (window % 2) * SPAN + token] = row * SIDE + column
    return order


def dot(a, b):
    return jnp.dot(a, b, preferred_element_type=wide)


def dot_nt(a, b):
    return lax.dot_general(a, b, (((1,), (1,)), ((), ())), preferred_element_type=wide)


def dot_tn(a, b):
    return lax.dot_general(a, b, (((0,), (0,)), ((), ())), preferred_element_type=wide)


def mean_of(values):
    return jnp.sum(values, axis=-1, keepdims=True) * (1.0 / C)


def normalize(values):
    centered = values - mean_of(values)
    inv_scale = lax.rsqrt(mean_of(centered * centered) + norm_eps)
    return centered * inv_scale, inv_scale


def normalize_back(grad_norm, normed, inv_scale, gain):
    scaled = grad_norm * gain
    return inv_scale * (scaled - mean_of(scaled) - normed * mean_of(scaled * normed))


def column_sum(values):
    return jnp.sum(values, axis=0, keepdims=True)


def head_masks():
    lane = lax.broadcasted_iota(jnp.int32, (1, 128), 1) // HD
    return [(lane == head).astype(wide).astype(low) for head in range(GROUP)]


def stack_heads(block, masks):
    return jnp.concatenate([block * mask for mask in masks], axis=0)


def pick_heads(stacked):
    lane = lax.broadcasted_iota(jnp.int32, (PAIR, 128), 1)
    parts = [stacked[PAIR * head : PAIR * (head + 1)] for head in range(GROUP)]
    return jnp.where(
        lane < 2 * HD,
        jnp.where(lane < HD, parts[0], parts[1]),
        jnp.where(lane < 3 * HD, parts[2], parts[3]),
    )


def layer_kernel(
    packed, place, images, cotangent, order, order_back, vectors, qv_bias, expand_bias, bias,
    qkv_hbm, proj_hbm, expand_hbm, contract_hbm,
    block_out, input_grad, *rest,
):
    n_grads = 1 if packed else 4
    grad_outs = rest[:n_grads]
    (small, table_sum, qkv_nat, qkv_w, proj_w, expand_w, contract_w,
     qkv_acc, proj_acc, expand_acc, contract_acc,
     qkv_s, att_s, back_s, probs_s, normed_s, first_s, middle_s, normed2_s, second_s,
     out_low_s, mlp_s, second_grad_s, sems) = rest[n_grads:]
    step = pl.program_id(0)
    steps = pl.num_programs(0)
    masks = head_masks()
    live = place[1] > place[0] + step
    live_scale = live.astype(wide)

    def fetch(which):
        if packed:
            counts = (48, 16, 64, 64)
            source = qkv_hbm.at[:, pl.ds(sum(counts[:which]), counts[which])]
            target = (qkv_nat, proj_w, expand_w, contract_w)[which]
        else:
            source = (qkv_hbm, proj_hbm, expand_hbm, contract_hbm)[which]
            target = (qkv_nat, proj_w, expand_w, contract_w)[which]
        return pltpu.make_async_copy(source, target, sems.at[which])

    def rows_of(ref, count):
        return ref[...].reshape(count, C)

    def begin():
        for which in range(4):
            fetch(which).start()
        for ref in (qkv_acc, proj_acc, expand_acc, contract_acc, small, table_sum):
            ref[...] = jnp.zeros_like(ref)
        for which in range(4):
            fetch(which).wait()
        natural = rows_of(qkv_nat, 3 * C).reshape(HEADS, 3, HD, C)
        for kind in range(3):
            qkv_w[kind] = natural[:, kind].reshape(C, C)

    pl.when(step == 0)(begin)

    tokens = dot(order[...], images[0])
    normed, inv_one = normalize(tokens)
    normed_s[...] = normed
    first_in = (normed * vectors[0:1] + vectors[1:2]).astype(low)
    first_s[...] = first_in
    for kind in range(3):
        projected = dot_nt(first_in, qkv_w[kind])
        if kind != 1:
            projected = projected + qv_bias[kind // 2 : kind // 2 + 1]
        projected = projected.astype(low)
        for group in range(4):
            qkv_s[kind * 4 + group] = projected[:, 128 * group : 128 * (group + 1)]
    score_scale = 1.0 / math.sqrt(HD)

    def attend(which, carry):
        pair, group = which // 4, which % 4
        rows = pl.ds(pl.multiple_of(pair * PAIR, 16), PAIR)
        queries = stack_heads(qkv_s[group, rows], masks)
        scores = dot_nt(queries, qkv_s[4 + group, rows]) * score_scale + bias[pair, group]
        top = jnp.max(scores, axis=-1, keepdims=True)
        exponent = jnp.exp(scores - top)
        attention = exponent / jnp.sum(exponent, axis=-1, keepdims=True)
        probs_s[which] = attention
        att_s[group, rows] = pick_heads(dot(attention.astype(low), qkv_s[8 + group, rows])).astype(low)
        return carry

    lax.fori_loop(0, 8, attend, 0)
    attended = jnp.concatenate([att_s[group] for group in range(4)], axis=1)
    middle = tokens + (dot(attended, rows_of(proj_w, C)) + vectors[4:5])
    middle_s[...] = middle
    normed_two, inv_two = normalize(middle)
    normed2_s[...] = normed_two
    second_in = (normed_two * vectors[2:3] + vectors[3:4]).astype(low)
    second_s[...] = second_in

    out_low = (dot(order[...], cotangent[0]) * live_scale).astype(low)
    out_low_s[...] = out_low
    mlp_s[...] = jnp.zeros_like(mlp_s)
    second_grad_s[...] = jnp.zeros_like(second_grad_s)
    chunk = 512
    owners = expand_w.shape[0] // (FF // chunk)

    def feed(which, carry):
        units = pl.ds(pl.multiple_of(which * owners, owners), owners)
        expand_part = expand_w[units].reshape(chunk, C)
        contract_part = contract_w[units].reshape(chunk, C)
        second = second_s[...]
        grad_rows = out_low_s[...]
        hidden = dot_nt(second, expand_part) + expand_bias[which]
        cumulative = 0.5 * (1.0 + lax.erf(hidden * (1.0 / math.sqrt(2.0))))
        acted = (hidden * cumulative).astype(low)
        slope = cumulative + hidden * jnp.exp(-0.5 * hidden * hidden) * (1.0 / math.sqrt(2.0 * math.pi))
        mlp_s[...] += dot(acted, contract_part)
        hidden_grad32 = dot_nt(grad_rows, contract_part) * slope
        hidden_grad = hidden_grad32.astype(low)
        small[pl.ds(8 + which, 1)] += column_sum(hidden_grad.astype(wide))
        second_grad_s[...] += dot(hidden_grad, expand_part)
        units_wide = pl.ds(pl.multiple_of(which * chunk, chunk), chunk)
        contract_acc[units_wide] += dot_tn(acted, grad_rows)
        expand_acc[units_wide] += dot_tn(hidden_grad, second)
        return carry

    lax.fori_loop(0, FF // chunk, feed, 0)
    result = middle_s[...] + (mlp_s[...] + vectors[5:6])
    result = jnp.where(live, result, 0.0).astype(low)
    block_out[0] = dot(order_back[...], result).astype(low)

    grad_out = out_low_s[...].astype(wide)
    second_grad = second_grad_s[...]
    normed_two = normed2_s[...]
    small[5:6] += column_sum(grad_out)
    small[3:4] += column_sum(second_grad)
    small[2:3] += column_sum(second_grad * normed_two)
    middle_grad = grad_out + normalize_back(second_grad, normed_two, inv_two, vectors[2:3])
    small[4:5] += column_sum(middle_grad)
    middle_s[...] = middle_grad
    attn_low = middle_grad.astype(low)
    attended = jnp.concatenate([att_s[group] for group in range(4)], axis=1)
    proj_acc[...] += dot_tn(attended, attn_low)
    attended_grad = dot_nt(attn_low, rows_of(proj_w, C)).astype(low)
    for group in range(4):
        att_s[group] = attended_grad[:, 128 * group : 128 * (group + 1)]

    def attend_back(which, carry):
        pair, group = which // 4, which % 4
        rows = pl.ds(pl.multiple_of(pair * PAIR, 16), PAIR)
        attention = probs_s[which]
        keys, values = qkv_s[4 + group, rows], qkv_s[8 + group, rows]
        grads = stack_heads(att_s[group, rows], masks)
        queries = stack_heads(qkv_s[group, rows], masks)
        probs_grad = dot_nt(grads, values)
        row_term = jnp.sum(attention * probs_grad, axis=-1, keepdims=True)
        score_grad = (attention * (probs_grad - row_term)).astype(low)
        table_sum[group] += score_grad.astype(wide)
        back_s[group, rows] = (pick_heads(dot(score_grad, keys)) * score_scale).astype(low)
        back_s[4 + group, rows] = (dot_tn(score_grad, queries) * score_scale).astype(low)
        back_s[8 + group, rows] = dot_tn(attention.astype(low), grads).astype(low)
        return carry

    lax.fori_loop(0, 8, attend_back, 0)
    first_in = first_s[...]
    first_grad = None
    for kind in range(3):
        back = jnp.concatenate([back_s[kind * 4 + group] for group in range(4)], axis=1)
        if kind != 1:
            row = 6 + kind // 2
            small[row : row + 1] += column_sum(back.astype(wide))
        qkv_acc[kind] += dot_tn(back, first_in)
        part = dot(back, qkv_w[kind])
        first_grad = part if first_grad is None else first_grad + part
    normed = normed_s[...]
    small[1:2] += column_sum(first_grad)
    small[0:1] += column_sum(first_grad * normed)
    token_grad = middle_s[...] + normalize_back(first_grad, normed, inv_one, vectors[0:1])
    input_grad[0] = dot(order_back[...], token_grad.astype(low)).astype(low)

    def finish():
        for kind in range(3):
            part = qkv_acc[kind].astype(low).reshape(HEADS, HD, C)
            if packed:
                out = grad_outs[0]
                for piece in range(2):
                    block = kind * 2 + piece
                    out[:, block // 3, pl.ds(16 * (block % 3), 16)] = part[:, 16 * piece : 16 * (piece + 1)]
            else:
                grad_outs[0][:, kind] = part
        if packed:
            out = grad_outs[0]
            out[:, :, pl.ds(48, 16)] = proj_acc[...].astype(low).reshape(16, 2, 16, C)
            out[:, :, pl.ds(64, 64)] = expand_acc[...].astype(low).reshape(16, 2, 64, C)
            out[:, :, pl.ds(128, 64)] = contract_acc[...].astype(low).reshape(16, 2, 64, C)
        else:
            grad_outs[1][...] = proj_acc[...].astype(low)
            grad_outs[2][...] = expand_acc[...].astype(low)
            grad_outs[3][...] = contract_acc[...].astype(low)

    pl.when(step == steps - 1)(finish)


def run_layer(packed, per_device, place, images, cotangent, vectors, qv_bias, expand_bias, bias, weights):
    order_np = window_order()
    onehot = (order_np[:, None] == np.arange(TOK)[None, :]).astype(np.float32)
    order = jnp.asarray(onehot, low)
    order_back = jnp.asarray(onehot.T, low)
    any_spec = pl.BlockSpec(memory_space=pl.ANY)

    def whole(shape):
        return pl.BlockSpec(shape, lambda i, s: (0,) * len(shape), pipeline_mode=pl.Buffered(1))

    image_spec = pl.BlockSpec((1, TOK, C), lambda i, s: (s[0] + i, 0, 0))
    out_spec = pl.BlockSpec((1, TOK, C), lambda i, s: (i, 0, 0))
    if packed:
        weights = (weights,) * 4
        grad_shapes = [(16, 2, 192, C)]
        weight_shapes = [(32, 48, C), (32, 16, C), (32, 64, C), (32, 64, C)]
    else:
        weights = (weights[0], weights[1], weights[2].reshape(FF // 64, 64, C), weights[3].reshape(FF // 64, 64, C))
        grad_shapes = [(HEADS, 3, HD, C), (C, C), (FF, C), (FF, C)]
        weight_shapes = [w.shape for w in weights]
    outs = pl.pallas_call(
        functools.partial(layer_kernel, packed),
        out_shape=[
            jax.ShapeDtypeStruct((per_device, TOK, C), low),
            jax.ShapeDtypeStruct((per_device, TOK, C), low),
            *[jax.ShapeDtypeStruct(shape, low) for shape in grad_shapes],
            jax.ShapeDtypeStruct((16, C), wide),
            jax.ShapeDtypeStruct((4, GROUP * PAIR, PAIR), wide),
        ],
        grid_spec=pltpu.PrefetchScalarGridSpec(
            num_scalar_prefetch=1,
            grid=(per_device,),
            in_specs=[
                image_spec, image_spec, whole((ROWS, TOK)), whole((TOK, ROWS)), whole((6, C)), whole((2, C)),
                whole((4, 1, C)), whole((2, 4, GROUP * PAIR, PAIR)), any_spec, any_spec, any_spec, any_spec,
            ],
            out_specs=[out_spec, out_spec]
            + [whole(shape) for shape in grad_shapes]
            + [whole((16, C)), whole((4, GROUP * PAIR, PAIR))],
            scratch_shapes=[pltpu.VMEM(shape, low) for shape in weight_shapes[:1]]
            + [pltpu.VMEM((3, C, C), low)]
            + [pltpu.VMEM(shape, low) for shape in weight_shapes[1:]]
            + [
                pltpu.VMEM((3, C, C), wide),
                pltpu.VMEM((C, C), wide),
                pltpu.VMEM((FF, C), wide),
                pltpu.VMEM((FF, C), wide),
                pltpu.VMEM((12, ROWS, 128), low),
                pltpu.VMEM((4, ROWS, 128), low),
                pltpu.VMEM((12, ROWS, 128), low),
                pltpu.VMEM((8, GROUP * PAIR, PAIR), wide),
                pltpu.VMEM((ROWS, C), wide),
                pltpu.VMEM((ROWS, C), low),
                pltpu.VMEM((ROWS, C), wide),
                pltpu.VMEM((ROWS, C), wide),
                pltpu.VMEM((ROWS, C), low),
                pltpu.VMEM((ROWS, C), low),
                pltpu.VMEM((ROWS, C), wide),
                pltpu.VMEM((ROWS, C), wide),
                pltpu.SemaphoreType.DMA((4,)),
            ],
        ),
        compiler_params=pltpu.CompilerParams(vmem_limit_bytes=60 * 1024 * 1024),
        name="window_layer",
    )(place, images, cotangent, order, order_back, vectors, qv_bias, expand_bias.reshape(4, 1, C), bias, *weights)
    grads = outs[2 : 2 + len(grad_shapes)]
    grads = grads[0].reshape(32, 192, C) if packed else [g.reshape(-1, C) for g in grads]
    return outs[0], outs[1], grads, outs[-2], outs[-1]


def pair_bias(pos_bias, window_mask):
    heads = pos_bias.shape[0]
    scores = pos_bias[None] + window_mask[:, None]
    scores = scores.reshape(2, 2, heads, SPAN, SPAN)
    first = jnp.pad(scores[:, 0], ((0, 0), (0, 0), (0, 0), (0, PAIR - SPAN)), constant_values=away)
    second = jnp.pad(scores[:, 1], ((0, 0), (0, 0), (0, 0), (SPAN, PAIR - 2 * SPAN)), constant_values=away)
    rest = jnp.broadcast_to(
        jnp.where(jnp.arange(PAIR) < SPAN, 0.0, away).astype(wide), (2, heads, PAIR - 2 * SPAN, PAIR)
    )
    return jnp.concatenate([first, second, rest], axis=2).reshape(2, heads // GROUP, GROUP * PAIR, PAIR)


MESH = pl.DeviceIdType.MESH
DEPTH = 4


class Place:
    def __init__(self):
        dp_index, mp_index = lax.axis_index("dp"), lax.axis_index("mp")
        self.z, self.x = dp_index // 2, dp_index % 2
        self.y, self.core = mp_index // 2, mp_index % 2
        self.dp_index, self.mp_index = dp_index, mp_index
        self.x_side = self.device(self.z, 1 - self.x, self.y, self.core)
        self.y_side = self.device(self.z, self.x, 1 - self.y, self.core)
        self.partner = self.device(self.z, self.x, self.y, 1 - self.core)
        self.above = self.device(self.z + 1, self.x, self.y, self.core)
        self.below = self.device(self.z - 1, self.x, self.y, self.core)

    @staticmethod
    def device(z, x, y, core):
        return {"dp": z * 2 + x, "mp": y * 2 + core}

    @staticmethod
    def owner(z, x, y, core):
        return (y * 2 + core) * 8 + z * 2 + x

    def greet(self):
        barrier = pltpu.get_barrier_semaphore()

        def signal(device):
            pl.semaphore_signal(barrier, inc=1, device_id=device, device_id_type=MESH)

        signal(self.x_side)
        signal(self.y_side)
        signal(self.partner)
        pl.when(self.z > 0)(lambda: signal(self.below))
        pl.when(self.z < DEPTH - 1)(lambda: signal(self.above))
        ends = (self.z == 0).astype(jnp.int32) + (self.z == DEPTH - 1).astype(jnp.int32)
        pl.semaphore_wait(barrier, 5 - ends)


def remote(src, dst, send_sem, recv_sem, device):
    return pltpu.make_async_remote_copy(
        src_ref=src,
        dst_ref=dst,
        send_sem=send_sem,
        recv_sem=recv_sem,
        device_id=device,
        device_id_type=MESH,
    )


def spread(at, own_ref, out_ref, own_sem, z_send, z_recv, side_send, side_recv, pair_send, pair_recv):
    rows = own_ref.shape[0]
    half = rows // 2
    z, x, y, core = at.z, at.x, at.y, at.core
    low, high = pl.ds(0, half), pl.ds(half, rows - half)

    def slot(source_z, other_x, other_y):
        return out_ref.at[
            at.owner(source_z, 1 - x if other_x else x, 1 - y if other_y else y, core)
        ]

    def up(source_z, src=None):
        dst = slot(source_z, False, False)
        return remote(dst if src is None else src, dst, z_send.at[0, source_z], z_recv.at[0, source_z], at.above)

    def down(source_z, src=None):
        dst = slot(source_z, False, False)
        return remote(dst if src is None else src, dst, z_send.at[1, source_z], z_recv.at[1, source_z], at.below)

    def side(kind, source_z, src=None):
        if kind == 0 or kind == 1:
            dst = slot(source_z, False, False)
        elif kind == 2:
            dst = slot(source_z, True, False).at[low]
        else:
            dst = slot(source_z, False, True).at[high]
        device = at.x_side if kind in (0, 3) else at.y_side
        return remote(
            dst if src is None else src, dst, side_send.at[kind, source_z], side_recv.at[kind, source_z], device
        )

    def side_arrival(kind, source_z):
        if kind == 0:
            dst = slot(source_z, True, False)
        elif kind == 1:
            dst = slot(source_z, False, True)
        elif kind == 2:
            dst = slot(source_z, True, True).at[low]
        else:
            dst = slot(source_z, True, True).at[high]
        device = at.x_side if kind in (0, 3) else at.y_side
        return remote(dst, dst, side_send.at[kind, source_z], side_recv.at[kind, source_z], device)

    def pair_region(kind, source_z, of_core):
        other_x, other_y = ((False, False), (True, False), (False, True), (True, True), (True, True))[kind]
        ref = out_ref.at[at.owner(source_z, 1 - x if other_x else x, 1 - y if other_y else y, of_core)]
        if kind == 3:
            ref = ref.at[low]
        elif kind == 4:
            ref = ref.at[high]
        return ref

    def pair(kind, source_z, src=None):
        dst = pair_region(kind, source_z, core)
        return remote(
            dst if src is None else src, dst, pair_send.at[kind, source_z], pair_recv.at[kind, source_z], at.partner
        )

    def pair_arrival(kind, source_z):
        dst = pair_region(kind, source_z, 1 - core)
        return remote(dst, dst, pair_send.at[kind, source_z], pair_recv.at[kind, source_z], at.partner)

    keep = pltpu.make_async_copy(own_ref, slot(z, False, False), own_sem)
    pl.when(z < DEPTH - 1)(lambda: up(z, own_ref).start())
    pl.when(z > 0)(lambda: down(z, own_ref).start())
    side(0, z, own_ref).start()
    side(1, z, own_ref).start()
    pair(0, z, own_ref).start()
    keep.start()

    def plane(source_z):
        side_arrival(0, source_z).wait_recv()
        side(2, source_z).start()
        pair(1, source_z).start()
        side_arrival(1, source_z).wait_recv()
        side(3, source_z).start()
        pair(2, source_z).start()

    def column(source_z):
        side(0, source_z).start()
        side(1, source_z).start()
        pair(0, source_z).start()

    for distance in range(1, DEPTH + 1):

        def from_below(source_z=z - distance):
            up(source_z).wait_recv()
            pl.when(z < DEPTH - 1)(lambda: up(source_z).start())
            column(source_z)

        def from_above(source_z=z + distance):
            down(source_z).wait_recv()
            pl.when(z > 0)(lambda: down(source_z).start())
            column(source_z)

        pl.when(z - distance >= 0)(from_below)
        pl.when(z + distance <= DEPTH - 1)(from_above)
        past = distance - 1
        if past == 0:
            plane(z)
        else:
            pl.when(z - past >= 0)(functools.partial(plane, z - past))
            pl.when(z + past <= DEPTH - 1)(functools.partial(plane, z + past))

    def corner(source_z):
        side_arrival(2, source_z).wait_recv()
        pair(3, source_z).start()
        side_arrival(3, source_z).wait_recv()
        pair(4, source_z).start()

    for distance in range(DEPTH):
        if distance == 0:
            corner(z)
        else:
            pl.when(z - distance >= 0)(functools.partial(corner, z - distance))
            pl.when(z + distance <= DEPTH - 1)(functools.partial(corner, z + distance))
    keep.wait()
    for source_z in range(DEPTH):
        for kind in range(5):
            pair_arrival(kind, source_z).wait_recv()
            pair(kind, source_z).wait_send()
        for kind in range(4):
            side(kind, source_z).wait_send()
        pl.when((z < DEPTH - 1) & (source_z <= z))(lambda: up(source_z).wait_send())
        pl.when((z > 0) & (source_z >= z))(lambda: down(source_z).wait_send())


SPREAD_SEMS = [
    pltpu.SemaphoreType.DMA,
    pltpu.SemaphoreType.DMA((2, DEPTH)),
    pltpu.SemaphoreType.DMA((2, DEPTH)),
    pltpu.SemaphoreType.DMA((4, DEPTH)),
    pltpu.SemaphoreType.DMA((4, DEPTH)),
    pltpu.SemaphoreType.DMA((5, DEPTH)),
    pltpu.SemaphoreType.DMA((5, DEPTH)),
]


def gather_kernel(own_ref, misc_ref, out_ref, misc_out, misc_send, misc_recv, *sems):
    at = Place()
    at.greet()
    to_pair = remote(misc_ref, misc_out.at[at.mp_index], misc_send.at[0], misc_recv.at[0], at.partner)
    to_side = remote(misc_ref, misc_out.at[at.mp_index], misc_send.at[1], misc_recv.at[1], at.y_side)
    to_pair.start()
    to_side.start()
    misc_out[at.mp_index] = misc_ref[...]
    over = (1 - at.y) * 2 + at.core
    from_side = remote(misc_ref, misc_out.at[over], misc_send.at[1], misc_recv.at[1], at.y_side)
    relay = remote(misc_out.at[over], misc_out.at[over], misc_send.at[2], misc_recv.at[2], at.partner)
    spread(at, own_ref, out_ref, *sems)
    from_side.wait_recv()
    relay.start()
    beside = at.y * 2 + 1 - at.core
    remote(misc_ref, misc_out.at[beside], misc_send.at[0], misc_recv.at[0], at.partner).wait_recv()
    across = (1 - at.y) * 2 + 1 - at.core
    remote(misc_ref, misc_out.at[across], misc_send.at[2], misc_recv.at[2], at.partner).wait_recv()
    to_pair.wait_send()
    to_side.wait_send()
    relay.wait_send()


def gather_all(own, misc):
    rows, columns = own.shape
    return pl.pallas_call(
        gather_kernel,
        out_shape=(
            jax.ShapeDtypeStruct((32, rows, columns), own.dtype),
            jax.ShapeDtypeStruct((4,) + misc.shape, misc.dtype),
        ),
        in_specs=[pl.BlockSpec(memory_space=pltpu.VMEM)] * 2,
        out_specs=(pl.BlockSpec(memory_space=pl.ANY), pl.BlockSpec(memory_space=pltpu.VMEM)),
        scratch_shapes=[pltpu.SemaphoreType.DMA((3,)), pltpu.SemaphoreType.DMA((3,))] + SPREAD_SEMS,
        compiler_params=pltpu.CompilerParams(collective_id=0, has_side_effects=True),
        name="gather_weights",
    )(own, misc)


def collect(at, grads, total_ref, mine, pair_buf, corner_x, corner_y, full_x, full_y, z_up, z_down, z_out,
            load_sem, pair_send, pair_recv, side_send, side_recv, z_send, z_recv):
    rows = total_ref.shape[0]
    half = rows // 2
    z, x, y, core = at.z, at.x, at.y, at.core
    low, high = pl.ds(0, half), pl.ds(half, rows - half)
    orders = ((3, 2, 1, 0), (3, 0, 2, 1), (0, 3, 1, 2), (0, 1, 2, 3))

    def turn(step):
        choice = jnp.int32(orders[3][step])
        for which in range(3):
            choice = jnp.where(z == which, jnp.int32(orders[which][step]), choice)
        return choice

    turns = [turn(step) for step in range(DEPTH)]

    def load(target, y_of):
        return pltpu.make_async_copy(
            grads.at[y_of * 2 + core, target], mine.at[y_of, target], load_sem.at[y_of, target]
        )

    def pair(target, y_of):
        return remote(
            grads.at[y_of * 2 + 1 - core, target], pair_buf.at[y_of, target],
            pair_send.at[y_of, target], pair_recv.at[y_of, target], at.partner,
        )

    def corner(kind, target):
        part = mine.at[1 - y, target, 1 - x]
        if kind == 0:
            return remote(part.at[low], corner_y.at[target], side_send.at[0, target], side_recv.at[0, target], at.y_side)
        return remote(part.at[high], corner_x.at[target], side_send.at[1, target], side_recv.at[1, target], at.x_side)

    def full(kind, target):
        if kind == 2:
            return remote(mine.at[y, target, 1 - x], full_x.at[target], side_send.at[2, target], side_recv.at[2, target], at.x_side)
        return remote(mine.at[1 - y, target, x], full_y.at[target], side_send.at[3, target], side_recv.at[3, target], at.y_side)

    def up(target):
        return remote(z_out.at[target], z_up.at[target], z_send.at[target], z_recv.at[0, target], at.above)

    def down(target):
        return remote(z_out.at[target], z_down.at[target], z_send.at[target], z_recv.at[1, target], at.below)

    wide = jnp.float32
    for target in turns:
        for y_of in (0, 1):
            pair(target, y_of).start()
            load(target, y_of).start()

    def first(target):
        for y_of in (0, 1):
            load(target, y_of).wait()
            pair(target, y_of).wait_recv()

        def add(which, carry):
            y_of, x_of = which // 2, which % 2
            mine[y_of, target, x_of] = (
                mine[y_of, target, x_of].astype(wide) + pair_buf[y_of, target, x_of].astype(wide)
            ).astype(mine.dtype)
            return carry

        lax.fori_loop(0, 4, add, 0)
        corner(0, target).start()
        corner(1, target).start()

    def second(target):
        corner(0, target).wait_recv()
        mine[y, target, 1 - x, low] = (
            mine[y, target, 1 - x, low].astype(wide) + corner_y[target].astype(wide)
        ).astype(mine.dtype)
        full(2, target).start()
        corner(1, target).wait_recv()
        mine[1 - y, target, x, high] = (
            mine[1 - y, target, x, high].astype(wide) + corner_x[target].astype(wide)
        ).astype(mine.dtype)
        full(3, target).start()

    def third(target, last):
        full(2, target).wait_recv()
        full(3, target).wait_recv()
        total_ref[...] = mine[y, target, x].astype(wide) + (
            full_x[target].astype(wide) + full_y[target].astype(wide)
        )

        def add_below():
            up(target).wait_recv()
            total_ref[...] += z_up[target].astype(wide)

        def add_above():
            down(target).wait_recv()
            total_ref[...] += z_down[target].astype(wide)

        pl.when((target >= z) & (z > 0))(add_below)
        pl.when((target <= z) & (z < DEPTH - 1))(add_above)
        if not last:
            z_out[target] = total_ref[...].astype(z_out.dtype)
            pl.when(target > z)(lambda: up(target).start())
            pl.when(target < z)(lambda: down(target).start())

    for step in range(DEPTH + 2):
        if step < DEPTH:
            first(turns[step])
        if 1 <= step <= DEPTH:
            second(turns[step - 1])
        if step >= 2:
            third(turns[step - 2], step - 2 == DEPTH - 1)
    for target in range(DEPTH):
        for y_of in (0, 1):
            pair(target, y_of).wait_send()
        for kind in (0, 1):
            corner(kind, target).wait_send()
        for kind in (2, 3):
            full(kind, target).wait_send()
        pl.when(target != z)(lambda: up(target).wait_send())


def collect_scratch(rows, columns, dtype):
    return [
        pltpu.VMEM((2, DEPTH, 2, rows, columns), dtype),
        pltpu.VMEM((2, DEPTH, 2, rows, columns), dtype),
        pltpu.VMEM((DEPTH, rows // 2, columns), dtype),
        pltpu.VMEM((DEPTH, rows // 2, columns), dtype),
        pltpu.VMEM((DEPTH, rows, columns), dtype),
        pltpu.VMEM((DEPTH, rows, columns), dtype),
        pltpu.VMEM((DEPTH, rows, columns), dtype),
        pltpu.VMEM((DEPTH, rows, columns), dtype),
        pltpu.VMEM((DEPTH, rows, columns), dtype),
        pltpu.SemaphoreType.DMA((2, DEPTH)),
        pltpu.SemaphoreType.DMA((2, DEPTH)),
        pltpu.SemaphoreType.DMA((2, DEPTH)),
        pltpu.SemaphoreType.DMA((4, DEPTH)),
        pltpu.SemaphoreType.DMA((4, DEPTH)),
        pltpu.SemaphoreType.DMA((DEPTH,)),
        pltpu.SemaphoreType.DMA((2, DEPTH)),
    ]


N_COLLECT = 16


def muon_kernel(grads, moment_ref, grad_out, moment_out, next_all, own_next, *scratch):
    at = Place()
    at.greet()
    collect(at, grads, grad_out, *scratch[:N_COLLECT])
    grad = grad_out[...]
    moment = muon_beta * moment_ref[...] + grad
    moment_out[...] = moment
    own_next[...] = (grad + muon_beta * moment).astype(own_next.dtype)
    spread(at, own_next, next_all, *scratch[N_COLLECT:])


def muon_exchange(grads, moment):
    rows, columns = moment.shape
    shape = jax.ShapeDtypeStruct((rows, columns), jnp.float32)
    vmem = pl.BlockSpec(memory_space=pltpu.VMEM)
    hbm = pl.BlockSpec(memory_space=pl.ANY)
    return pl.pallas_call(
        muon_kernel,
        out_shape=(shape, shape, jax.ShapeDtypeStruct((32, rows, columns), jnp.bfloat16)),
        in_specs=[hbm, vmem],
        out_specs=(vmem, vmem, hbm),
        scratch_shapes=[pltpu.VMEM((rows, columns), jnp.bfloat16)]
        + collect_scratch(rows, columns, jnp.bfloat16)
        + SPREAD_SEMS,
        compiler_params=pltpu.CompilerParams(
            collective_id=1, has_side_effects=True, vmem_limit_bytes=40 * 1024 * 1024
        ),
        name="muon_exchange",
    )(grads.reshape(4, DEPTH, 2, rows, columns), moment)


def ns_kernel(next_all, products, rows_buf, map_buf, sem):
    mp_index, dp_index = lax.axis_index("mp"), lax.axis_index("dp")
    counts = (48, 16, 64, 64)

    def fetch(which):
        count = counts[which]
        copy = pltpu.make_async_copy(
            next_all.at[:, pl.ds(sum(counts[:which]), count)], rows_buf.at[:, pl.ds(0, count)], sem
        )
        copy.start()
        if count < 64:
            rows_buf[:, pl.ds(count, 64 - count)] = jnp.zeros((32, 64 - count, C), rows_buf.dtype)
        copy.wait()

    for which in range(4):
        pl.when(mp_index == which)(functools.partial(fetch, which))

    gram = None
    for part in range(4):
        block = rows_buf[8 * part : 8 * (part + 1)].reshape(512, C)
        term = dot_tn(block, block)
        gram = term if gram is None else gram + term
    eye = (
        lax.broadcasted_iota(jnp.int32, (C, C), 0) == lax.broadcasted_iota(jnp.int32, (C, C), 1)
    ).astype(wide)
    norm_value = jnp.sqrt(jnp.sum(jnp.sum(gram * eye, axis=1, keepdims=True), axis=0, keepdims=True)) + ns_eps
    gram = gram / (norm_value * norm_value)

    def dot_high(a, b):
        return jnp.dot(a, b, precision=lax.Precision.HIGH, preferred_element_type=wide)

    total = None
    for iteration in range(NS_ITERS):
        square = dot_high(gram, gram)
        poly = coef_a * eye + (coef_b * gram + coef_c * square)
        total = poly if total is None else dot_high(total, poly)
        if iteration + 1 < NS_ITERS:
            gram = dot_high(dot_high(gram, poly), poly)
    map_buf[...] = total / norm_value
    for group in range(4):
        rows = rows_buf[group * 8 + dp_index].astype(wide)
        products[group] = dot_high(rows, map_buf[...]).astype(products.dtype)


def newton_schulz_rows(next_all):
    return pl.pallas_call(
        ns_kernel,
        out_shape=jax.ShapeDtypeStruct((4, 64, C), low),
        in_specs=[pl.BlockSpec(memory_space=pl.ANY)],
        out_specs=pl.BlockSpec(memory_space=pltpu.VMEM),
        scratch_shapes=[
            pltpu.VMEM((32, 64, C), low),
            pltpu.VMEM((C, C), wide),
            pltpu.SemaphoreType.DMA,
        ],
        compiler_params=pltpu.CompilerParams(vmem_limit_bytes=40 * 1024 * 1024),
        name="newton_schulz",
    )(next_all)


def swap_kernel(products, swapped, send_sem, recv_sem):
    mp_index = lax.axis_index("mp")
    barrier = pltpu.get_barrier_semaphore()
    peers = [lax.rem(mp_index + shift, 4) for shift in (1, 2, 3)]
    for peer in peers:
        pl.semaphore_signal(
            barrier, inc=1, device_id={"dp": lax.axis_index("dp"), "mp": peer}, device_id_type=MESH
        )
    pl.semaphore_wait(barrier, 3)

    def send(which):
        return remote(
            products.at[peers[which]], swapped.at[mp_index], send_sem.at[which], recv_sem.at[which],
            {"dp": lax.axis_index("dp"), "mp": peers[which]},
        )

    for which in range(3):
        send(which).start()
    swapped[mp_index] = products[mp_index]
    for which in range(3):
        source = peers[2 - which]
        remote(
            products.at[source], swapped.at[source], send_sem.at[which], recv_sem.at[which],
            {"dp": lax.axis_index("dp"), "mp": source},
        ).wait_recv()
        send(which).wait_send()


def swap_rows(products):
    vmem = pl.BlockSpec(memory_space=pltpu.VMEM)
    return pl.pallas_call(
        swap_kernel,
        out_shape=jax.ShapeDtypeStruct(products.shape, products.dtype),
        in_specs=[vmem],
        out_specs=vmem,
        scratch_shapes=[pltpu.SemaphoreType.DMA((3,)), pltpu.SemaphoreType.DMA((3,))],
        compiler_params=pltpu.CompilerParams(collective_id=2, has_side_effects=True),
        name="swap_rows",
    )(products)


def split_low(values):
    high = lax.reduce_precision(values, exponent_bits=8, mantissa_bits=7)
    return high.astype(jnp.bfloat16), (values - high).astype(jnp.bfloat16)


def dot_three(left, right):
    left_high, left_rest = left
    right_high, right_rest = right
    wide = dict(preferred_element_type=jnp.float32)
    return (
        jnp.dot(left_rest, right_high, **wide)
        + jnp.dot(left_high, right_rest, **wide)
        + jnp.dot(left_high, right_high, **wide)
    )


def newton_schulz(gram):
    width = gram.shape[0]
    eye = jnp.eye(width, dtype=jnp.float32)
    norm_value = jnp.sqrt(jnp.sum(gram * eye)) + ns_eps
    gram = gram / (norm_value * norm_value)
    total = None
    for iteration in range(NS_ITERS):
        parts = split_low(gram)
        square = dot_three(parts, parts)
        poly = coef_a * eye + (coef_b * gram + coef_c * square)
        poly_parts = split_low(poly)
        total = poly if total is None else dot_three(split_low(total), poly_parts)
        if iteration + 1 < NS_ITERS:
            half = dot_three(parts, poly_parts)
            gram = dot_three(split_low(half), poly_parts)
    return total / norm_value


def adam_update(grad_sum, first_moment, second_moment):
    first_new = adam_one * first_moment + (1.0 - adam_one) * grad_sum
    second_new = adam_two * second_moment + (1.0 - adam_two) * grad_sum * grad_sum
    first_hat = first_new / (1.0 - adam_one**adam_step)
    second_hat = second_new / (1.0 - adam_two**adam_step)
    return (-adam_rate * first_hat / (jnp.sqrt(second_hat) + adam_eps), first_new, second_new)


def exchange_plain(own_low, own_moments, rows):
    everyone = ("mp", "dp")
    starts = [sum(rows[:which]) for which in range(4)]

    def cut(stacked):
        return [stacked[:, start : start + count] for start, count in zip(starts, rows)]

    gathered = [
        part.reshape(-1, C) for part in cut(lax.all_gather(own_low, everyone, axis=0, tiled=False))
    ]

    def finish(big_local):
        mp_size, dp_size = lax.axis_size("mp"), lax.axis_size("dp")
        mp_index, dp_index = lax.axis_index("mp"), lax.axis_index("dp")
        devices = mp_size * dp_size
        stacked_grads = jnp.concatenate(
            [grad.reshape(devices, count, C) for grad, count in zip(big_local, rows)], axis=1
        )
        own_grads = lax.psum_scatter(
            stacked_grads.reshape(devices * sum(rows), C), everyone, scatter_dimension=0, tiled=True
        ).astype(wide)
        own_buffers = muon_beta * own_moments + own_grads
        own_nesterov = own_grads + muon_beta * own_buffers
        iterate_all = lax.all_gather(own_nesterov.astype(low), everyone, axis=0, tiled=False)
        grams = jnp.stack([dot_tn(part.reshape(-1, C), part.reshape(-1, C)) for part in cut(iterate_all)])
        ortho_map = newton_schulz(lax.dynamic_index_in_dim(grams, mp_index, 0, keepdims=False))
        most = max(rows)
        picked = lax.dynamic_slice(
            iterate_all.reshape(mp_size, dp_size, sum(rows), C),
            (
                jnp.int32(0),
                dp_index.astype(jnp.int32),
                jnp.array(starts, jnp.int32)[mp_index],
                jnp.int32(0),
            ),
            (mp_size, 1, most, C),
        ).reshape(mp_size * most, C)
        map_parts = split_low(ortho_map)
        products = dot(picked, map_parts[0]) + dot(picked, map_parts[1])
        swapped = lax.all_to_all(products.reshape(mp_size, most, C), "mp", 0, 0, tiled=False)
        return own_grads, own_buffers, swapped

    return gathered, finish


def shards(
    images,
    cotangent,
    qkv_weight,
    proj_weight,
    expand_weight,
    contract_weight,
    qkv_moment,
    proj_moment,
    expand_moment,
    contract_moment,
    vectors,
    qv_bias,
    expand_bias,
    rel_table,
    vectors_first,
    vectors_second,
    qv_first,
    qv_second,
    expand_bias_first,
    expand_bias_second,
    table_first,
    table_second,
    region_ids,
    pos_index,
    image_counts,
):
    everyone = ("mp", "dp")
    mp_size, dp_size = lax.axis_size("mp"), lax.axis_size("dp")
    mp_index = lax.axis_index("mp")
    linked = mp_size == 4 and dp_size == 8
    per_device = IMG_DEV // mp_size
    place = jnp.stack([(mp_index * per_device).astype(jnp.int32), image_counts[0]])
    weights_all = (qkv_weight, proj_weight, expand_weight, contract_weight)
    rows = [weight.shape[0] for weight in weights_all]
    starts = [sum(rows[:which]) for which in range(4)]
    own_low = jnp.concatenate([weight.astype(low) for weight in weights_all], axis=0)
    own_moments = jnp.concatenate(
        (qkv_moment, proj_moment, expand_moment, contract_moment), axis=0
    )
    if linked:
        misc = jnp.concatenate(
            [
                expand_bias[None],
                jnp.pad(qv_bias.reshape(1, -1), ((0, 0), (0, C - qv_bias.size))),
                jnp.pad(rel_table.T, ((0, 2), (0, C - TABLE))),
            ],
            axis=0,
        )
        gathered, misc_all = gather_all(own_low, misc)
        expand_full = misc_all[:, 0].reshape(4, C)
        qv_full = misc_all[:, 1, : qv_bias.size].reshape(4, 2, -1).transpose(1, 0, 2).reshape(2, C)
        table_full = misc_all[:, 2:6, :TABLE].reshape(HEADS, TABLE)
    else:
        gathered, finish_plain = exchange_plain(own_low, own_moments, rows)
        qv_full = lax.all_gather(qv_bias, "mp", axis=1, tiled=True)
        expand_full = lax.all_gather(expand_bias, "mp", axis=0, tiled=True).reshape(4, C)
        table_full = lax.all_gather(rel_table.T, "mp", axis=0, tiled=True)
    onehot = (
        jnp.arange(TABLE, dtype=jnp.int32)[:, None] == pos_index.reshape(1, SPAN * SPAN)
    ).astype(wide)
    pos_bias = jnp.dot(table_full, onehot, precision=highest).reshape(HEADS, SPAN, SPAN)
    window_regions = to_windows(region_ids.reshape(1, TOK, 1))[:, :, 0]
    window_mask = jnp.where(
        window_regions[:, :, None] != window_regions[:, None, :], mask_value, 0.0
    ).astype(wide)
    bias = pair_bias(pos_bias, window_mask)
    block_low, input_low, big_local, small_rows, table_pairs = run_layer(
        linked, per_device, place, images, cotangent, vectors, qv_full, expand_full, bias, gathered
    )
    block_out = lax.all_gather(block_low, "mp", axis=0, tiled=True)
    input_grad = lax.all_gather(input_low, "mp", axis=0, tiled=True)
    pairs = table_pairs.reshape(HEADS, PAIR, PAIR)
    bias_heads = pairs[:, :SPAN, :SPAN] + pairs[:, SPAN : 2 * SPAN, SPAN : 2 * SPAN]
    table_local = lax.dot_general(
        bias_heads.reshape(HEADS, SPAN * SPAN),
        onehot,
        (((1,), (1,)), ((), ())),
        precision=highest,
        preferred_element_type=wide,
    )
    small_full, table_all = lax.psum((small_rows, table_local), everyone)
    if linked:
        own_grads, own_buffers, next_all = muon_exchange(big_local, own_moments)
        swapped = swap_rows(newton_schulz_rows(next_all))
    else:
        own_grads, own_buffers, swapped = finish_plain(big_local)
    ortho = [swapped[which, :count].astype(wide) for which, count in enumerate(rows)]
    shares = [own_grads[start : start + count] for start, count in zip(starts, rows)]
    buffers = [own_buffers[start : start + count] for start, count in zip(starts, rows)]

    def own_columns(full, width):
        return lax.dynamic_slice_in_dim(full, mp_index * width, width, full.ndim - 1)

    small_sums = (
        small_full[:6],
        own_columns(small_full[6:8], qv_bias.shape[1]),
        own_columns(small_full[8:12].reshape(FF), expand_bias.shape[0]),
        lax.dynamic_slice_in_dim(table_all, mp_index * rel_table.shape[1], rel_table.shape[1], 0).T,
    )
    factors = (math.sqrt(3.0), 1.0, math.sqrt(max(1.0, FF / C)), 1.0)
    new_steps = tuple(
        (
            -muon_rate * (muon_decay * weight + factor * ortho_part)
            for weight, ortho_part, factor in zip(weights_all, ortho, factors)
        )
    )
    vectors_step, vectors_first_new, vectors_second_new = adam_update(
        small_sums[0], vectors_first, vectors_second
    )
    qv_step, qv_first_new, qv_second_new = adam_update(small_sums[1], qv_first, qv_second)
    expand_bias_step, expand_bias_first_new, expand_bias_second_new = adam_update(
        small_sums[2], expand_bias_first, expand_bias_second
    )
    table_step, table_first_new, table_second_new = adam_update(
        small_sums[3], table_first, table_second
    )
    return (
        block_out,
        input_grad,
        shares[0],
        shares[1],
        shares[2],
        shares[3],
        small_sums[0],
        small_sums[1],
        small_sums[2],
        small_sums[3],
        new_steps[0],
        new_steps[1],
        new_steps[2],
        new_steps[3],
        buffers[0],
        buffers[1],
        buffers[2],
        buffers[3],
        vectors_step,
        qv_step,
        expand_bias_step,
        table_step,
        vectors_first_new,
        vectors_second_new,
        qv_first_new,
        qv_second_new,
        expand_bias_first_new,
        expand_bias_second_new,
        table_first_new,
        table_second_new,
    )


def solution(mesh):
    return jax.shard_map(
        shards,
        mesh=mesh,
        in_specs=(
            P("dp", None, None),
            P("dp", None, None),
            P(("mp", "dp"), None),
            P(("mp", "dp"), None),
            P(("mp", "dp"), None),
            P(("mp", "dp"), None),
            P(("mp", "dp"), None),
            P(("mp", "dp"), None),
            P(("mp", "dp"), None),
            P(("mp", "dp"), None),
            P(),
            P(None, "mp"),
            P("mp"),
            P(None, "mp"),
            P(),
            P(),
            P(None, "mp"),
            P(None, "mp"),
            P("mp"),
            P("mp"),
            P(None, "mp"),
            P(None, "mp"),
            P(),
            P(),
            P("dp"),
        ),
        out_specs=(
            P("dp", None, None),
            P("dp", None, None),
            P(("mp", "dp"), None),
            P(("mp", "dp"), None),
            P(("mp", "dp"), None),
            P(("mp", "dp"), None),
            P(),
            P(None, "mp"),
            P("mp"),
            P(None, "mp"),
            P(("mp", "dp"), None),
            P(("mp", "dp"), None),
            P(("mp", "dp"), None),
            P(("mp", "dp"), None),
            P(("mp", "dp"), None),
            P(("mp", "dp"), None),
            P(("mp", "dp"), None),
            P(("mp", "dp"), None),
            P(),
            P(None, "mp"),
            P("mp"),
            P(None, "mp"),
            P(),
            P(),
            P(None, "mp"),
            P(None, "mp"),
            P("mp"),
            P("mp"),
            P(None, "mp"),
            P(None, "mp"),
        ),
        check_vma=False,
    )
```

```python
import functools
import math

import jax
import jax.numpy as jnp
import numpy as np
from jax import lax
from jax.experimental import pallas as pl
from jax.experimental.pallas import tpu as pltpu
from jax.sharding import PartitionSpec as P

C = 512
HEADS = 16
HD = 32
FF = 2048
WIN = 7
SIDE = 14
SHIFT = 3
SPAN = WIN * WIN
TOK = SIDE * SIDE
NS_ITERS = 5
IMG_DEV = 16
TABLE = 169
PAIR = 112
ROWS = 2 * PAIR
GROUP = 4

norm_eps = 1e-05
ns_eps = 1e-07
coef_a = 3.4445
coef_b = -4.775
coef_c = 2.0315
muon_rate = 0.3
muon_decay = 0.1
muon_beta = 0.95
adam_rate = 0.1
adam_one = 0.9
adam_two = 0.999
adam_eps = 1e-08
adam_step = 4
mask_value = -100.0
away = -1e30
wide = jnp.float32
low = jnp.bfloat16
highest = lax.Precision.HIGHEST


def to_windows(field_values):
    image_total = field_values.shape[0]
    channels = field_values.shape[-1]
    blocks = SIDE // WIN
    grid_values = field_values.reshape(image_total, SIDE, SIDE, channels)
    grid_values = jnp.roll(grid_values, (-SHIFT, -SHIFT), axis=(1, 2))
    grid_values = grid_values.reshape(image_total, blocks, WIN, blocks, WIN, channels)
    grid_values = grid_values.transpose(0, 1, 3, 2, 4, 5)
    return grid_values.reshape(image_total * blocks * blocks, WIN * WIN, channels)


def window_order():
    order = np.full((ROWS,), -1, np.int64)
    for window in range(4):
        top, left = window // 2, window % 2
        for token in range(SPAN):
            row = (top * WIN + token // WIN + SHIFT) % SIDE
            column = (left * WIN + token % WIN + SHIFT) % SIDE
            order[(window // 2) * PAIR + (window % 2) * SPAN + token] = row * SIDE + column
    return order


def dot(a, b):
    return jnp.dot(a, b, preferred_element_type=wide)


def dot_nt(a, b):
    return lax.dot_general(a, b, (((1,), (1,)), ((), ())), preferred_element_type=wide)


def dot_tn(a, b):
    return lax.dot_general(a, b, (((0,), (0,)), ((), ())), preferred_element_type=wide)


def mean_of(values):
    return jnp.sum(values, axis=-1, keepdims=True) * (1.0 / C)


def normalize(values):
    centered = values - mean_of(values)
    inv_scale = lax.rsqrt(mean_of(centered * centered) + norm_eps)
    return centered * inv_scale, inv_scale


def normalize_back(grad_norm, normed, inv_scale, gain):
    scaled = grad_norm * gain
    return inv_scale * (scaled - mean_of(scaled) - normed * mean_of(scaled * normed))


def column_sum(values):
    return jnp.sum(values, axis=0, keepdims=True)


def head_masks():
    lane = lax.broadcasted_iota(jnp.int32, (1, 128), 1) // HD
    return [(lane == head).astype(wide).astype(low) for head in range(GROUP)]


def stack_heads(block, masks):
    return jnp.concatenate([block * mask for mask in masks], axis=0)


def pick_heads(stacked):
    lane = lax.broadcasted_iota(jnp.int32, (PAIR, 128), 1)
    parts = [stacked[PAIR * head : PAIR * (head + 1)] for head in range(GROUP)]
    return jnp.where(
        lane < 2 * HD,
        jnp.where(lane < HD, parts[0], parts[1]),
        jnp.where(lane < 3 * HD, parts[2], parts[3]),
    )


def layer_kernel(
    packed, place, images, cotangent, order, order_back, vectors, qv_bias, expand_bias, bias,
    qkv_hbm, proj_hbm, expand_hbm, contract_hbm,
    block_out, input_grad, *rest,
):
    n_grads = 1 if packed else 4
    grad_outs = rest[:n_grads]
    (small, table_sum, qkv_nat, qkv_w, proj_w, expand_w, contract_w,
     qkv_acc, proj_acc, expand_acc, contract_acc,
     qkv_s, att_s, back_s, probs_s, normed_s, first_s, middle_s, normed2_s, second_s,
     out_low_s, mlp_s, second_grad_s, sems) = rest[n_grads : n_grads + 24]
    step = pl.program_id(0)
    steps = pl.num_programs(0)
    masks = head_masks()
    if packed:
        staged, keep_sem, act_send, act_recv = rest[n_grads + 24 :]
        dp_index, mp_index = lax.axis_index("dp"), lax.axis_index("mp")
        per_device = staged.shape[1]

        def peer(shift):
            return {"dp": dp_index, "mp": lax.rem(mp_index + shift, 4)}

        def keep_copy(kind, image):
            out = (block_out, input_grad)[kind]
            return pltpu.make_async_copy(
                staged.at[kind, image], out.at[mp_index * per_device + image], keep_sem.at[kind, image]
            )

        def send_copy(kind, image, shift):
            out = (block_out, input_grad)[kind]
            return remote(
                staged.at[kind, image], out.at[mp_index * per_device + image],
                act_send.at[kind, image, shift - 1], act_recv.at[kind, image, shift - 1], peer(shift),
            )

        def arrival(kind, image, shift):
            out = (block_out, input_grad)[kind]
            source = lax.rem(mp_index + 4 - shift, 4)
            return remote(
                staged.at[kind, image], out.at[source * per_device + image],
                act_send.at[kind, image, shift - 1], act_recv.at[kind, image, shift - 1], peer(shift),
            )

        def greet():
            barrier = pltpu.get_barrier_semaphore()
            for shift in (1, 2, 3):
                pl.semaphore_signal(barrier, inc=1, device_id=peer(shift), device_id_type=MESH)
            pl.semaphore_wait(barrier, 3)

        pl.when(step == 0)(greet)

    def put(kind, value):
        if packed:
            staged[kind, step] = value
            for shift in (2, 3, 1):
                send_copy(kind, step, shift).start()
            keep_copy(kind, step).start()
        else:
            (block_out, input_grad)[kind][0] = value

    live = place[1] > place[0] + step
    live_scale = live.astype(wide)

    def fetch(which):
        if packed:
            counts = (48, 16, 64, 64)
            source = qkv_hbm.at[:, pl.ds(sum(counts[:which]), counts[which])]
            target = (qkv_nat, proj_w, expand_w, contract_w)[which]
        else:
            source = (qkv_hbm, proj_hbm, expand_hbm, contract_hbm)[which]
            target = (qkv_nat, proj_w, expand_w, contract_w)[which]
        return pltpu.make_async_copy(source, target, sems.at[which])

    def rows_of(ref, count):
        return ref[...].reshape(count, C)

    def begin():
        for which in range(4):
            fetch(which).start()
        for ref in (qkv_acc, proj_acc, expand_acc, contract_acc, small, table_sum):
            ref[...] = jnp.zeros_like(ref)
        for which in range(4):
            fetch(which).wait()
        natural = rows_of(qkv_nat, 3 * C).reshape(HEADS, 3, HD, C)
        for kind in range(3):
            qkv_w[kind] = natural[:, kind].reshape(C, C)

    pl.when(step == 0)(begin)

    tokens = dot(order[...], images[0])
    normed, inv_one = normalize(tokens)
    normed_s[...] = normed
    first_in = (normed * vectors[0:1] + vectors[1:2]).astype(low)
    first_s[...] = first_in
    for kind in range(3):
        projected = dot_nt(first_in, qkv_w[kind])
        if kind != 1:
            projected = projected + qv_bias[kind // 2 : kind // 2 + 1]
        projected = projected.astype(low)
        for group in range(4):
            qkv_s[kind * 4 + group] = projected[:, 128 * group : 128 * (group + 1)]
    score_scale = 1.0 / math.sqrt(HD)

    def attend(which, carry):
        pair, group = which // 4, which % 4
        rows = pl.ds(pl.multiple_of(pair * PAIR, 16), PAIR)
        queries = stack_heads(qkv_s[group, rows], masks)
        scores = dot_nt(queries, qkv_s[4 + group, rows]) * score_scale + bias[pair, group]
        top = jnp.max(scores, axis=-1, keepdims=True)
        exponent = jnp.exp(scores - top)
        attention = exponent / jnp.sum(exponent, axis=-1, keepdims=True)
        probs_s[which] = attention
        att_s[group, rows] = pick_heads(dot(attention.astype(low), qkv_s[8 + group, rows])).astype(low)
        return carry

    lax.fori_loop(0, 8, attend, 0)
    attended = jnp.concatenate([att_s[group] for group in range(4)], axis=1)
    middle = tokens + (dot(attended, rows_of(proj_w, C)) + vectors[4:5])
    middle_s[...] = middle
    normed_two, inv_two = normalize(middle)
    normed2_s[...] = normed_two
    second_in = (normed_two * vectors[2:3] + vectors[3:4]).astype(low)
    second_s[...] = second_in

    out_low = (dot(order[...], cotangent[0]) * live_scale).astype(low)
    out_low_s[...] = out_low
    mlp_s[...] = jnp.zeros_like(mlp_s)
    second_grad_s[...] = jnp.zeros_like(second_grad_s)
    chunk = 512
    owners = expand_w.shape[0] // (FF // chunk)

    def feed(which, carry):
        units = pl.ds(pl.multiple_of(which * owners, owners), owners)
        expand_part = expand_w[units].reshape(chunk, C)
        contract_part = contract_w[units].reshape(chunk, C)
        second = second_s[...]
        grad_rows = out_low_s[...]
        hidden = dot_nt(second, expand_part) + expand_bias[which]
        cumulative = 0.5 * (1.0 + lax.erf(hidden * (1.0 / math.sqrt(2.0))))
        acted = (hidden * cumulative).astype(low)
        slope = cumulative + hidden * jnp.exp(-0.5 * hidden * hidden) * (1.0 / math.sqrt(2.0 * math.pi))
        mlp_s[...] += dot(acted, contract_part)
        hidden_grad32 = dot_nt(grad_rows, contract_part) * slope
        hidden_grad = hidden_grad32.astype(low)
        small[pl.ds(8 + which, 1)] += column_sum(hidden_grad.astype(wide))
        second_grad_s[...] += dot(hidden_grad, expand_part)
        units_wide = pl.ds(pl.multiple_of(which * chunk, chunk), chunk)
        contract_acc[units_wide] += dot_tn(acted, grad_rows)
        expand_acc[units_wide] += dot_tn(hidden_grad, second)
        return carry

    lax.fori_loop(0, FF // chunk, feed, 0)
    result = middle_s[...] + (mlp_s[...] + vectors[5:6])
    result = jnp.where(live, result, 0.0).astype(low)
    put(0, dot(order_back[...], result).astype(low))

    grad_out = out_low_s[...].astype(wide)
    second_grad = second_grad_s[...]
    normed_two = normed2_s[...]
    small[5:6] += column_sum(grad_out)
    small[3:4] += column_sum(second_grad)
    small[2:3] += column_sum(second_grad * normed_two)
    middle_grad = grad_out + normalize_back(second_grad, normed_two, inv_two, vectors[2:3])
    small[4:5] += column_sum(middle_grad)
    middle_s[...] = middle_grad
    attn_low = middle_grad.astype(low)
    attended = jnp.concatenate([att_s[group] for group in range(4)], axis=1)
    proj_acc[...] += dot_tn(attended, attn_low)
    attended_grad = dot_nt(attn_low, rows_of(proj_w, C)).astype(low)
    for group in range(4):
        att_s[group] = attended_grad[:, 128 * group : 128 * (group + 1)]

    def attend_back(which, carry):
        pair, group = which // 4, which % 4
        rows = pl.ds(pl.multiple_of(pair * PAIR, 16), PAIR)
        attention = probs_s[which]
        keys, values = qkv_s[4 + group, rows], qkv_s[8 + group, rows]
        grads = stack_heads(att_s[group, rows], masks)
        queries = stack_heads(qkv_s[group, rows], masks)
        probs_grad = dot_nt(grads, values)
        row_term = jnp.sum(attention * probs_grad, axis=-1, keepdims=True)
        score_grad = (attention * (probs_grad - row_term)).astype(low)
        table_sum[group] += score_grad.astype(wide)
        back_s[group, rows] = (pick_heads(dot(score_grad, keys)) * score_scale).astype(low)
        back_s[4 + group, rows] = (dot_tn(score_grad, queries) * score_scale).astype(low)
        back_s[8 + group, rows] = dot_tn(attention.astype(low), grads).astype(low)
        return carry

    lax.fori_loop(0, 8, attend_back, 0)
    first_in = first_s[...]
    first_grad = None
    for kind in range(3):
        back = jnp.concatenate([back_s[kind * 4 + group] for group in range(4)], axis=1)
        if kind != 1:
            row = 6 + kind // 2
            small[row : row + 1] += column_sum(back.astype(wide))
        qkv_acc[kind] += dot_tn(back, first_in)
        part = dot(back, qkv_w[kind])
        first_grad = part if first_grad is None else first_grad + part
    normed = normed_s[...]
    small[1:2] += column_sum(first_grad)
    small[0:1] += column_sum(first_grad * normed)
    token_grad = middle_s[...] + normalize_back(first_grad, normed, inv_one, vectors[0:1])
    put(1, dot(order_back[...], token_grad.astype(low)).astype(low))

    def finish():
        for kind in range(3):
            part = qkv_acc[kind].astype(low).reshape(HEADS, HD, C)
            if packed:
                out = grad_outs[0]
                for piece in range(2):
                    block = kind * 2 + piece
                    out[:, block // 3, pl.ds(16 * (block % 3), 16)] = part[:, 16 * piece : 16 * (piece + 1)]
            else:
                grad_outs[0][:, kind] = part
        if packed:
            out = grad_outs[0]
            out[:, :, pl.ds(48, 16)] = proj_acc[...].astype(low).reshape(16, 2, 16, C)
            out[:, :, pl.ds(64, 64)] = expand_acc[...].astype(low).reshape(16, 2, 64, C)
            out[:, :, pl.ds(128, 64)] = contract_acc[...].astype(low).reshape(16, 2, 64, C)
        else:
            grad_outs[1][...] = proj_acc[...].astype(low)
            grad_outs[2][...] = expand_acc[...].astype(low)
            grad_outs[3][...] = contract_acc[...].astype(low)
        if packed:

            def settle(image, carry):
                for kind in (0, 1):
                    for shift in (2, 3, 1):
                        arrival(kind, image, shift).wait_recv()
                        send_copy(kind, image, shift).wait_send()
                    keep_copy(kind, image).wait()
                return carry

            lax.fori_loop(0, per_device, settle, 0)

    pl.when(step == steps - 1)(finish)


def run_layer(packed, per_device, place, images, cotangent, vectors, qv_bias, expand_bias, bias, weights):
    order_np = window_order()
    onehot = (order_np[:, None] == np.arange(TOK)[None, :]).astype(np.float32)
    order = jnp.asarray(onehot, low)
    order_back = jnp.asarray(onehot.T, low)
    any_spec = pl.BlockSpec(memory_space=pl.ANY)

    def whole(shape):
        return pl.BlockSpec(shape, lambda i, s: (0,) * len(shape), pipeline_mode=pl.Buffered(1))

    image_spec = pl.BlockSpec((1, TOK, C), lambda i, s: (i, 0, 0))
    out_spec = any_spec if packed else pl.BlockSpec((1, TOK, C), lambda i, s: (i, 0, 0))
    images_out = IMG_DEV if packed else per_device
    exchange = [
        pltpu.VMEM((2, per_device, TOK, C), low),
        pltpu.SemaphoreType.DMA((2, per_device)),
        pltpu.SemaphoreType.DMA((2, per_device, 3)),
        pltpu.SemaphoreType.DMA((2, per_device, 3)),
    ]
    limit = 60 * 1024 * 1024
    if packed:
        params = pltpu.CompilerParams(collective_id=3, has_side_effects=True, vmem_limit_bytes=limit)
    else:
        params = pltpu.CompilerParams(vmem_limit_bytes=limit)
    if packed:
        weights = (weights,) * 4
        grad_shapes = [(16, 2, 192, C)]
        weight_shapes = [(32, 48, C), (32, 16, C), (32, 64, C), (32, 64, C)]
    else:
        weights = (weights[0], weights[1], weights[2].reshape(FF // 64, 64, C), weights[3].reshape(FF // 64, 64, C))
        grad_shapes = [(HEADS, 3, HD, C), (C, C), (FF, C), (FF, C)]
        weight_shapes = [w.shape for w in weights]
    outs = pl.pallas_call(
        functools.partial(layer_kernel, packed),
        out_shape=[
            jax.ShapeDtypeStruct((images_out, TOK, C), low),
            jax.ShapeDtypeStruct((images_out, TOK, C), low),
            *[jax.ShapeDtypeStruct(shape, low) for shape in grad_shapes],
            jax.ShapeDtypeStruct((16, C), wide),
            jax.ShapeDtypeStruct((4, GROUP * PAIR, PAIR), wide),
        ],
        grid_spec=pltpu.PrefetchScalarGridSpec(
            num_scalar_prefetch=1,
            grid=(per_device,),
            in_specs=[
                image_spec, image_spec, whole((ROWS, TOK)), whole((TOK, ROWS)), whole((6, C)), whole((2, C)),
                whole((4, 1, C)), whole((2, 4, GROUP * PAIR, PAIR)), any_spec, any_spec, any_spec, any_spec,
            ],
            out_specs=[out_spec, out_spec]
            + [whole(shape) for shape in grad_shapes]
            + [whole((16, C)), whole((4, GROUP * PAIR, PAIR))],
            scratch_shapes=[pltpu.VMEM(shape, low) for shape in weight_shapes[:1]]
            + [pltpu.VMEM((3, C, C), low)]
            + [pltpu.VMEM(shape, low) for shape in weight_shapes[1:]]
            + [
                pltpu.VMEM((3, C, C), wide),
                pltpu.VMEM((C, C), wide),
                pltpu.VMEM((FF, C), wide),
                pltpu.VMEM((FF, C), wide),
                pltpu.VMEM((12, ROWS, 128), low),
                pltpu.VMEM((4, ROWS, 128), low),
                pltpu.VMEM((12, ROWS, 128), low),
                pltpu.VMEM((8, GROUP * PAIR, PAIR), wide),
                pltpu.VMEM((ROWS, C), wide),
                pltpu.VMEM((ROWS, C), low),
                pltpu.VMEM((ROWS, C), wide),
                pltpu.VMEM((ROWS, C), wide),
                pltpu.VMEM((ROWS, C), low),
                pltpu.VMEM((ROWS, C), low),
                pltpu.VMEM((ROWS, C), wide),
                pltpu.VMEM((ROWS, C), wide),
                pltpu.SemaphoreType.DMA((4,)),
            ]
            + (exchange if packed else []),
        ),
        compiler_params=params,
        name="window_layer",
    )(place, images, cotangent, order, order_back, vectors, qv_bias, expand_bias.reshape(4, 1, C), bias, *weights)
    grads = outs[2 : 2 + len(grad_shapes)]
    grads = grads[0].reshape(32, 192, C) if packed else [g.reshape(-1, C) for g in grads]
    return outs[0], outs[1], grads, outs[-2], outs[-1]


def pair_bias(pos_bias, window_mask):
    heads = pos_bias.shape[0]
    scores = pos_bias[None] + window_mask[:, None]
    scores = scores.reshape(2, 2, heads, SPAN, SPAN)
    first = jnp.pad(scores[:, 0], ((0, 0), (0, 0), (0, 0), (0, PAIR - SPAN)), constant_values=away)
    second = jnp.pad(scores[:, 1], ((0, 0), (0, 0), (0, 0), (SPAN, PAIR - 2 * SPAN)), constant_values=away)
    rest = jnp.broadcast_to(
        jnp.where(jnp.arange(PAIR) < SPAN, 0.0, away).astype(wide), (2, heads, PAIR - 2 * SPAN, PAIR)
    )
    return jnp.concatenate([first, second, rest], axis=2).reshape(2, heads // GROUP, GROUP * PAIR, PAIR)


MESH = pl.DeviceIdType.MESH
DEPTH = 4


class Place:
    def __init__(self):
        dp_index, mp_index = lax.axis_index("dp"), lax.axis_index("mp")
        self.z, self.x = dp_index // 2, dp_index % 2
        self.y, self.core = mp_index // 2, mp_index % 2
        self.dp_index, self.mp_index = dp_index, mp_index
        self.x_side = self.device(self.z, 1 - self.x, self.y, self.core)
        self.y_side = self.device(self.z, self.x, 1 - self.y, self.core)
        self.partner = self.device(self.z, self.x, self.y, 1 - self.core)
        self.above = self.device(self.z + 1, self.x, self.y, self.core)
        self.below = self.device(self.z - 1, self.x, self.y, self.core)
        self.z_near = self.device(self.z + 1 - 2 * lax.rem(self.z, 2), self.x, self.y, self.core)
        self.z_far = self.device(lax.rem(self.z + 2, DEPTH), self.x, self.y, self.core)

    @staticmethod
    def device(z, x, y, core):
        return {"dp": z * 2 + x, "mp": y * 2 + core}

    @staticmethod
    def owner(z, x, y, core):
        return (y * 2 + core) * 8 + z * 2 + x

    def greet(self, far=False):
        barrier = pltpu.get_barrier_semaphore()

        def signal(device):
            pl.semaphore_signal(barrier, inc=1, device_id=device, device_id_type=MESH)

        signal(self.x_side)
        signal(self.y_side)
        signal(self.partner)
        pl.when(self.z > 0)(lambda: signal(self.below))
        pl.when(self.z < DEPTH - 1)(lambda: signal(self.above))
        if far:
            signal(self.z_far)
        ends = (self.z == 0).astype(jnp.int32) + (self.z == DEPTH - 1).astype(jnp.int32)
        pl.semaphore_wait(barrier, (6 if far else 5) - ends)


def remote(src, dst, send_sem, recv_sem, device):
    return pltpu.make_async_remote_copy(
        src_ref=src,
        dst_ref=dst,
        send_sem=send_sem,
        recv_sem=recv_sem,
        device_id=device,
        device_id_type=MESH,
    )


def spread(at, own_ref, out_ref, own_sem, z_send, z_recv, side_send, side_recv, pair_send, pair_recv):
    rows = own_ref.shape[0]
    half = rows // 2
    z, x, y, core = at.z, at.x, at.y, at.core
    low, high = pl.ds(0, half), pl.ds(half, rows - half)

    def slot(source_z, other_x, other_y):
        return out_ref.at[
            at.owner(source_z, 1 - x if other_x else x, 1 - y if other_y else y, core)
        ]

    def up(source_z, src=None):
        dst = slot(source_z, False, False)
        return remote(dst if src is None else src, dst, z_send.at[0, source_z], z_recv.at[0, source_z], at.above)

    def down(source_z, src=None):
        dst = slot(source_z, False, False)
        return remote(dst if src is None else src, dst, z_send.at[1, source_z], z_recv.at[1, source_z], at.below)

    def side(kind, source_z, src=None):
        if kind == 0 or kind == 1:
            dst = slot(source_z, False, False)
        elif kind == 2:
            dst = slot(source_z, True, False).at[low]
        else:
            dst = slot(source_z, False, True).at[high]
        device = at.x_side if kind in (0, 3) else at.y_side
        return remote(
            dst if src is None else src, dst, side_send.at[kind, source_z], side_recv.at[kind, source_z], device
        )

    def side_arrival(kind, source_z):
        if kind == 0:
            dst = slot(source_z, True, False)
        elif kind == 1:
            dst = slot(source_z, False, True)
        elif kind == 2:
            dst = slot(source_z, True, True).at[low]
        else:
            dst = slot(source_z, True, True).at[high]
        device = at.x_side if kind in (0, 3) else at.y_side
        return remote(dst, dst, side_send.at[kind, source_z], side_recv.at[kind, source_z], device)

    def pair_region(kind, source_z, of_core):
        other_x, other_y = ((False, False), (True, False), (False, True), (True, True), (True, True))[kind]
        ref = out_ref.at[at.owner(source_z, 1 - x if other_x else x, 1 - y if other_y else y, of_core)]
        if kind == 3:
            ref = ref.at[low]
        elif kind == 4:
            ref = ref.at[high]
        return ref

    def pair(kind, source_z, src=None):
        dst = pair_region(kind, source_z, core)
        return remote(
            dst if src is None else src, dst, pair_send.at[kind, source_z], pair_recv.at[kind, source_z], at.partner
        )

    def pair_arrival(kind, source_z):
        dst = pair_region(kind, source_z, 1 - core)
        return remote(dst, dst, pair_send.at[kind, source_z], pair_recv.at[kind, source_z], at.partner)

    keep = pltpu.make_async_copy(own_ref, slot(z, False, False), own_sem)
    pl.when(z < DEPTH - 1)(lambda: up(z, own_ref).start())
    pl.when(z > 0)(lambda: down(z, own_ref).start())
    side(0, z, own_ref).start()
    side(1, z, own_ref).start()
    pair(0, z, own_ref).start()
    keep.start()

    def plane(source_z):
        side_arrival(0, source_z).wait_recv()
        side(2, source_z).start()
        pair(1, source_z).start()
        side_arrival(1, source_z).wait_recv()
        side(3, source_z).start()
        pair(2, source_z).start()

    def column(source_z):
        side(0, source_z).start()
        side(1, source_z).start()
        pair(0, source_z).start()

    for distance in range(1, DEPTH + 1):

        def from_below(source_z=z - distance):
            up(source_z).wait_recv()
            pl.when(z < DEPTH - 1)(lambda: up(source_z).start())
            column(source_z)

        def from_above(source_z=z + distance):
            down(source_z).wait_recv()
            pl.when(z > 0)(lambda: down(source_z).start())
            column(source_z)

        pl.when(z - distance >= 0)(from_below)
        pl.when(z + distance <= DEPTH - 1)(from_above)
        past = distance - 1
        if past == 0:
            plane(z)
        else:
            pl.when(z - past >= 0)(functools.partial(plane, z - past))
            pl.when(z + past <= DEPTH - 1)(functools.partial(plane, z + past))

    def corner(source_z):
        side_arrival(2, source_z).wait_recv()
        pair(3, source_z).start()
        side_arrival(3, source_z).wait_recv()
        pair(4, source_z).start()

    for distance in range(DEPTH):
        if distance == 0:
            corner(z)
        else:
            pl.when(z - distance >= 0)(functools.partial(corner, z - distance))
            pl.when(z + distance <= DEPTH - 1)(functools.partial(corner, z + distance))
    keep.wait()
    for source_z in range(DEPTH):
        for kind in range(5):
            pair_arrival(kind, source_z).wait_recv()
            pair(kind, source_z).wait_send()
        for kind in range(4):
            side(kind, source_z).wait_send()
        pl.when((z < DEPTH - 1) & (source_z <= z))(lambda: up(source_z).wait_send())
        pl.when((z > 0) & (source_z >= z))(lambda: down(source_z).wait_send())


SPREAD_SEMS = [
    pltpu.SemaphoreType.DMA,
    pltpu.SemaphoreType.DMA((2, DEPTH)),
    pltpu.SemaphoreType.DMA((2, DEPTH)),
    pltpu.SemaphoreType.DMA((4, DEPTH)),
    pltpu.SemaphoreType.DMA((4, DEPTH)),
    pltpu.SemaphoreType.DMA((5, DEPTH)),
    pltpu.SemaphoreType.DMA((5, DEPTH)),
]


def gather_kernel(own_ref, misc_ref, out_ref, misc_out, misc_send, misc_recv, *sems):
    at = Place()
    at.greet()
    to_pair = remote(misc_ref, misc_out.at[at.mp_index], misc_send.at[0], misc_recv.at[0], at.partner)
    to_side = remote(misc_ref, misc_out.at[at.mp_index], misc_send.at[1], misc_recv.at[1], at.y_side)
    to_pair.start()
    to_side.start()
    misc_out[at.mp_index] = misc_ref[...]
    over = (1 - at.y) * 2 + at.core
    from_side = remote(misc_ref, misc_out.at[over], misc_send.at[1], misc_recv.at[1], at.y_side)
    relay = remote(misc_out.at[over], misc_out.at[over], misc_send.at[2], misc_recv.at[2], at.partner)
    spread(at, own_ref, out_ref, *sems)
    from_side.wait_recv()
    relay.start()
    beside = at.y * 2 + 1 - at.core
    remote(misc_ref, misc_out.at[beside], misc_send.at[0], misc_recv.at[0], at.partner).wait_recv()
    across = (1 - at.y) * 2 + 1 - at.core
    remote(misc_ref, misc_out.at[across], misc_send.at[2], misc_recv.at[2], at.partner).wait_recv()
    to_pair.wait_send()
    to_side.wait_send()
    relay.wait_send()


def gather_all(own, misc):
    rows, columns = own.shape
    return pl.pallas_call(
        gather_kernel,
        out_shape=(
            jax.ShapeDtypeStruct((32, rows, columns), own.dtype),
            jax.ShapeDtypeStruct((4,) + misc.shape, misc.dtype),
        ),
        in_specs=[pl.BlockSpec(memory_space=pltpu.VMEM)] * 2,
        out_specs=(pl.BlockSpec(memory_space=pl.ANY), pl.BlockSpec(memory_space=pltpu.VMEM)),
        scratch_shapes=[pltpu.SemaphoreType.DMA((3,)), pltpu.SemaphoreType.DMA((3,))] + SPREAD_SEMS,
        compiler_params=pltpu.CompilerParams(collective_id=0, has_side_effects=True),
        name="gather_weights",
    )(own, misc)


def collect(at, grads, total_ref, mine, pair_buf, corner_x, corner_y, full_x, full_y, z_up, z_down, z_out,
            load_sem, pair_send, pair_recv, side_send, side_recv, z_send, z_recv, between):
    rows = total_ref.shape[0]
    half = rows // 2
    z, x, y, core = at.z, at.x, at.y, at.core
    low, high = pl.ds(0, half), pl.ds(half, rows - half)
    orders = ((3, 2, 1, 0), (3, 0, 2, 1), (0, 3, 1, 2), (0, 1, 2, 3))

    def turn(step):
        choice = jnp.int32(orders[3][step])
        for which in range(3):
            choice = jnp.where(z == which, jnp.int32(orders[which][step]), choice)
        return choice

    turns = [turn(step) for step in range(DEPTH)]

    def load(target, y_of):
        return pltpu.make_async_copy(
            grads.at[y_of * 2 + core, target], mine.at[y_of, target], load_sem.at[y_of, target]
        )

    def pair(target, y_of):
        return remote(
            grads.at[y_of * 2 + 1 - core, target], pair_buf.at[y_of, target],
            pair_send.at[y_of, target], pair_recv.at[y_of, target], at.partner,
        )

    def corner(kind, target):
        part = mine.at[1 - y, target, 1 - x]
        if kind == 0:
            return remote(part.at[low], corner_y.at[target], side_send.at[0, target], side_recv.at[0, target], at.y_side)
        return remote(part.at[high], corner_x.at[target], side_send.at[1, target], side_recv.at[1, target], at.x_side)

    def full(kind, target):
        if kind == 2:
            return remote(mine.at[y, target, 1 - x], full_x.at[target], side_send.at[2, target], side_recv.at[2, target], at.x_side)
        return remote(mine.at[1 - y, target, x], full_y.at[target], side_send.at[3, target], side_recv.at[3, target], at.y_side)

    def up(target):
        return remote(z_out.at[target], z_up.at[target], z_send.at[target], z_recv.at[0, target], at.above)

    def down(target):
        return remote(z_out.at[target], z_down.at[target], z_send.at[target], z_recv.at[1, target], at.below)

    wide = jnp.float32
    for target in turns:
        for y_of in (0, 1):
            pair(target, y_of).start()
            load(target, y_of).start()

    def first(target):
        for y_of in (0, 1):
            load(target, y_of).wait()
            pair(target, y_of).wait_recv()

        def add(which, carry):
            y_of, x_of = which // 2, which % 2
            mine[y_of, target, x_of] = (
                mine[y_of, target, x_of].astype(wide) + pair_buf[y_of, target, x_of].astype(wide)
            ).astype(mine.dtype)
            return carry

        lax.fori_loop(0, 4, add, 0)
        corner(0, target).start()
        corner(1, target).start()

    def second(target):
        corner(0, target).wait_recv()
        mine[y, target, 1 - x, low] = (
            mine[y, target, 1 - x, low].astype(wide) + corner_y[target].astype(wide)
        ).astype(mine.dtype)
        full(2, target).start()
        corner(1, target).wait_recv()
        mine[1 - y, target, x, high] = (
            mine[1 - y, target, x, high].astype(wide) + corner_x[target].astype(wide)
        ).astype(mine.dtype)
        full(3, target).start()

    def third(target, last):
        full(2, target).wait_recv()
        full(3, target).wait_recv()
        total_ref[...] = mine[y, target, x].astype(wide) + (
            full_x[target].astype(wide) + full_y[target].astype(wide)
        )

        def add_below():
            up(target).wait_recv()
            total_ref[...] += z_up[target].astype(wide)

        def add_above():
            down(target).wait_recv()
            total_ref[...] += z_down[target].astype(wide)

        pl.when((target >= z) & (z > 0))(add_below)
        pl.when((target <= z) & (z < DEPTH - 1))(add_above)
        if not last:
            z_out[target] = total_ref[...].astype(z_out.dtype)
            pl.when(target > z)(lambda: up(target).start())
            pl.when(target < z)(lambda: down(target).start())

    for step in range(DEPTH + 2):
        between(step)
        if step < DEPTH:
            first(turns[step])
        if 1 <= step <= DEPTH:
            second(turns[step - 1])
        if step >= 2:
            third(turns[step - 2], step - 2 == DEPTH - 1)
    for target in range(DEPTH):
        for y_of in (0, 1):
            pair(target, y_of).wait_send()
        for kind in (0, 1):
            corner(kind, target).wait_send()
        for kind in (2, 3):
            full(kind, target).wait_send()
        pl.when(target != z)(lambda: up(target).wait_send())


def collect_scratch(rows, columns, dtype):
    return [
        pltpu.VMEM((2, DEPTH, 2, rows, columns), dtype),
        pltpu.VMEM((2, DEPTH, 2, rows, columns), dtype),
        pltpu.VMEM((DEPTH, rows // 2, columns), dtype),
        pltpu.VMEM((DEPTH, rows // 2, columns), dtype),
        pltpu.VMEM((DEPTH, rows, columns), dtype),
        pltpu.VMEM((DEPTH, rows, columns), dtype),
        pltpu.VMEM((DEPTH, rows, columns), dtype),
        pltpu.VMEM((DEPTH, rows, columns), dtype),
        pltpu.VMEM((DEPTH, rows, columns), dtype),
        pltpu.SemaphoreType.DMA((2, DEPTH)),
        pltpu.SemaphoreType.DMA((2, DEPTH)),
        pltpu.SemaphoreType.DMA((2, DEPTH)),
        pltpu.SemaphoreType.DMA((4, DEPTH)),
        pltpu.SemaphoreType.DMA((4, DEPTH)),
        pltpu.SemaphoreType.DMA((DEPTH,)),
        pltpu.SemaphoreType.DMA((2, DEPTH)),
    ]


N_COLLECT = 16


def muon_kernel(grads, moment_ref, small_ref, grad_out, moment_out, next_all, small_out,
                own_next, small_parts, small_in, small_send, small_recv, *scratch):
    at = Place()
    at.greet(far=True)
    peers = (at.partner, at.x_side, at.y_side, at.z_near, at.z_far)

    def swap(stage):
        source = small_ref if stage == 0 else small_parts.at[stage - 1]
        return remote(source, small_in.at[stage], small_send.at[stage], small_recv.at[stage], peers[stage])

    def between(step):
        if 1 <= step <= 5:
            stage = step - 1
            swap(stage).wait_recv()
            held = small_ref[...] if stage == 0 else small_parts[stage - 1]
            held = held + small_in[stage]
            if stage < 4:
                small_parts[stage] = held
            else:
                small_out[...] = held
        if step < 5:
            swap(step).start()

    collect(at, grads, grad_out, *scratch[:N_COLLECT], between)
    for stage in range(5):
        swap(stage).wait_send()
    grad = grad_out[...]
    moment = muon_beta * moment_ref[...] + grad
    moment_out[...] = moment
    own_next[...] = (grad + muon_beta * moment).astype(own_next.dtype)
    spread(at, own_next, next_all, *scratch[N_COLLECT:])


def muon_exchange(grads, moment, small):
    rows, columns = moment.shape
    shape = jax.ShapeDtypeStruct((rows, columns), jnp.float32)
    vmem = pl.BlockSpec(memory_space=pltpu.VMEM)
    hbm = pl.BlockSpec(memory_space=pl.ANY)
    return pl.pallas_call(
        muon_kernel,
        out_shape=(
            shape,
            shape,
            jax.ShapeDtypeStruct((32, rows, columns), jnp.bfloat16),
            jax.ShapeDtypeStruct(small.shape, jnp.float32),
        ),
        in_specs=[hbm, vmem, vmem],
        out_specs=(vmem, vmem, hbm, vmem),
        scratch_shapes=[
            pltpu.VMEM((rows, columns), jnp.bfloat16),
            pltpu.VMEM((4,) + small.shape, jnp.float32),
            pltpu.VMEM((5,) + small.shape, jnp.float32),
            pltpu.SemaphoreType.DMA((5,)),
            pltpu.SemaphoreType.DMA((5,)),
        ]
        + collect_scratch(rows, columns, jnp.bfloat16)
        + SPREAD_SEMS,
        compiler_params=pltpu.CompilerParams(
            collective_id=1, has_side_effects=True, vmem_limit_bytes=40 * 1024 * 1024
        ),
        name="muon_exchange",
    )(grads.reshape(4, DEPTH, 2, rows, columns), moment, small)


def ns_kernel(next_all, products, rows_buf, map_buf, sem):
    mp_index, dp_index = lax.axis_index("mp"), lax.axis_index("dp")
    counts = (48, 16, 64, 64)

    def fetch(which):
        count = counts[which]
        copy = pltpu.make_async_copy(
            next_all.at[:, pl.ds(sum(counts[:which]), count)], rows_buf.at[:, pl.ds(0, count)], sem
        )
        copy.start()
        if count < 64:
            rows_buf[:, pl.ds(count, 64 - count)] = jnp.zeros((32, 64 - count, C), rows_buf.dtype)
        copy.wait()

    for which in range(4):
        pl.when(mp_index == which)(functools.partial(fetch, which))

    gram = None
    for part in range(4):
        block = rows_buf[8 * part : 8 * (part + 1)].reshape(512, C)
        term = dot_tn(block, block)
        gram = term if gram is None else gram + term
    eye = (
        lax.broadcasted_iota(jnp.int32, (C, C), 0) == lax.broadcasted_iota(jnp.int32, (C, C), 1)
    ).astype(wide)
    norm_value = jnp.sqrt(jnp.sum(jnp.sum(gram * eye, axis=1, keepdims=True), axis=0, keepdims=True)) + ns_eps
    gram = gram / (norm_value * norm_value)

    def dot_high(a, b):
        return jnp.dot(a, b, precision=lax.Precision.HIGH, preferred_element_type=wide)

    total = None
    for iteration in range(NS_ITERS):
        square = dot_high(gram, gram)
        poly = coef_a * eye + (coef_b * gram + coef_c * square)
        total = poly if total is None else dot_high(total, poly)
        if iteration + 1 < NS_ITERS:
            gram = dot_high(dot_high(gram, poly), poly)
    map_buf[...] = total / norm_value
    for group in range(4):
        rows = rows_buf[group * 8 + dp_index].astype(wide)
        products[group] = dot_high(rows, map_buf[...]).astype(products.dtype)


def newton_schulz_rows(next_all):
    return pl.pallas_call(
        ns_kernel,
        out_shape=jax.ShapeDtypeStruct((4, 64, C), low),
        in_specs=[pl.BlockSpec(memory_space=pl.ANY)],
        out_specs=pl.BlockSpec(memory_space=pltpu.VMEM),
        scratch_shapes=[
            pltpu.VMEM((32, 64, C), low),
            pltpu.VMEM((C, C), wide),
            pltpu.SemaphoreType.DMA,
        ],
        compiler_params=pltpu.CompilerParams(vmem_limit_bytes=40 * 1024 * 1024),
        name="newton_schulz",
    )(next_all)


def swap_kernel(products, swapped, send_sem, recv_sem):
    mp_index = lax.axis_index("mp")
    barrier = pltpu.get_barrier_semaphore()
    peers = [lax.rem(mp_index + shift, 4) for shift in (1, 2, 3)]
    for peer in peers:
        pl.semaphore_signal(
            barrier, inc=1, device_id={"dp": lax.axis_index("dp"), "mp": peer}, device_id_type=MESH
        )
    pl.semaphore_wait(barrier, 3)

    def send(which):
        return remote(
            products.at[peers[which]], swapped.at[mp_index], send_sem.at[which], recv_sem.at[which],
            {"dp": lax.axis_index("dp"), "mp": peers[which]},
        )

    for which in range(3):
        send(which).start()
    swapped[mp_index] = products[mp_index]
    for which in range(3):
        source = peers[2 - which]
        remote(
            products.at[source], swapped.at[source], send_sem.at[which], recv_sem.at[which],
            {"dp": lax.axis_index("dp"), "mp": source},
        ).wait_recv()
        send(which).wait_send()


def swap_rows(products):
    vmem = pl.BlockSpec(memory_space=pltpu.VMEM)
    return pl.pallas_call(
        swap_kernel,
        out_shape=jax.ShapeDtypeStruct(products.shape, products.dtype),
        in_specs=[vmem],
        out_specs=vmem,
        scratch_shapes=[pltpu.SemaphoreType.DMA((3,)), pltpu.SemaphoreType.DMA((3,))],
        compiler_params=pltpu.CompilerParams(collective_id=2, has_side_effects=True),
        name="swap_rows",
    )(products)


def split_low(values):
    high = lax.reduce_precision(values, exponent_bits=8, mantissa_bits=7)
    return high.astype(jnp.bfloat16), (values - high).astype(jnp.bfloat16)


def dot_three(left, right):
    left_high, left_rest = left
    right_high, right_rest = right
    wide = dict(preferred_element_type=jnp.float32)
    return (
        jnp.dot(left_rest, right_high, **wide)
        + jnp.dot(left_high, right_rest, **wide)
        + jnp.dot(left_high, right_high, **wide)
    )


def newton_schulz(gram):
    width = gram.shape[0]
    eye = jnp.eye(width, dtype=jnp.float32)
    norm_value = jnp.sqrt(jnp.sum(gram * eye)) + ns_eps
    gram = gram / (norm_value * norm_value)
    total = None
    for iteration in range(NS_ITERS):
        parts = split_low(gram)
        square = dot_three(parts, parts)
        poly = coef_a * eye + (coef_b * gram + coef_c * square)
        poly_parts = split_low(poly)
        total = poly if total is None else dot_three(split_low(total), poly_parts)
        if iteration + 1 < NS_ITERS:
            half = dot_three(parts, poly_parts)
            gram = dot_three(split_low(half), poly_parts)
    return total / norm_value


def adam_update(grad_sum, first_moment, second_moment):
    first_new = adam_one * first_moment + (1.0 - adam_one) * grad_sum
    second_new = adam_two * second_moment + (1.0 - adam_two) * grad_sum * grad_sum
    first_hat = first_new / (1.0 - adam_one**adam_step)
    second_hat = second_new / (1.0 - adam_two**adam_step)
    return (-adam_rate * first_hat / (jnp.sqrt(second_hat) + adam_eps), first_new, second_new)


def exchange_plain(own_low, own_moments, rows):
    everyone = ("mp", "dp")
    starts = [sum(rows[:which]) for which in range(4)]

    def cut(stacked):
        return [stacked[:, start : start + count] for start, count in zip(starts, rows)]

    gathered = [
        part.reshape(-1, C) for part in cut(lax.all_gather(own_low, everyone, axis=0, tiled=False))
    ]

    def finish(big_local):
        mp_size, dp_size = lax.axis_size("mp"), lax.axis_size("dp")
        mp_index, dp_index = lax.axis_index("mp"), lax.axis_index("dp")
        devices = mp_size * dp_size
        stacked_grads = jnp.concatenate(
            [grad.reshape(devices, count, C) for grad, count in zip(big_local, rows)], axis=1
        )
        own_grads = lax.psum_scatter(
            stacked_grads.reshape(devices * sum(rows), C), everyone, scatter_dimension=0, tiled=True
        ).astype(wide)
        own_buffers = muon_beta * own_moments + own_grads
        own_nesterov = own_grads + muon_beta * own_buffers
        iterate_all = lax.all_gather(own_nesterov.astype(low), everyone, axis=0, tiled=False)
        grams = jnp.stack([dot_tn(part.reshape(-1, C), part.reshape(-1, C)) for part in cut(iterate_all)])
        ortho_map = newton_schulz(lax.dynamic_index_in_dim(grams, mp_index, 0, keepdims=False))
        most = max(rows)
        picked = lax.dynamic_slice(
            iterate_all.reshape(mp_size, dp_size, sum(rows), C),
            (
                jnp.int32(0),
                dp_index.astype(jnp.int32),
                jnp.array(starts, jnp.int32)[mp_index],
                jnp.int32(0),
            ),
            (mp_size, 1, most, C),
        ).reshape(mp_size * most, C)
        map_parts = split_low(ortho_map)
        products = dot(picked, map_parts[0]) + dot(picked, map_parts[1])
        swapped = lax.all_to_all(products.reshape(mp_size, most, C), "mp", 0, 0, tiled=False)
        return own_grads, own_buffers, swapped

    return gathered, finish


def shards(
    images,
    cotangent,
    qkv_weight,
    proj_weight,
    expand_weight,
    contract_weight,
    qkv_moment,
    proj_moment,
    expand_moment,
    contract_moment,
    vectors,
    qv_bias,
    expand_bias,
    rel_table,
    vectors_first,
    vectors_second,
    qv_first,
    qv_second,
    expand_bias_first,
    expand_bias_second,
    table_first,
    table_second,
    region_ids,
    pos_index,
    image_counts,
):
    everyone = ("mp", "dp")
    mp_size, dp_size = lax.axis_size("mp"), lax.axis_size("dp")
    mp_index = lax.axis_index("mp")
    linked = mp_size == 4 and dp_size == 8
    per_device = IMG_DEV // mp_size
    first_image = (mp_index * per_device).astype(jnp.int32)
    place = jnp.stack([first_image, image_counts[0]])
    own_images = lax.dynamic_slice_in_dim(images, first_image, per_device, 0)
    own_cotangent = lax.dynamic_slice_in_dim(cotangent, first_image, per_device, 0)
    weights_all = (qkv_weight, proj_weight, expand_weight, contract_weight)
    rows = [weight.shape[0] for weight in weights_all]
    starts = [sum(rows[:which]) for which in range(4)]
    own_low = jnp.concatenate([weight.astype(low) for weight in weights_all], axis=0)
    own_moments = jnp.concatenate(
        (qkv_moment, proj_moment, expand_moment, contract_moment), axis=0
    )
    if linked:
        misc = jnp.concatenate(
            [
                expand_bias[None],
                jnp.pad(qv_bias.reshape(1, -1), ((0, 0), (0, C - qv_bias.size))),
                jnp.pad(rel_table.T, ((0, 2), (0, C - TABLE))),
            ],
            axis=0,
        )
        gathered, misc_all = gather_all(own_low, misc)
        expand_full = misc_all[:, 0].reshape(4, C)
        qv_full = misc_all[:, 1, : qv_bias.size].reshape(4, 2, -1).transpose(1, 0, 2).reshape(2, C)
        table_full = misc_all[:, 2:6, :TABLE].reshape(HEADS, TABLE)
    else:
        gathered, finish_plain = exchange_plain(own_low, own_moments, rows)
        qv_full = lax.all_gather(qv_bias, "mp", axis=1, tiled=True)
        expand_full = lax.all_gather(expand_bias, "mp", axis=0, tiled=True).reshape(4, C)
        table_full = lax.all_gather(rel_table.T, "mp", axis=0, tiled=True)
    onehot = (
        jnp.arange(TABLE, dtype=jnp.int32)[:, None] == pos_index.reshape(1, SPAN * SPAN)
    ).astype(wide)
    pos_bias = jnp.dot(table_full, onehot, precision=highest).reshape(HEADS, SPAN, SPAN)
    window_regions = to_windows(region_ids.reshape(1, TOK, 1))[:, :, 0]
    window_mask = jnp.where(
        window_regions[:, :, None] != window_regions[:, None, :], mask_value, 0.0
    ).astype(wide)
    bias = pair_bias(pos_bias, window_mask)
    block_low, input_low, big_local, small_rows, table_pairs = run_layer(
        linked, per_device, place, own_images, own_cotangent, vectors, qv_full, expand_full, bias, gathered
    )
    if linked:
        block_out, input_grad = block_low, input_low
    else:
        block_out = lax.all_gather(block_low, "mp", axis=0, tiled=True)
        input_grad = lax.all_gather(input_low, "mp", axis=0, tiled=True)
    pairs = table_pairs.reshape(HEADS, PAIR, PAIR)
    bias_heads = pairs[:, :SPAN, :SPAN] + pairs[:, SPAN : 2 * SPAN, SPAN : 2 * SPAN]
    table_local = lax.dot_general(
        bias_heads.reshape(HEADS, SPAN * SPAN),
        onehot,
        (((1,), (1,)), ((), ())),
        precision=highest,
        preferred_element_type=wide,
    )
    if linked:
        small_own = jnp.concatenate(
            [small_rows, jnp.pad(table_local, ((0, 0), (0, C - TABLE)))], axis=0
        )
        own_grads, own_buffers, next_all, small_all = muon_exchange(big_local, own_moments, small_own)
        small_full, table_all = small_all[:HEADS], small_all[HEADS:, :TABLE]
        swapped = swap_rows(newton_schulz_rows(next_all))
    else:
        small_full, table_all = lax.psum((small_rows, table_local), everyone)
        own_grads, own_buffers, swapped = finish_plain(big_local)
    ortho = [swapped[which, :count].astype(wide) for which, count in enumerate(rows)]
    shares = [own_grads[start : start + count] for start, count in zip(starts, rows)]
    buffers = [own_buffers[start : start + count] for start, count in zip(starts, rows)]

    def own_columns(full, width):
        return lax.dynamic_slice_in_dim(full, mp_index * width, width, full.ndim - 1)

    small_sums = (
        small_full[:6],
        own_columns(small_full[6:8], qv_bias.shape[1]),
        own_columns(small_full[8:12].reshape(FF), expand_bias.shape[0]),
        lax.dynamic_slice_in_dim(table_all, mp_index * rel_table.shape[1], rel_table.shape[1], 0).T,
    )
    factors = (math.sqrt(3.0), 1.0, math.sqrt(max(1.0, FF / C)), 1.0)
    new_steps = tuple(
        (
            -muon_rate * (muon_decay * weight + factor * ortho_part)
            for weight, ortho_part, factor in zip(weights_all, ortho, factors)
        )
    )
    vectors_step, vectors_first_new, vectors_second_new = adam_update(
        small_sums[0], vectors_first, vectors_second
    )
    qv_step, qv_first_new, qv_second_new = adam_update(small_sums[1], qv_first, qv_second)
    expand_bias_step, expand_bias_first_new, expand_bias_second_new = adam_update(
        small_sums[2], expand_bias_first, expand_bias_second
    )
    table_step, table_first_new, table_second_new = adam_update(
        small_sums[3], table_first, table_second
    )
    return (
        block_out,
        input_grad,
        shares[0],
        shares[1],
        shares[2],
        shares[3],
        small_sums[0],
        small_sums[1],
        small_sums[2],
        small_sums[3],
        new_steps[0],
        new_steps[1],
        new_steps[2],
        new_steps[3],
        buffers[0],
        buffers[1],
        buffers[2],
        buffers[3],
        vectors_step,
        qv_step,
        expand_bias_step,
        table_step,
        vectors_first_new,
        vectors_second_new,
        qv_first_new,
        qv_second_new,
        expand_bias_first_new,
        expand_bias_second_new,
        table_first_new,
        table_second_new,
    )


def solution(mesh):
    return jax.shard_map(
        shards,
        mesh=mesh,
        in_specs=(
            P("dp", None, None),
            P("dp", None, None),
            P(("mp", "dp"), None),
            P(("mp", "dp"), None),
            P(("mp", "dp"), None),
            P(("mp", "dp"), None),
            P(("mp", "dp"), None),
            P(("mp", "dp"), None),
            P(("mp", "dp"), None),
            P(("mp", "dp"), None),
            P(),
            P(None, "mp"),
            P("mp"),
            P(None, "mp"),
            P(),
            P(),
            P(None, "mp"),
            P(None, "mp"),
            P("mp"),
            P("mp"),
            P(None, "mp"),
            P(None, "mp"),
            P(),
            P(),
            P("dp"),
        ),
        out_specs=(
            P("dp", None, None),
            P("dp", None, None),
            P(("mp", "dp"), None),
            P(("mp", "dp"), None),
            P(("mp", "dp"), None),
            P(("mp", "dp"), None),
            P(),
            P(None, "mp"),
            P("mp"),
            P(None, "mp"),
            P(("mp", "dp"), None),
            P(("mp", "dp"), None),
            P(("mp", "dp"), None),
            P(("mp", "dp"), None),
            P(("mp", "dp"), None),
            P(("mp", "dp"), None),
            P(("mp", "dp"), None),
            P(("mp", "dp"), None),
            P(),
            P(None, "mp"),
            P("mp"),
            P(None, "mp"),
            P(),
            P(),
            P(None, "mp"),
            P(None, "mp"),
            P("mp"),
            P("mp"),
            P(None, "mp"),
            P(None, "mp"),
        ),
        check_vma=False,
    )
```

```python
import functools
import math

import jax
import jax.numpy as jnp
import numpy as np
from jax import lax
from jax.experimental import pallas as pl
from jax.experimental.pallas import tpu as pltpu
from jax.sharding import PartitionSpec as P

C = 512
HEADS = 16
HD = 32
FF = 2048
WIN = 7
SIDE = 14
SHIFT = 3
SPAN = WIN * WIN
TOK = SIDE * SIDE
NS_ITERS = 5
IMG_DEV = 16
TABLE = 169
PAIR = 112
ROWS = 2 * PAIR
GROUP = 4

norm_eps = 1e-05
ns_eps = 1e-07
coef_a = 3.4445
coef_b = -4.775
coef_c = 2.0315
muon_rate = 0.3
muon_decay = 0.1
muon_beta = 0.95
adam_rate = 0.1
adam_one = 0.9
adam_two = 0.999
adam_eps = 1e-08
adam_step = 4
mask_value = -100.0
away = -1e30
wide = jnp.float32
low = jnp.bfloat16
highest = lax.Precision.HIGHEST


def to_windows(field_values):
    image_total = field_values.shape[0]
    channels = field_values.shape[-1]
    blocks = SIDE // WIN
    grid_values = field_values.reshape(image_total, SIDE, SIDE, channels)
    grid_values = jnp.roll(grid_values, (-SHIFT, -SHIFT), axis=(1, 2))
    grid_values = grid_values.reshape(image_total, blocks, WIN, blocks, WIN, channels)
    grid_values = grid_values.transpose(0, 1, 3, 2, 4, 5)
    return grid_values.reshape(image_total * blocks * blocks, WIN * WIN, channels)


def window_order():
    order = np.full((ROWS,), -1, np.int64)
    for window in range(4):
        top, left = window // 2, window % 2
        for token in range(SPAN):
            row = (top * WIN + token // WIN + SHIFT) % SIDE
            column = (left * WIN + token % WIN + SHIFT) % SIDE
            order[(window // 2) * PAIR + (window % 2) * SPAN + token] = row * SIDE + column
    return order


def dot(a, b):
    return jnp.dot(a, b, preferred_element_type=wide)


def dot_nt(a, b):
    return lax.dot_general(a, b, (((1,), (1,)), ((), ())), preferred_element_type=wide)


def dot_tn(a, b):
    return lax.dot_general(a, b, (((0,), (0,)), ((), ())), preferred_element_type=wide)


def mean_of(values):
    return jnp.sum(values, axis=-1, keepdims=True) * (1.0 / C)


def normalize(values):
    centered = values - mean_of(values)
    inv_scale = lax.rsqrt(mean_of(centered * centered) + norm_eps)
    return centered * inv_scale, inv_scale


def normalize_back(grad_norm, normed, inv_scale, gain):
    scaled = grad_norm * gain
    return inv_scale * (scaled - mean_of(scaled) - normed * mean_of(scaled * normed))


def column_sum(values):
    return jnp.sum(values, axis=0, keepdims=True)


def head_masks():
    lane = lax.broadcasted_iota(jnp.int32, (1, 128), 1) // HD
    return [(lane == head).astype(wide).astype(low) for head in range(GROUP)]


def stack_heads(block, masks):
    return jnp.concatenate([block * mask for mask in masks], axis=0)


def pick_heads(stacked):
    lane = lax.broadcasted_iota(jnp.int32, (PAIR, 128), 1)
    parts = [stacked[PAIR * head : PAIR * (head + 1)] for head in range(GROUP)]
    return jnp.where(
        lane < 2 * HD,
        jnp.where(lane < HD, parts[0], parts[1]),
        jnp.where(lane < 3 * HD, parts[2], parts[3]),
    )


def layer_kernel(
    packed, batch, place, images, cotangent, order, order_back, vectors, qv_bias, expand_bias, bias,
    qkv_hbm, proj_hbm, expand_hbm, contract_hbm,
    block_out, input_grad, *rest,
):
    n_grads = 1 if packed else 4
    grad_outs = rest[:n_grads]
    (small, table_sum, qkv_nat, qkv_w, proj_w, expand_w, contract_w,
     qkv_acc, proj_acc, expand_acc, contract_acc,
     qkv_s, att_s, back_s, probs_s, normed_s, first_s, middle_s, normed2_s, second_s,
     out_low_s, mlp_s, second_grad_s, sems) = rest[n_grads : n_grads + 24]
    step = pl.program_id(0)
    steps = pl.num_programs(0)
    masks = head_masks()
    if packed:
        staged, keep_sem, act_send, act_recv = rest[n_grads + 24 :]
        at = Place()
        per_device = staged.shape[0]
        over = (1 - at.y) * 2 + at.core
        across = (1 - at.y) * 2 + 1 - at.core
        beside = at.y * 2 + 1 - at.core

        def slot(mp_index, image):
            return block_out.at[mp_index * per_device + image]

        def keep_copy(image):
            return pltpu.make_async_copy(staged.at[image], slot(at.mp_index, image), keep_sem.at[image])

        def own_copy(which, image):
            device = (at.partner, at.y_side)[which]
            return remote(
                staged.at[image], slot(at.mp_index, image),
                act_send.at[which, image], act_recv.at[which, image], device,
            )

        def own_arrival(which, image):
            source, device = ((beside, at.partner), (over, at.y_side))[which]
            return remote(
                staged.at[image], slot(source, image),
                act_send.at[which, image], act_recv.at[which, image], device,
            )

        def relay(image):
            return remote(
                slot(over, image), slot(over, image), act_send.at[2, image], act_recv.at[2, image], at.partner
            )

        def relay_arrival(image):
            return remote(
                slot(across, image), slot(across, image), act_send.at[2, image], act_recv.at[2, image], at.partner
            )

        def pass_on(of_step):
            for slice_ in range(batch):
                image = of_step * batch + slice_
                own_arrival(1, image).wait_recv()
                relay(image).start()

        def greet():
            barrier = pltpu.get_barrier_semaphore()
            for device in (at.partner, at.y_side):
                pl.semaphore_signal(barrier, inc=1, device_id=device, device_id_type=MESH)
            pl.semaphore_wait(barrier, 2)

        pl.when(step == 0)(greet)

    def put_block(slice_, value):
        if packed:
            image = step * batch + slice_
            staged[image] = value
            own_copy(1, image).start()
            own_copy(0, image).start()
            keep_copy(image).start()
        else:
            block_out[slice_] = value

    def put_grad(slice_, value):
        input_grad[slice_] = value

    row = lax.broadcasted_iota(jnp.int32, (batch * ROWS, 1), 0) // ROWS
    live_scale = jnp.zeros((batch * ROWS, 1), wide)
    for slice_ in range(batch):
        is_live = (place[1] > place[0] + step * batch + slice_).astype(wide)
        live_scale = jnp.where(row == slice_, is_live, live_scale)

    def fetch(which):
        if packed:
            counts = (48, 16, 64, 64)
            source = qkv_hbm.at[:, pl.ds(sum(counts[:which]), counts[which])]
            target = (qkv_nat, proj_w, expand_w, contract_w)[which]
        else:
            source = (qkv_hbm, proj_hbm, expand_hbm, contract_hbm)[which]
            target = (qkv_nat, proj_w, expand_w, contract_w)[which]
        return pltpu.make_async_copy(source, target, sems.at[which])

    def rows_of(ref, count):
        return ref[...].reshape(count, C)

    def begin():
        for which in range(4):
            fetch(which).start()
        for ref in (qkv_acc, proj_acc, expand_acc, contract_acc, small, table_sum):
            ref[...] = jnp.zeros_like(ref)
        for which in range(4):
            fetch(which).wait()
        natural = rows_of(qkv_nat, 3 * C).reshape(HEADS, 3, HD, C)
        for kind in range(3):
            qkv_w[kind] = natural[:, kind].reshape(C, C)

    pl.when(step == 0)(begin)

    tokens = jnp.concatenate([dot(order[...], images[slice_]) for slice_ in range(batch)], axis=0)
    normed, inv_one = normalize(tokens)
    normed_s[...] = normed
    first_in = (normed * vectors[0:1] + vectors[1:2]).astype(low)
    first_s[...] = first_in
    for kind in range(3):
        projected = dot_nt(first_in, qkv_w[kind])
        if kind != 1:
            projected = projected + qv_bias[kind // 2 : kind // 2 + 1]
        projected = projected.astype(low)
        for group in range(4):
            qkv_s[kind * 4 + group] = projected[:, 128 * group : 128 * (group + 1)]
    score_scale = 1.0 / math.sqrt(HD)

    def attend(which, carry):
        pair, group = which // 4, which % 4
        pair_scores = bias[pair, group]
        for slice_ in range(batch):
            rows = pl.ds(pl.multiple_of(slice_ * ROWS + pair * PAIR, 16), PAIR)
            queries = stack_heads(qkv_s[group, rows], masks)
            scores = dot_nt(queries, qkv_s[4 + group, rows]) * score_scale + pair_scores
            top = jnp.max(scores, axis=-1, keepdims=True)
            exponent = jnp.exp(scores - top)
            attention = exponent / jnp.sum(exponent, axis=-1, keepdims=True)
            probs_s[slice_, which] = attention
            att_s[group, rows] = pick_heads(dot(attention.astype(low), qkv_s[8 + group, rows])).astype(low)
        return carry

    lax.fori_loop(0, 8, attend, 0)
    attended = jnp.concatenate([att_s[group] for group in range(4)], axis=1)
    middle = tokens + (dot(attended, rows_of(proj_w, C)) + vectors[4:5])
    middle_s[...] = middle
    normed_two, inv_two = normalize(middle)
    normed2_s[...] = normed_two
    second_in = (normed_two * vectors[2:3] + vectors[3:4]).astype(low)
    second_s[...] = second_in

    grad_tokens = jnp.concatenate([dot(order[...], cotangent[slice_]) for slice_ in range(batch)], axis=0)
    out_low = (grad_tokens * live_scale).astype(low)
    out_low_s[...] = out_low
    mlp_s[...] = jnp.zeros_like(mlp_s)
    second_grad_s[...] = jnp.zeros_like(second_grad_s)
    chunk = 512
    owners = expand_w.shape[0] // (FF // chunk)

    def feed(which, carry):
        units = pl.ds(pl.multiple_of(which * owners, owners), owners)
        expand_part = expand_w[units].reshape(chunk, C)
        contract_part = contract_w[units].reshape(chunk, C)
        second = second_s[...]
        grad_rows = out_low_s[...]
        hidden = dot_nt(second, expand_part) + expand_bias[which]
        cumulative = 0.5 * (1.0 + lax.erf(hidden * (1.0 / math.sqrt(2.0))))
        acted = (hidden * cumulative).astype(low)
        slope = cumulative + hidden * jnp.exp(-0.5 * hidden * hidden) * (1.0 / math.sqrt(2.0 * math.pi))
        mlp_s[...] += dot(acted, contract_part)
        hidden_grad32 = dot_nt(grad_rows, contract_part) * slope
        hidden_grad = hidden_grad32.astype(low)
        small[pl.ds(8 + which, 1)] += column_sum(hidden_grad.astype(wide))
        second_grad_s[...] += dot(hidden_grad, expand_part)
        units_wide = pl.ds(pl.multiple_of(which * chunk, chunk), chunk)
        contract_acc[units_wide] += dot_tn(acted, grad_rows)
        expand_acc[units_wide] += dot_tn(hidden_grad, second)
        return carry

    lax.fori_loop(0, FF // chunk, feed, 0)
    result = middle_s[...] + (mlp_s[...] + vectors[5:6])
    result = jnp.where(live_scale > 0.0, result, 0.0).astype(low)
    if packed:
        pl.when(step > 0)(lambda: pass_on(step - 1))
    for slice_ in range(batch):
        put_block(slice_, dot(order_back[...], result[ROWS * slice_ : ROWS * (slice_ + 1)]).astype(low))

    grad_out = out_low_s[...].astype(wide)
    second_grad = second_grad_s[...]
    normed_two = normed2_s[...]
    small[5:6] += column_sum(grad_out)
    small[3:4] += column_sum(second_grad)
    small[2:3] += column_sum(second_grad * normed_two)
    middle_grad = grad_out + normalize_back(second_grad, normed_two, inv_two, vectors[2:3])
    small[4:5] += column_sum(middle_grad)
    middle_s[...] = middle_grad
    attn_low = middle_grad.astype(low)
    attended = jnp.concatenate([att_s[group] for group in range(4)], axis=1)
    proj_acc[...] += dot_tn(attended, attn_low)
    attended_grad = dot_nt(attn_low, rows_of(proj_w, C)).astype(low)
    for group in range(4):
        att_s[group] = attended_grad[:, 128 * group : 128 * (group + 1)]

    def attend_back(which, carry):
        pair, group = which // 4, which % 4
        bias_grad = None
        for slice_ in range(batch):
            rows = pl.ds(pl.multiple_of(slice_ * ROWS + pair * PAIR, 16), PAIR)
            attention = probs_s[slice_, which]
            keys, values = qkv_s[4 + group, rows], qkv_s[8 + group, rows]
            grads = stack_heads(att_s[group, rows], masks)
            queries = stack_heads(qkv_s[group, rows], masks)
            probs_grad = dot_nt(grads, values)
            row_term = jnp.sum(attention * probs_grad, axis=-1, keepdims=True)
            score_grad = (attention * (probs_grad - row_term)).astype(low)
            wide_grad = score_grad.astype(wide)
            bias_grad = wide_grad if bias_grad is None else bias_grad + wide_grad
            back_s[group, rows] = (pick_heads(dot(score_grad, keys)) * score_scale).astype(low)
            back_s[4 + group, rows] = (dot_tn(score_grad, queries) * score_scale).astype(low)
            back_s[8 + group, rows] = dot_tn(attention.astype(low), grads).astype(low)
        table_sum[group] += bias_grad
        return carry

    lax.fori_loop(0, 8, attend_back, 0)
    first_in = first_s[...]
    first_grad = None
    for kind in range(3):
        back = jnp.concatenate([back_s[kind * 4 + group] for group in range(4)], axis=1)
        if kind != 1:
            row = 6 + kind // 2
            small[row : row + 1] += column_sum(back.astype(wide))
        qkv_acc[kind] += dot_tn(back, first_in)
        part = dot(back, qkv_w[kind])
        first_grad = part if first_grad is None else first_grad + part
    normed = normed_s[...]
    small[1:2] += column_sum(first_grad)
    small[0:1] += column_sum(first_grad * normed)
    token_grad = middle_s[...] + normalize_back(first_grad, normed, inv_one, vectors[0:1])
    token_low = token_grad.astype(low)
    for slice_ in range(batch):
        put_grad(slice_, dot(order_back[...], token_low[ROWS * slice_ : ROWS * (slice_ + 1)]).astype(low))

    def finish():
        if packed:
            pass_on(steps - 1)
        for kind in range(3):
            part = qkv_acc[kind].astype(low).reshape(HEADS, HD, C)
            if packed:
                out = grad_outs[0]
                for piece in range(2):
                    block = kind * 2 + piece
                    out[:, block // 3, pl.ds(16 * (block % 3), 16)] = part[:, 16 * piece : 16 * (piece + 1)]
            else:
                grad_outs[0][:, kind] = part
        if packed:
            out = grad_outs[0]
            out[:, :, pl.ds(48, 16)] = proj_acc[...].astype(low).reshape(16, 2, 16, C)
            out[:, :, pl.ds(64, 64)] = expand_acc[...].astype(low).reshape(16, 2, 64, C)
            out[:, :, pl.ds(128, 64)] = contract_acc[...].astype(low).reshape(16, 2, 64, C)
        else:
            grad_outs[1][...] = proj_acc[...].astype(low)
            grad_outs[2][...] = expand_acc[...].astype(low)
            grad_outs[3][...] = contract_acc[...].astype(low)
        if packed:

            def settle(image, carry):
                own_arrival(0, image).wait_recv()
                relay_arrival(image).wait_recv()
                own_copy(0, image).wait_send()
                own_copy(1, image).wait_send()
                relay(image).wait_send()
                keep_copy(image).wait()
                return carry

            lax.fori_loop(0, per_device, settle, 0)

    pl.when(step == steps - 1)(finish)


def run_layer(packed, per_device, place, images, cotangent, vectors, qv_bias, expand_bias, bias, weights):
    order_np = window_order()
    onehot = (order_np[:, None] == np.arange(TOK)[None, :]).astype(np.float32)
    order = jnp.asarray(onehot, low)
    order_back = jnp.asarray(onehot.T, low)
    any_spec = pl.BlockSpec(memory_space=pl.ANY)

    def whole(shape):
        return pl.BlockSpec(shape, lambda i, s: (0,) * len(shape), pipeline_mode=pl.Buffered(1))

    batch = 2 if per_device % 2 == 0 else 1
    span = batch * ROWS
    image_spec = pl.BlockSpec((batch, TOK, C), lambda i, s: (i, 0, 0))
    out_spec = any_spec if packed else image_spec
    images_out = IMG_DEV if packed else per_device
    exchange = [
        pltpu.VMEM((per_device, TOK, C), low),
        pltpu.SemaphoreType.DMA((per_device,)),
        pltpu.SemaphoreType.DMA((3, per_device)),
        pltpu.SemaphoreType.DMA((3, per_device)),
    ]
    limit = 60 * 1024 * 1024
    if packed:
        params = pltpu.CompilerParams(collective_id=3, has_side_effects=True, vmem_limit_bytes=limit)
    else:
        params = pltpu.CompilerParams(vmem_limit_bytes=limit)
    if packed:
        weights = (weights,) * 4
        grad_shapes = [(16, 2, 192, C)]
        weight_shapes = [(32, 48, C), (32, 16, C), (32, 64, C), (32, 64, C)]
    else:
        weights = (weights[0], weights[1], weights[2].reshape(FF // 64, 64, C), weights[3].reshape(FF // 64, 64, C))
        grad_shapes = [(HEADS, 3, HD, C), (C, C), (FF, C), (FF, C)]
        weight_shapes = [w.shape for w in weights]
    outs = pl.pallas_call(
        functools.partial(layer_kernel, packed, batch),
        out_shape=[
            jax.ShapeDtypeStruct((images_out, TOK, C), low),
            jax.ShapeDtypeStruct((per_device, TOK, C), low),
            *[jax.ShapeDtypeStruct(shape, low) for shape in grad_shapes],
            jax.ShapeDtypeStruct((16, C), wide),
            jax.ShapeDtypeStruct((4, GROUP * PAIR, PAIR), wide),
        ],
        grid_spec=pltpu.PrefetchScalarGridSpec(
            num_scalar_prefetch=1,
            grid=(per_device // batch,),
            in_specs=[
                image_spec, image_spec, whole((ROWS, TOK)), whole((TOK, ROWS)), whole((6, C)), whole((2, C)),
                whole((4, 1, C)), whole((2, 4, GROUP * PAIR, PAIR)), any_spec, any_spec, any_spec, any_spec,
            ],
            out_specs=[out_spec, image_spec]
            + [whole(shape) for shape in grad_shapes]
            + [whole((16, C)), whole((4, GROUP * PAIR, PAIR))],
            scratch_shapes=[pltpu.VMEM(shape, low) for shape in weight_shapes[:1]]
            + [pltpu.VMEM((3, C, C), low)]
            + [pltpu.VMEM(shape, low) for shape in weight_shapes[1:]]
            + [
                pltpu.VMEM((3, C, C), wide),
                pltpu.VMEM((C, C), wide),
                pltpu.VMEM((FF, C), wide),
                pltpu.VMEM((FF, C), wide),
                pltpu.VMEM((12, span, 128), low),
                pltpu.VMEM((4, span, 128), low),
                pltpu.VMEM((12, span, 128), low),
                pltpu.VMEM((batch, 8, GROUP * PAIR, PAIR), wide),
                pltpu.VMEM((span, C), wide),
                pltpu.VMEM((span, C), low),
                pltpu.VMEM((span, C), wide),
                pltpu.VMEM((span, C), wide),
                pltpu.VMEM((span, C), low),
                pltpu.VMEM((span, C), low),
                pltpu.VMEM((span, C), wide),
                pltpu.VMEM((span, C), wide),
                pltpu.SemaphoreType.DMA((4,)),
            ]
            + (exchange if packed else []),
        ),
        compiler_params=params,
        name="window_layer",
    )(place, images, cotangent, order, order_back, vectors, qv_bias, expand_bias.reshape(4, 1, C), bias, *weights)
    grads = outs[2 : 2 + len(grad_shapes)]
    grads = grads[0].reshape(32, 192, C) if packed else [g.reshape(-1, C) for g in grads]
    return outs[0], outs[1], grads, outs[-2], outs[-1]


def pair_bias(pos_bias, window_mask):
    heads = pos_bias.shape[0]
    scores = pos_bias[None] + window_mask[:, None]
    scores = scores.reshape(2, 2, heads, SPAN, SPAN)
    first = jnp.pad(scores[:, 0], ((0, 0), (0, 0), (0, 0), (0, PAIR - SPAN)), constant_values=away)
    second = jnp.pad(scores[:, 1], ((0, 0), (0, 0), (0, 0), (SPAN, PAIR - 2 * SPAN)), constant_values=away)
    rest = jnp.broadcast_to(
        jnp.where(jnp.arange(PAIR) < SPAN, 0.0, away).astype(wide), (2, heads, PAIR - 2 * SPAN, PAIR)
    )
    return jnp.concatenate([first, second, rest], axis=2).reshape(2, heads // GROUP, GROUP * PAIR, PAIR)


MESH = pl.DeviceIdType.MESH
DEPTH = 4


class Place:
    def __init__(self):
        dp_index, mp_index = lax.axis_index("dp"), lax.axis_index("mp")
        self.z, self.x = dp_index // 2, dp_index % 2
        self.y, self.core = mp_index // 2, mp_index % 2
        self.dp_index, self.mp_index = dp_index, mp_index
        self.x_side = self.device(self.z, 1 - self.x, self.y, self.core)
        self.y_side = self.device(self.z, self.x, 1 - self.y, self.core)
        self.partner = self.device(self.z, self.x, self.y, 1 - self.core)
        self.above = self.device(self.z + 1, self.x, self.y, self.core)
        self.below = self.device(self.z - 1, self.x, self.y, self.core)
        self.z_near = self.device(self.z + 1 - 2 * lax.rem(self.z, 2), self.x, self.y, self.core)
        self.z_far = self.device(lax.rem(self.z + 2, DEPTH), self.x, self.y, self.core)

    @staticmethod
    def device(z, x, y, core):
        return {"dp": z * 2 + x, "mp": y * 2 + core}

    @staticmethod
    def owner(z, x, y, core):
        return (y * 2 + core) * 8 + z * 2 + x

    def greet(self, far=False):
        barrier = pltpu.get_barrier_semaphore()

        def signal(device):
            pl.semaphore_signal(barrier, inc=1, device_id=device, device_id_type=MESH)

        signal(self.x_side)
        signal(self.y_side)
        signal(self.partner)
        pl.when(self.z > 0)(lambda: signal(self.below))
        pl.when(self.z < DEPTH - 1)(lambda: signal(self.above))
        ends = (self.z == 0).astype(jnp.int32) + (self.z == DEPTH - 1).astype(jnp.int32)
        if far:
            signal(self.z_far)
        pl.semaphore_wait(barrier, (6 if far else 5) - ends)


def remote(src, dst, send_sem, recv_sem, device):
    return pltpu.make_async_remote_copy(
        src_ref=src,
        dst_ref=dst,
        send_sem=send_sem,
        recv_sem=recv_sem,
        device_id=device,
        device_id_type=MESH,
    )


def spread(at, own_ref, out_ref, own_sem, z_send, z_recv, side_send, side_recv, pair_send, pair_recv):
    rows = own_ref.shape[0]
    half = rows // 2
    z, x, y, core = at.z, at.x, at.y, at.core
    low, high = pl.ds(0, half), pl.ds(half, rows - half)

    def slot(source_z, other_x, other_y):
        return out_ref.at[
            at.owner(source_z, 1 - x if other_x else x, 1 - y if other_y else y, core)
        ]

    def up(source_z, src=None):
        dst = slot(source_z, False, False)
        return remote(dst if src is None else src, dst, z_send.at[0, source_z], z_recv.at[0, source_z], at.above)

    def down(source_z, src=None):
        dst = slot(source_z, False, False)
        return remote(dst if src is None else src, dst, z_send.at[1, source_z], z_recv.at[1, source_z], at.below)

    def side(kind, source_z, src=None):
        if kind == 0 or kind == 1:
            dst = slot(source_z, False, False)
        elif kind == 2:
            dst = slot(source_z, True, False).at[low]
        else:
            dst = slot(source_z, False, True).at[high]
        device = at.x_side if kind in (0, 3) else at.y_side
        return remote(
            dst if src is None else src, dst, side_send.at[kind, source_z], side_recv.at[kind, source_z], device
        )

    def side_arrival(kind, source_z):
        if kind == 0:
            dst = slot(source_z, True, False)
        elif kind == 1:
            dst = slot(source_z, False, True)
        elif kind == 2:
            dst = slot(source_z, True, True).at[low]
        else:
            dst = slot(source_z, True, True).at[high]
        device = at.x_side if kind in (0, 3) else at.y_side
        return remote(dst, dst, side_send.at[kind, source_z], side_recv.at[kind, source_z], device)

    def pair_region(kind, source_z, of_core):
        other_x, other_y = ((False, False), (True, False), (False, True), (True, True), (True, True))[kind]
        ref = out_ref.at[at.owner(source_z, 1 - x if other_x else x, 1 - y if other_y else y, of_core)]
        if kind == 3:
            ref = ref.at[low]
        elif kind == 4:
            ref = ref.at[high]
        return ref

    def pair(kind, source_z, src=None):
        dst = pair_region(kind, source_z, core)
        return remote(
            dst if src is None else src, dst, pair_send.at[kind, source_z], pair_recv.at[kind, source_z], at.partner
        )

    def pair_arrival(kind, source_z):
        dst = pair_region(kind, source_z, 1 - core)
        return remote(dst, dst, pair_send.at[kind, source_z], pair_recv.at[kind, source_z], at.partner)

    keep = pltpu.make_async_copy(own_ref, slot(z, False, False), own_sem)
    pl.when(z < DEPTH - 1)(lambda: up(z, own_ref).start())
    pl.when(z > 0)(lambda: down(z, own_ref).start())
    side(0, z, own_ref).start()
    side(1, z, own_ref).start()
    pair(0, z, own_ref).start()
    keep.start()

    def plane(source_z):
        side_arrival(0, source_z).wait_recv()
        side(2, source_z).start()
        pair(1, source_z).start()
        side_arrival(1, source_z).wait_recv()
        side(3, source_z).start()
        pair(2, source_z).start()

    def column(source_z):
        side(0, source_z).start()
        side(1, source_z).start()
        pair(0, source_z).start()

    for distance in range(1, DEPTH + 1):

        def from_below(source_z=z - distance):
            up(source_z).wait_recv()
            pl.when(z < DEPTH - 1)(lambda: up(source_z).start())
            column(source_z)

        def from_above(source_z=z + distance):
            down(source_z).wait_recv()
            pl.when(z > 0)(lambda: down(source_z).start())
            column(source_z)

        pl.when(z - distance >= 0)(from_below)
        pl.when(z + distance <= DEPTH - 1)(from_above)
        past = distance - 1
        if past == 0:
            plane(z)
        else:
            pl.when(z - past >= 0)(functools.partial(plane, z - past))
            pl.when(z + past <= DEPTH - 1)(functools.partial(plane, z + past))

    def corner(source_z):
        side_arrival(2, source_z).wait_recv()
        pair(3, source_z).start()
        side_arrival(3, source_z).wait_recv()
        pair(4, source_z).start()

    for distance in range(DEPTH):
        if distance == 0:
            corner(z)
        else:
            pl.when(z - distance >= 0)(functools.partial(corner, z - distance))
            pl.when(z + distance <= DEPTH - 1)(functools.partial(corner, z + distance))
    keep.wait()
    for source_z in range(DEPTH):
        for kind in range(5):
            pair_arrival(kind, source_z).wait_recv()
            pair(kind, source_z).wait_send()
        for kind in range(4):
            side(kind, source_z).wait_send()
        pl.when((z < DEPTH - 1) & (source_z <= z))(lambda: up(source_z).wait_send())
        pl.when((z > 0) & (source_z >= z))(lambda: down(source_z).wait_send())


SPREAD_SEMS = [
    pltpu.SemaphoreType.DMA,
    pltpu.SemaphoreType.DMA((2, DEPTH)),
    pltpu.SemaphoreType.DMA((2, DEPTH)),
    pltpu.SemaphoreType.DMA((4, DEPTH)),
    pltpu.SemaphoreType.DMA((4, DEPTH)),
    pltpu.SemaphoreType.DMA((5, DEPTH)),
    pltpu.SemaphoreType.DMA((5, DEPTH)),
]


def gather_kernel(own_ref, misc_ref, out_ref, misc_out, misc_send, misc_recv, *sems):
    at = Place()
    at.greet()
    to_pair = remote(misc_ref, misc_out.at[at.mp_index], misc_send.at[0], misc_recv.at[0], at.partner)
    to_side = remote(misc_ref, misc_out.at[at.mp_index], misc_send.at[1], misc_recv.at[1], at.y_side)
    to_pair.start()
    to_side.start()
    misc_out[at.mp_index] = misc_ref[...]
    over = (1 - at.y) * 2 + at.core
    from_side = remote(misc_ref, misc_out.at[over], misc_send.at[1], misc_recv.at[1], at.y_side)
    relay = remote(misc_out.at[over], misc_out.at[over], misc_send.at[2], misc_recv.at[2], at.partner)
    spread(at, own_ref, out_ref, *sems)
    from_side.wait_recv()
    relay.start()
    beside = at.y * 2 + 1 - at.core
    remote(misc_ref, misc_out.at[beside], misc_send.at[0], misc_recv.at[0], at.partner).wait_recv()
    across = (1 - at.y) * 2 + 1 - at.core
    remote(misc_ref, misc_out.at[across], misc_send.at[2], misc_recv.at[2], at.partner).wait_recv()
    to_pair.wait_send()
    to_side.wait_send()
    relay.wait_send()


def gather_all(own, misc):
    rows, columns = own.shape
    return pl.pallas_call(
        gather_kernel,
        out_shape=(
            jax.ShapeDtypeStruct((32, rows, columns), own.dtype),
            jax.ShapeDtypeStruct((4,) + misc.shape, misc.dtype),
        ),
        in_specs=[pl.BlockSpec(memory_space=pltpu.VMEM)] * 2,
        out_specs=(pl.BlockSpec(memory_space=pl.ANY), pl.BlockSpec(memory_space=pltpu.VMEM)),
        scratch_shapes=[pltpu.SemaphoreType.DMA((3,)), pltpu.SemaphoreType.DMA((3,))] + SPREAD_SEMS,
        compiler_params=pltpu.CompilerParams(collective_id=0, has_side_effects=True),
        name="gather_weights",
    )(own, misc)


def collect(at, grads, total_ref, mine, pair_buf, corner_x, corner_y, full_x, full_y, z_up, z_down, z_out,
            load_sem, pair_send, pair_recv, side_send, side_recv, z_send, z_recv, between):
    rows = total_ref.shape[0]
    half = rows // 2
    z, x, y, core = at.z, at.x, at.y, at.core
    low, high = pl.ds(0, half), pl.ds(half, rows - half)
    orders = ((3, 2, 1, 0), (3, 0, 2, 1), (0, 3, 1, 2), (0, 1, 2, 3))

    def turn(step):
        choice = jnp.int32(orders[3][step])
        for which in range(3):
            choice = jnp.where(z == which, jnp.int32(orders[which][step]), choice)
        return choice

    turns = [turn(step) for step in range(DEPTH)]

    def load(target, y_of):
        return pltpu.make_async_copy(
            grads.at[y_of * 2 + core, target], mine.at[y_of, target], load_sem.at[y_of, target]
        )

    def pair(target, y_of):
        return remote(
            grads.at[y_of * 2 + 1 - core, target], pair_buf.at[y_of, target],
            pair_send.at[y_of, target], pair_recv.at[y_of, target], at.partner,
        )

    def corner(kind, target):
        part = mine.at[1 - y, target, 1 - x]
        if kind == 0:
            return remote(part.at[low], corner_y.at[target], side_send.at[0, target], side_recv.at[0, target], at.y_side)
        return remote(part.at[high], corner_x.at[target], side_send.at[1, target], side_recv.at[1, target], at.x_side)

    def full(kind, target):
        if kind == 2:
            return remote(mine.at[y, target, 1 - x], full_x.at[target], side_send.at[2, target], side_recv.at[2, target], at.x_side)
        return remote(mine.at[1 - y, target, x], full_y.at[target], side_send.at[3, target], side_recv.at[3, target], at.y_side)

    def up(target):
        return remote(z_out.at[target], z_up.at[target], z_send.at[target], z_recv.at[0, target], at.above)

    def down(target):
        return remote(z_out.at[target], z_down.at[target], z_send.at[target], z_recv.at[1, target], at.below)

    wide = jnp.float32
    for target in turns:
        for y_of in (0, 1):
            pair(target, y_of).start()
            load(target, y_of).start()

    def first(target):
        for y_of in (0, 1):
            load(target, y_of).wait()
            pair(target, y_of).wait_recv()

        def add(which, carry):
            y_of, x_of = which // 2, which % 2
            mine[y_of, target, x_of] = (
                mine[y_of, target, x_of].astype(wide) + pair_buf[y_of, target, x_of].astype(wide)
            ).astype(mine.dtype)
            return carry

        lax.fori_loop(0, 4, add, 0)
        corner(0, target).start()
        corner(1, target).start()

    def second(target):
        corner(0, target).wait_recv()
        mine[y, target, 1 - x, low] = (
            mine[y, target, 1 - x, low].astype(wide) + corner_y[target].astype(wide)
        ).astype(mine.dtype)
        full(2, target).start()
        corner(1, target).wait_recv()
        mine[1 - y, target, x, high] = (
            mine[1 - y, target, x, high].astype(wide) + corner_x[target].astype(wide)
        ).astype(mine.dtype)
        full(3, target).start()

    def third(target, last):
        full(2, target).wait_recv()
        full(3, target).wait_recv()
        total_ref[...] = mine[y, target, x].astype(wide) + (
            full_x[target].astype(wide) + full_y[target].astype(wide)
        )

        def add_below():
            up(target).wait_recv()
            total_ref[...] += z_up[target].astype(wide)

        def add_above():
            down(target).wait_recv()
            total_ref[...] += z_down[target].astype(wide)

        pl.when((target >= z) & (z > 0))(add_below)
        pl.when((target <= z) & (z < DEPTH - 1))(add_above)
        if not last:
            z_out[target] = total_ref[...].astype(z_out.dtype)
            pl.when(target > z)(lambda: up(target).start())
            pl.when(target < z)(lambda: down(target).start())

    for step in range(DEPTH + 2):
        between(step)
        if step < DEPTH:
            first(turns[step])
        if 1 <= step <= DEPTH:
            second(turns[step - 1])
        if step >= 2:
            third(turns[step - 2], step - 2 == DEPTH - 1)
    for target in range(DEPTH):
        for y_of in (0, 1):
            pair(target, y_of).wait_send()
        for kind in (0, 1):
            corner(kind, target).wait_send()
        for kind in (2, 3):
            full(kind, target).wait_send()
        pl.when(target != z)(lambda: up(target).wait_send())


def collect_scratch(rows, columns, dtype):
    return [
        pltpu.VMEM((2, DEPTH, 2, rows, columns), dtype),
        pltpu.VMEM((2, DEPTH, 2, rows, columns), dtype),
        pltpu.VMEM((DEPTH, rows // 2, columns), dtype),
        pltpu.VMEM((DEPTH, rows // 2, columns), dtype),
        pltpu.VMEM((DEPTH, rows, columns), dtype),
        pltpu.VMEM((DEPTH, rows, columns), dtype),
        pltpu.VMEM((DEPTH, rows, columns), dtype),
        pltpu.VMEM((DEPTH, rows, columns), dtype),
        pltpu.VMEM((DEPTH, rows, columns), dtype),
        pltpu.SemaphoreType.DMA((2, DEPTH)),
        pltpu.SemaphoreType.DMA((2, DEPTH)),
        pltpu.SemaphoreType.DMA((2, DEPTH)),
        pltpu.SemaphoreType.DMA((4, DEPTH)),
        pltpu.SemaphoreType.DMA((4, DEPTH)),
        pltpu.SemaphoreType.DMA((DEPTH,)),
        pltpu.SemaphoreType.DMA((2, DEPTH)),
    ]


N_COLLECT = 16


def muon_kernel(grads, moment_ref, small_ref, grad_out, moment_out, next_all, small_out,
                own_next, small_parts, small_in, small_send, small_recv, *scratch):
    at = Place()
    at.greet(far=True)
    peers = (at.partner, at.x_side, at.y_side, at.z_near, at.z_far)

    def swap(stage):
        source = small_ref if stage == 0 else small_parts.at[stage - 1]
        return remote(source, small_in.at[stage], small_send.at[stage], small_recv.at[stage], peers[stage])

    def between(step):
        if 1 <= step <= 5:
            stage = step - 1
            swap(stage).wait_recv()
            held = small_ref[...] if stage == 0 else small_parts[stage - 1]
            held = held + small_in[stage]
            if stage < 4:
                small_parts[stage] = held
            else:
                small_out[...] = held
        if step < 5:
            swap(step).start()

    collect(at, grads, grad_out, *scratch[:N_COLLECT], between)
    for stage in range(5):
        swap(stage).wait_send()
    grad = grad_out[...]
    moment = muon_beta * moment_ref[...] + grad
    moment_out[...] = moment
    own_next[...] = (grad + muon_beta * moment).astype(own_next.dtype)
    spread(at, own_next, next_all, *scratch[N_COLLECT:])


def muon_exchange(grads, moment, small):
    rows, columns = moment.shape
    shape = jax.ShapeDtypeStruct((rows, columns), jnp.float32)
    vmem = pl.BlockSpec(memory_space=pltpu.VMEM)
    hbm = pl.BlockSpec(memory_space=pl.ANY)
    return pl.pallas_call(
        muon_kernel,
        out_shape=(
            shape,
            shape,
            jax.ShapeDtypeStruct((32, rows, columns), jnp.bfloat16),
            jax.ShapeDtypeStruct(small.shape, jnp.float32),
        ),
        in_specs=[hbm, vmem, vmem],
        out_specs=(vmem, vmem, hbm, vmem),
        scratch_shapes=[
            pltpu.VMEM((rows, columns), jnp.bfloat16),
            pltpu.VMEM((4,) + small.shape, jnp.float32),
            pltpu.VMEM((5,) + small.shape, jnp.float32),
            pltpu.SemaphoreType.DMA((5,)),
            pltpu.SemaphoreType.DMA((5,)),
        ]
        + collect_scratch(rows, columns, jnp.bfloat16)
        + SPREAD_SEMS,
        compiler_params=pltpu.CompilerParams(
            collective_id=1, has_side_effects=True, vmem_limit_bytes=40 * 1024 * 1024
        ),
        name="muon_exchange",
    )(grads.reshape(4, DEPTH, 2, rows, columns), moment, small)


def ns_kernel(next_all, own_images, swapped, images_all, products, rows_buf, map_buf, sem, keep_sem,
              act_send, act_recv, swap_send, swap_recv):
    at = Place()
    mp_index, dp_index = at.mp_index, at.dp_index
    counts = (48, 16, 64, 64)
    pieces = own_images.shape[0]
    over = (1 - at.y) * 2 + at.core
    across = (1 - at.y) * 2 + 1 - at.core
    beside = at.y * 2 + 1 - at.core
    mp_peers = [{"dp": dp_index, "mp": lax.rem(mp_index + shift, 4)} for shift in (1, 2, 3)]
    barrier = pltpu.get_barrier_semaphore()
    for device in mp_peers:
        pl.semaphore_signal(barrier, inc=1, device_id=device, device_id_type=MESH)

    def fetch(which):
        count = counts[which]
        copy = pltpu.make_async_copy(
            next_all.at[:, pl.ds(sum(counts[:which]), count)], rows_buf.at[:, pl.ds(0, count)], sem
        )
        copy.start()
        if count < 64:
            rows_buf[:, pl.ds(count, 64 - count)] = jnp.zeros((32, 64 - count, C), rows_buf.dtype)
        copy.wait()

    for which in range(4):
        pl.when(mp_index == which)(functools.partial(fetch, which))
    pl.semaphore_wait(barrier, 3)

    def slot(of_mp, image):
        return images_all.at[of_mp * pieces + image]

    def keep_copy(image):
        return pltpu.make_async_copy(own_images.at[image], slot(mp_index, image), keep_sem.at[image])

    def own_copy(which, image):
        device = (at.partner, at.y_side)[which]
        return remote(
            own_images.at[image], slot(mp_index, image), act_send.at[which, image], act_recv.at[which, image], device
        )

    def own_arrival(which, image):
        source, device = ((beside, at.partner), (over, at.y_side))[which]
        return remote(
            own_images.at[image], slot(source, image), act_send.at[which, image], act_recv.at[which, image], device
        )

    def relay(image):
        return remote(slot(over, image), slot(over, image), act_send.at[2, image], act_recv.at[2, image], at.partner)

    def relay_arrival(image):
        return remote(
            slot(across, image), slot(across, image), act_send.at[2, image], act_recv.at[2, image], at.partner
        )

    for image in range(pieces):
        own_copy(1, image).start()
    for image in range(pieces):
        own_copy(0, image).start()
        keep_copy(image).start()

    gram = None
    for part in range(4):
        block = rows_buf[8 * part : 8 * (part + 1)].reshape(512, C)
        term = dot_tn(block, block)
        gram = term if gram is None else gram + term
    eye = (
        lax.broadcasted_iota(jnp.int32, (C, C), 0) == lax.broadcasted_iota(jnp.int32, (C, C), 1)
    ).astype(wide)
    norm_value = jnp.sqrt(jnp.sum(jnp.sum(gram * eye, axis=1, keepdims=True), axis=0, keepdims=True)) + ns_eps
    gram = gram / (norm_value * norm_value)

    def dot_high(a, b):
        return jnp.dot(a, b, precision=lax.Precision.HIGH, preferred_element_type=wide)

    def pass_on(image):
        own_arrival(1, image).wait_recv()
        relay(image).start()

    total = None
    for iteration in range(NS_ITERS):
        square = dot_high(gram, gram)
        poly = coef_a * eye + (coef_b * gram + coef_c * square)
        total = poly if total is None else dot_high(total, poly)
        if iteration + 1 < NS_ITERS:
            gram = dot_high(dot_high(gram, poly), poly)
    map_buf[...] = total / norm_value

    def swap_copy(which):
        return remote(
            products.at[lax.rem(mp_index + which + 1, 4)], swapped.at[mp_index],
            swap_send.at[which], swap_recv.at[which], mp_peers[which],
        )

    for group in range(4):
        rows = rows_buf[group * 8 + dp_index].astype(wide)
        products[group] = dot_high(rows, map_buf[...]).astype(products.dtype)
    for which in (1, 2, 0):
        swap_copy(which).start()
    swapped[mp_index] = products[mp_index]
    for image in range(pieces):
        pass_on(image)
    for image in range(pieces):
        own_arrival(0, image).wait_recv()
        relay_arrival(image).wait_recv()
        own_copy(0, image).wait_send()
        own_copy(1, image).wait_send()
        relay(image).wait_send()
        keep_copy(image).wait()
    for which in range(3):
        source = lax.rem(mp_index + 3 - which, 4)
        remote(
            products.at[source], swapped.at[source], swap_send.at[which], swap_recv.at[which],
            {"dp": dp_index, "mp": source},
        ).wait_recv()
        swap_copy(which).wait_send()


def newton_schulz_rows(next_all, own_images):
    vmem = pl.BlockSpec(memory_space=pltpu.VMEM)
    hbm = pl.BlockSpec(memory_space=pl.ANY)
    pieces = own_images.shape[0]
    return pl.pallas_call(
        ns_kernel,
        out_shape=(
            jax.ShapeDtypeStruct((4, 64, C), low),
            jax.ShapeDtypeStruct((4 * pieces,) + own_images.shape[1:], low),
        ),
        in_specs=[hbm, vmem],
        out_specs=(vmem, hbm),
        scratch_shapes=[
            pltpu.VMEM((4, 64, C), low),
            pltpu.VMEM((32, 64, C), low),
            pltpu.VMEM((C, C), wide),
            pltpu.SemaphoreType.DMA,
            pltpu.SemaphoreType.DMA((pieces,)),
            pltpu.SemaphoreType.DMA((3, pieces)),
            pltpu.SemaphoreType.DMA((3, pieces)),
            pltpu.SemaphoreType.DMA((3,)),
            pltpu.SemaphoreType.DMA((3,)),
        ],
        compiler_params=pltpu.CompilerParams(
            collective_id=2, has_side_effects=True, vmem_limit_bytes=40 * 1024 * 1024
        ),
        name="newton_schulz",
    )(next_all, own_images)


def split_low(values):
    high = lax.reduce_precision(values, exponent_bits=8, mantissa_bits=7)
    return high.astype(jnp.bfloat16), (values - high).astype(jnp.bfloat16)


def dot_three(left, right):
    left_high, left_rest = left
    right_high, right_rest = right
    wide = dict(preferred_element_type=jnp.float32)
    return (
        jnp.dot(left_rest, right_high, **wide)
        + jnp.dot(left_high, right_rest, **wide)
        + jnp.dot(left_high, right_high, **wide)
    )


def newton_schulz(gram):
    width = gram.shape[0]
    eye = jnp.eye(width, dtype=jnp.float32)
    norm_value = jnp.sqrt(jnp.sum(gram * eye)) + ns_eps
    gram = gram / (norm_value * norm_value)
    total = None
    for iteration in range(NS_ITERS):
        parts = split_low(gram)
        square = dot_three(parts, parts)
        poly = coef_a * eye + (coef_b * gram + coef_c * square)
        poly_parts = split_low(poly)
        total = poly if total is None else dot_three(split_low(total), poly_parts)
        if iteration + 1 < NS_ITERS:
            half = dot_three(parts, poly_parts)
            gram = dot_three(split_low(half), poly_parts)
    return total / norm_value


def adam_update(grad_sum, first_moment, second_moment):
    first_new = adam_one * first_moment + (1.0 - adam_one) * grad_sum
    second_new = adam_two * second_moment + (1.0 - adam_two) * grad_sum * grad_sum
    first_hat = first_new / (1.0 - adam_one**adam_step)
    second_hat = second_new / (1.0 - adam_two**adam_step)
    return (-adam_rate * first_hat / (jnp.sqrt(second_hat) + adam_eps), first_new, second_new)


def exchange_plain(own_low, own_moments, rows):
    everyone = ("mp", "dp")
    starts = [sum(rows[:which]) for which in range(4)]

    def cut(stacked):
        return [stacked[:, start : start + count] for start, count in zip(starts, rows)]

    gathered = [
        part.reshape(-1, C) for part in cut(lax.all_gather(own_low, everyone, axis=0, tiled=False))
    ]

    def finish(big_local):
        mp_size, dp_size = lax.axis_size("mp"), lax.axis_size("dp")
        mp_index, dp_index = lax.axis_index("mp"), lax.axis_index("dp")
        devices = mp_size * dp_size
        stacked_grads = jnp.concatenate(
            [grad.reshape(devices, count, C) for grad, count in zip(big_local, rows)], axis=1
        )
        own_grads = lax.psum_scatter(
            stacked_grads.reshape(devices * sum(rows), C), everyone, scatter_dimension=0, tiled=True
        ).astype(wide)
        own_buffers = muon_beta * own_moments + own_grads
        own_nesterov = own_grads + muon_beta * own_buffers
        iterate_all = lax.all_gather(own_nesterov.astype(low), everyone, axis=0, tiled=False)
        grams = jnp.stack([dot_tn(part.reshape(-1, C), part.reshape(-1, C)) for part in cut(iterate_all)])
        ortho_map = newton_schulz(lax.dynamic_index_in_dim(grams, mp_index, 0, keepdims=False))
        most = max(rows)
        picked = lax.dynamic_slice(
            iterate_all.reshape(mp_size, dp_size, sum(rows), C),
            (
                jnp.int32(0),
                dp_index.astype(jnp.int32),
                jnp.array(starts, jnp.int32)[mp_index],
                jnp.int32(0),
            ),
            (mp_size, 1, most, C),
        ).reshape(mp_size * most, C)
        map_parts = split_low(ortho_map)
        products = dot(picked, map_parts[0]) + dot(picked, map_parts[1])
        swapped = lax.all_to_all(products.reshape(mp_size, most, C), "mp", 0, 0, tiled=False)
        return own_grads, own_buffers, swapped

    return gathered, finish


def shards(
    images,
    cotangent,
    qkv_weight,
    proj_weight,
    expand_weight,
    contract_weight,
    qkv_moment,
    proj_moment,
    expand_moment,
    contract_moment,
    vectors,
    qv_bias,
    expand_bias,
    rel_table,
    vectors_first,
    vectors_second,
    qv_first,
    qv_second,
    expand_bias_first,
    expand_bias_second,
    table_first,
    table_second,
    region_ids,
    pos_index,
    image_counts,
):
    everyone = ("mp", "dp")
    mp_size, dp_size = lax.axis_size("mp"), lax.axis_size("dp")
    mp_index = lax.axis_index("mp")
    linked = mp_size == 4 and dp_size == 8
    per_device = IMG_DEV // mp_size
    first_image = (mp_index * per_device).astype(jnp.int32)
    place = jnp.stack([first_image, image_counts[0]])
    own_images = lax.dynamic_slice_in_dim(images, first_image, per_device, 0)
    own_cotangent = lax.dynamic_slice_in_dim(cotangent, first_image, per_device, 0)
    weights_all = (qkv_weight, proj_weight, expand_weight, contract_weight)
    rows = [weight.shape[0] for weight in weights_all]
    starts = [sum(rows[:which]) for which in range(4)]
    own_low = jnp.concatenate([weight.astype(low) for weight in weights_all], axis=0)
    own_moments = jnp.concatenate(
        (qkv_moment, proj_moment, expand_moment, contract_moment), axis=0
    )
    if linked:
        misc = jnp.concatenate(
            [
                expand_bias[None],
                jnp.pad(qv_bias.reshape(1, -1), ((0, 0), (0, C - qv_bias.size))),
                jnp.pad(rel_table.T, ((0, 2), (0, C - TABLE))),
            ],
            axis=0,
        )
        gathered, misc_all = gather_all(own_low, misc)
        expand_full = misc_all[:, 0].reshape(4, C)
        qv_full = misc_all[:, 1, : qv_bias.size].reshape(4, 2, -1).transpose(1, 0, 2).reshape(2, C)
        table_full = misc_all[:, 2:6, :TABLE].reshape(HEADS, TABLE)
    else:
        gathered, finish_plain = exchange_plain(own_low, own_moments, rows)
        qv_full = lax.all_gather(qv_bias, "mp", axis=1, tiled=True)
        expand_full = lax.all_gather(expand_bias, "mp", axis=0, tiled=True).reshape(4, C)
        table_full = lax.all_gather(rel_table.T, "mp", axis=0, tiled=True)
    onehot = (
        jnp.arange(TABLE, dtype=jnp.int32)[:, None] == pos_index.reshape(1, SPAN * SPAN)
    ).astype(wide)
    pos_bias = jnp.dot(table_full, onehot, precision=highest).reshape(HEADS, SPAN, SPAN)
    window_regions = to_windows(region_ids.reshape(1, TOK, 1))[:, :, 0]
    window_mask = jnp.where(
        window_regions[:, :, None] != window_regions[:, None, :], mask_value, 0.0
    ).astype(wide)
    bias = pair_bias(pos_bias, window_mask)
    block_low, input_low, big_local, small_rows, table_pairs = run_layer(
        linked, per_device, place, own_images, own_cotangent, vectors, qv_full, expand_full, bias, gathered
    )
    if linked:
        block_out = block_low
    else:
        block_out = lax.all_gather(block_low, "mp", axis=0, tiled=True)
        input_grad = lax.all_gather(input_low, "mp", axis=0, tiled=True)
    pairs = table_pairs.reshape(HEADS, PAIR, PAIR)
    bias_heads = pairs[:, :SPAN, :SPAN] + pairs[:, SPAN : 2 * SPAN, SPAN : 2 * SPAN]
    table_local = lax.dot_general(
        bias_heads.reshape(HEADS, SPAN * SPAN),
        onehot,
        (((1,), (1,)), ((), ())),
        precision=highest,
        preferred_element_type=wide,
    )
    if linked:
        small_own = jnp.concatenate(
            [small_rows, jnp.pad(table_local, ((0, 0), (0, C - TABLE)))], axis=0
        )
        own_grads, own_buffers, next_all, small_all = muon_exchange(big_local, own_moments, small_own)
        swapped, input_grad = newton_schulz_rows(next_all, input_low)
        small_full, table_all = small_all[:HEADS], small_all[HEADS:, :TABLE]
    else:
        small_full, table_all = lax.psum((small_rows, table_local), everyone)
        own_grads, own_buffers, swapped = finish_plain(big_local)
    ortho = [swapped[which, :count].astype(wide) for which, count in enumerate(rows)]
    shares = [own_grads[start : start + count] for start, count in zip(starts, rows)]
    buffers = [own_buffers[start : start + count] for start, count in zip(starts, rows)]

    def own_columns(full, width):
        return lax.dynamic_slice_in_dim(full, mp_index * width, width, full.ndim - 1)

    small_sums = (
        small_full[:6],
        own_columns(small_full[6:8], qv_bias.shape[1]),
        own_columns(small_full[8:12].reshape(FF), expand_bias.shape[0]),
        lax.dynamic_slice_in_dim(table_all, mp_index * rel_table.shape[1], rel_table.shape[1], 0).T,
    )
    factors = (math.sqrt(3.0), 1.0, math.sqrt(max(1.0, FF / C)), 1.0)
    new_steps = tuple(
        (
            -muon_rate * (muon_decay * weight + factor * ortho_part)
            for weight, ortho_part, factor in zip(weights_all, ortho, factors)
        )
    )
    vectors_step, vectors_first_new, vectors_second_new = adam_update(
        small_sums[0], vectors_first, vectors_second
    )
    qv_step, qv_first_new, qv_second_new = adam_update(small_sums[1], qv_first, qv_second)
    expand_bias_step, expand_bias_first_new, expand_bias_second_new = adam_update(
        small_sums[2], expand_bias_first, expand_bias_second
    )
    table_step, table_first_new, table_second_new = adam_update(
        small_sums[3], table_first, table_second
    )
    return (
        block_out,
        input_grad,
        shares[0],
        shares[1],
        shares[2],
        shares[3],
        small_sums[0],
        small_sums[1],
        small_sums[2],
        small_sums[3],
        new_steps[0],
        new_steps[1],
        new_steps[2],
        new_steps[3],
        buffers[0],
        buffers[1],
        buffers[2],
        buffers[3],
        vectors_step,
        qv_step,
        expand_bias_step,
        table_step,
        vectors_first_new,
        vectors_second_new,
        qv_first_new,
        qv_second_new,
        expand_bias_first_new,
        expand_bias_second_new,
        table_first_new,
        table_second_new,
    )


def solution(mesh):
    return jax.shard_map(
        shards,
        mesh=mesh,
        in_specs=(
            P("dp", None, None),
            P("dp", None, None),
            P(("mp", "dp"), None),
            P(("mp", "dp"), None),
            P(("mp", "dp"), None),
            P(("mp", "dp"), None),
            P(("mp", "dp"), None),
            P(("mp", "dp"), None),
            P(("mp", "dp"), None),
            P(("mp", "dp"), None),
            P(),
            P(None, "mp"),
            P("mp"),
            P(None, "mp"),
            P(),
            P(),
            P(None, "mp"),
            P(None, "mp"),
            P("mp"),
            P("mp"),
            P(None, "mp"),
            P(None, "mp"),
            P(),
            P(),
            P("dp"),
        ),
        out_specs=(
            P("dp", None, None),
            P("dp", None, None),
            P(("mp", "dp"), None),
            P(("mp", "dp"), None),
            P(("mp", "dp"), None),
            P(("mp", "dp"), None),
            P(),
            P(None, "mp"),
            P("mp"),
            P(None, "mp"),
            P(("mp", "dp"), None),
            P(("mp", "dp"), None),
            P(("mp", "dp"), None),
            P(("mp", "dp"), None),
            P(("mp", "dp"), None),
            P(("mp", "dp"), None),
            P(("mp", "dp"), None),
            P(("mp", "dp"), None),
            P(),
            P(None, "mp"),
            P("mp"),
            P(None, "mp"),
            P(),
            P(),
            P(None, "mp"),
            P(None, "mp"),
            P("mp"),
            P("mp"),
            P(None, "mp"),
            P(None, "mp"),
        ),
        check_vma=False,
    )
```

```python
import functools
import math

import jax
import jax.numpy as jnp
import numpy as np
from jax import lax
from jax.experimental import pallas as pl
from jax.experimental.pallas import tpu as pltpu
from jax.sharding import PartitionSpec as P

C = 512
HEADS = 16
HD = 32
FF = 2048
WIN = 7
SIDE = 14
SHIFT = 3
SPAN = WIN * WIN
TOK = SIDE * SIDE
NS_ITERS = 5
IMG_DEV = 16
TABLE = 169
PAIR = 112
ROWS = 2 * PAIR
GROUP = 4

norm_eps = 1e-05
ns_eps = 1e-07
coef_a = 3.4445
coef_b = -4.775
coef_c = 2.0315
muon_rate = 0.3
muon_decay = 0.1
muon_beta = 0.95
adam_rate = 0.1
adam_one = 0.9
adam_two = 0.999
adam_eps = 1e-08
adam_step = 4
mask_value = -100.0
away = -1e30
wide = jnp.float32
low = jnp.bfloat16
highest = lax.Precision.HIGHEST


def to_windows(field_values):
    image_total = field_values.shape[0]
    channels = field_values.shape[-1]
    blocks = SIDE // WIN
    grid_values = field_values.reshape(image_total, SIDE, SIDE, channels)
    grid_values = jnp.roll(grid_values, (-SHIFT, -SHIFT), axis=(1, 2))
    grid_values = grid_values.reshape(image_total, blocks, WIN, blocks, WIN, channels)
    grid_values = grid_values.transpose(0, 1, 3, 2, 4, 5)
    return grid_values.reshape(image_total * blocks * blocks, WIN * WIN, channels)


def window_order():
    order = np.full((ROWS,), -1, np.int64)
    for window in range(4):
        top, left = window // 2, window % 2
        for token in range(SPAN):
            row = (top * WIN + token // WIN + SHIFT) % SIDE
            column = (left * WIN + token % WIN + SHIFT) % SIDE
            order[(window // 2) * PAIR + (window % 2) * SPAN + token] = row * SIDE + column
    return order


def dot(a, b):
    return jnp.dot(a, b, preferred_element_type=wide)


def dot_nt(a, b):
    return lax.dot_general(a, b, (((1,), (1,)), ((), ())), preferred_element_type=wide)


def dot_tn(a, b):
    return lax.dot_general(a, b, (((0,), (0,)), ((), ())), preferred_element_type=wide)


def mean_of(values):
    return jnp.sum(values, axis=-1, keepdims=True) * (1.0 / C)


def normalize(values):
    centered = values - mean_of(values)
    inv_scale = lax.rsqrt(mean_of(centered * centered) + norm_eps)
    return centered * inv_scale, inv_scale


def normalize_back(grad_norm, normed, inv_scale, gain):
    scaled = grad_norm * gain
    return inv_scale * (scaled - mean_of(scaled) - normed * mean_of(scaled * normed))


def column_sum(values):
    return jnp.sum(values, axis=0, keepdims=True)


def head_masks():
    lane = lax.broadcasted_iota(jnp.int32, (1, 128), 1) // HD
    return [(lane == head).astype(wide).astype(low) for head in range(GROUP)]


def stack_heads(block, masks):
    return jnp.concatenate([block * mask for mask in masks], axis=0)


def pick_heads(stacked):
    lane = lax.broadcasted_iota(jnp.int32, (PAIR, 128), 1)
    parts = [stacked[PAIR * head : PAIR * (head + 1)] for head in range(GROUP)]
    return jnp.where(
        lane < 2 * HD,
        jnp.where(lane < HD, parts[0], parts[1]),
        jnp.where(lane < 3 * HD, parts[2], parts[3]),
    )


def layer_kernel(
    packed, batch, place, images, cotangent, order, order_back, vectors, qv_bias, expand_bias, bias,
    qkv_hbm, proj_hbm, expand_hbm, contract_hbm,
    block_out, input_grad, *rest,
):
    n_grads = 1 if packed else 4
    grad_outs = rest[:n_grads]
    (small, table_sum, qkv_nat, qkv_w, proj_w, expand_w, contract_w,
     qkv_acc, proj_acc, expand_acc, contract_acc,
     qkv_s, att_s, back_s, probs_s, normed_s, first_s, middle_s, normed2_s, second_s,
     out_low_s, mlp_s, second_grad_s, sems) = rest[n_grads : n_grads + 24]
    step = pl.program_id(0)
    steps = pl.num_programs(0)
    masks = head_masks()
    if packed:
        staged, keep_sem, act_send, act_recv = rest[n_grads + 24 :]
        at = Place()
        per_device = staged.shape[0]
        over = (1 - at.y) * 2 + at.core
        across = (1 - at.y) * 2 + 1 - at.core
        beside = at.y * 2 + 1 - at.core

        def slot(mp_index, image):
            return block_out.at[mp_index * per_device + image]

        def keep_copy(image):
            return pltpu.make_async_copy(staged.at[image], slot(at.mp_index, image), keep_sem.at[image])

        def own_copy(which, image):
            device = (at.partner, at.y_side)[which]
            return remote(
                staged.at[image], slot(at.mp_index, image),
                act_send.at[which, image], act_recv.at[which, image], device,
            )

        def own_arrival(which, image):
            source, device = ((beside, at.partner), (over, at.y_side))[which]
            return remote(
                staged.at[image], slot(source, image),
                act_send.at[which, image], act_recv.at[which, image], device,
            )

        def relay(image):
            return remote(
                slot(over, image), slot(over, image), act_send.at[2, image], act_recv.at[2, image], at.partner
            )

        def relay_arrival(image):
            return remote(
                slot(across, image), slot(across, image), act_send.at[2, image], act_recv.at[2, image], at.partner
            )

        def pass_on(of_step):
            for slice_ in range(batch):
                image = of_step * batch + slice_
                own_arrival(1, image).wait_recv()
                relay(image).start()

        def greet():
            barrier = pltpu.get_barrier_semaphore()
            for device in (at.partner, at.y_side):
                pl.semaphore_signal(barrier, inc=1, device_id=device, device_id_type=MESH)
            pl.semaphore_wait(barrier, 2)

        pl.when(step == 0)(greet)

    def put_block(slice_, value):
        if packed:
            image = step * batch + slice_
            staged[image] = value
            own_copy(1, image).start()
            own_copy(0, image).start()
            keep_copy(image).start()
        else:
            block_out[slice_] = value

    def put_grad(slice_, value):
        input_grad[slice_] = value

    row = lax.broadcasted_iota(jnp.int32, (batch * ROWS, 1), 0) // ROWS
    live_scale = jnp.zeros((batch * ROWS, 1), wide)
    for slice_ in range(batch):
        is_live = (place[1] > place[0] + step * batch + slice_).astype(wide)
        live_scale = jnp.where(row == slice_, is_live, live_scale)

    def fetch(which):
        if packed:
            counts = (48, 16, 64, 64)
            source = qkv_hbm.at[:, pl.ds(sum(counts[:which]), counts[which])]
            target = (qkv_nat, proj_w, expand_w, contract_w)[which]
        else:
            source = (qkv_hbm, proj_hbm, expand_hbm, contract_hbm)[which]
            target = (qkv_nat, proj_w, expand_w, contract_w)[which]
        return pltpu.make_async_copy(source, target, sems.at[which])

    def rows_of(ref, count):
        return ref[...].reshape(count, C)

    def begin():
        for which in range(4):
            fetch(which).start()
        for ref in (qkv_acc, proj_acc, expand_acc, contract_acc, small, table_sum):
            ref[...] = jnp.zeros_like(ref)
        for which in range(4):
            fetch(which).wait()
        natural = rows_of(qkv_nat, 3 * C).reshape(HEADS, 3, HD, C)
        for kind in range(3):
            qkv_w[kind] = natural[:, kind].reshape(C, C)

    pl.when(step == 0)(begin)

    tokens = jnp.concatenate([dot(order[...], images[slice_]) for slice_ in range(batch)], axis=0)
    normed, inv_one = normalize(tokens)
    normed_s[...] = normed
    first_in = (normed * vectors[0:1] + vectors[1:2]).astype(low)
    first_s[...] = first_in
    for kind in range(3):
        projected = dot_nt(first_in, qkv_w[kind])
        if kind != 1:
            projected = projected + qv_bias[kind // 2 : kind // 2 + 1]
        projected = projected.astype(low)
        for group in range(4):
            qkv_s[kind * 4 + group] = projected[:, 128 * group : 128 * (group + 1)]
    score_scale = 1.0 / math.sqrt(HD)

    def attend(which, carry):
        pair, group = which // 4, which % 4
        pair_scores = bias[pair, group]
        for slice_ in range(batch):
            rows = pl.ds(pl.multiple_of(slice_ * ROWS + pair * PAIR, 16), PAIR)
            queries = stack_heads(qkv_s[group, rows], masks)
            scores = dot_nt(queries, qkv_s[4 + group, rows]) * score_scale + pair_scores
            top = jnp.max(scores, axis=-1, keepdims=True)
            exponent = jnp.exp(scores - top)
            attention = exponent / jnp.sum(exponent, axis=-1, keepdims=True)
            probs_s[slice_, which] = attention
            att_s[group, rows] = pick_heads(dot(attention.astype(low), qkv_s[8 + group, rows])).astype(low)
        return carry

    lax.fori_loop(0, 8, attend, 0)
    attended = jnp.concatenate([att_s[group] for group in range(4)], axis=1)
    middle = tokens + (dot(attended, rows_of(proj_w, C)) + vectors[4:5])
    middle_s[...] = middle
    normed_two, inv_two = normalize(middle)
    normed2_s[...] = normed_two
    second_in = (normed_two * vectors[2:3] + vectors[3:4]).astype(low)
    second_s[...] = second_in

    grad_tokens = jnp.concatenate([dot(order[...], cotangent[slice_]) for slice_ in range(batch)], axis=0)
    out_low = (grad_tokens * live_scale).astype(low)
    out_low_s[...] = out_low
    mlp_s[...] = jnp.zeros_like(mlp_s)
    second_grad_s[...] = jnp.zeros_like(second_grad_s)
    chunk = 512
    owners = expand_w.shape[0] // (FF // chunk)

    def feed(which, carry):
        units = pl.ds(pl.multiple_of(which * owners, owners), owners)
        expand_part = expand_w[units].reshape(chunk, C)
        contract_part = contract_w[units].reshape(chunk, C)
        second = second_s[...]
        grad_rows = out_low_s[...]
        hidden = dot_nt(second, expand_part) + expand_bias[which]
        cumulative = 0.5 * (1.0 + lax.erf(hidden * (1.0 / math.sqrt(2.0))))
        acted = (hidden * cumulative).astype(low)
        slope = cumulative + hidden * jnp.exp(-0.5 * hidden * hidden) * (1.0 / math.sqrt(2.0 * math.pi))
        mlp_s[...] += dot(acted, contract_part)
        hidden_grad32 = dot_nt(grad_rows, contract_part) * slope
        hidden_grad = hidden_grad32.astype(low)
        small[pl.ds(8 + which, 1)] += column_sum(hidden_grad.astype(wide))
        second_grad_s[...] += dot(hidden_grad, expand_part)
        units_wide = pl.ds(pl.multiple_of(which * chunk, chunk), chunk)
        contract_acc[units_wide] += dot_tn(acted, grad_rows)
        expand_acc[units_wide] += dot_tn(hidden_grad, second)
        return carry

    lax.fori_loop(0, FF // chunk, feed, 0)
    result = middle_s[...] + (mlp_s[...] + vectors[5:6])
    result = jnp.where(live_scale > 0.0, result, 0.0).astype(low)
    if packed:
        pl.when(step > 0)(lambda: pass_on(step - 1))
    for slice_ in range(batch):
        put_block(slice_, dot(order_back[...], result[ROWS * slice_ : ROWS * (slice_ + 1)]).astype(low))

    grad_out = out_low_s[...].astype(wide)
    second_grad = second_grad_s[...]
    normed_two = normed2_s[...]
    small[5:6] += column_sum(grad_out)
    small[3:4] += column_sum(second_grad)
    small[2:3] += column_sum(second_grad * normed_two)
    middle_grad = grad_out + normalize_back(second_grad, normed_two, inv_two, vectors[2:3])
    small[4:5] += column_sum(middle_grad)
    middle_s[...] = middle_grad
    attn_low = middle_grad.astype(low)
    attended = jnp.concatenate([att_s[group] for group in range(4)], axis=1)
    proj_acc[...] += dot_tn(attended, attn_low)
    attended_grad = dot_nt(attn_low, rows_of(proj_w, C)).astype(low)
    for group in range(4):
        att_s[group] = attended_grad[:, 128 * group : 128 * (group + 1)]

    def attend_back(which, carry):
        pair, group = which // 4, which % 4
        bias_grad = None
        for slice_ in range(batch):
            rows = pl.ds(pl.multiple_of(slice_ * ROWS + pair * PAIR, 16), PAIR)
            attention = probs_s[slice_, which]
            keys, values = qkv_s[4 + group, rows], qkv_s[8 + group, rows]
            grads = stack_heads(att_s[group, rows], masks)
            queries = stack_heads(qkv_s[group, rows], masks)
            probs_grad = dot_nt(grads, values)
            row_term = jnp.sum(attention * probs_grad, axis=-1, keepdims=True)
            score_grad = (attention * (probs_grad - row_term)).astype(low)
            wide_grad = score_grad.astype(wide)
            bias_grad = wide_grad if bias_grad is None else bias_grad + wide_grad
            back_s[group, rows] = (pick_heads(dot(score_grad, keys)) * score_scale).astype(low)
            back_s[4 + group, rows] = (dot_tn(score_grad, queries) * score_scale).astype(low)
            back_s[8 + group, rows] = dot_tn(attention.astype(low), grads).astype(low)
        table_sum[group] += bias_grad
        return carry

    lax.fori_loop(0, 8, attend_back, 0)
    first_in = first_s[...]
    first_grad = None
    for kind in range(3):
        back = jnp.concatenate([back_s[kind * 4 + group] for group in range(4)], axis=1)
        if kind != 1:
            row = 6 + kind // 2
            small[row : row + 1] += column_sum(back.astype(wide))
        qkv_acc[kind] += dot_tn(back, first_in)
        part = dot(back, qkv_w[kind])
        first_grad = part if first_grad is None else first_grad + part
    normed = normed_s[...]
    small[1:2] += column_sum(first_grad)
    small[0:1] += column_sum(first_grad * normed)
    token_grad = middle_s[...] + normalize_back(first_grad, normed, inv_one, vectors[0:1])
    token_low = token_grad.astype(low)
    for slice_ in range(batch):
        put_grad(slice_, dot(order_back[...], token_low[ROWS * slice_ : ROWS * (slice_ + 1)]).astype(low))

    def finish():
        if packed:
            pass_on(steps - 1)
        for kind in range(3):
            part = qkv_acc[kind].astype(low).reshape(HEADS, HD, C)
            if packed:
                out = grad_outs[0]
                for piece in range(2):
                    block = kind * 2 + piece
                    out[:, block // 3, pl.ds(16 * (block % 3), 16)] = part[:, 16 * piece : 16 * (piece + 1)]
            else:
                grad_outs[0][:, kind] = part
        if packed:
            out = grad_outs[0]
            out[:, :, pl.ds(48, 16)] = proj_acc[...].astype(low).reshape(16, 2, 16, C)
            out[:, :, pl.ds(64, 64)] = expand_acc[...].astype(low).reshape(16, 2, 64, C)
            out[:, :, pl.ds(128, 64)] = contract_acc[...].astype(low).reshape(16, 2, 64, C)
        else:
            grad_outs[1][...] = proj_acc[...].astype(low)
            grad_outs[2][...] = expand_acc[...].astype(low)
            grad_outs[3][...] = contract_acc[...].astype(low)
        if packed:

            def settle(image, carry):
                own_arrival(0, image).wait_recv()
                relay_arrival(image).wait_recv()
                own_copy(0, image).wait_send()
                own_copy(1, image).wait_send()
                relay(image).wait_send()
                keep_copy(image).wait()
                return carry

            lax.fori_loop(0, per_device, settle, 0)

    pl.when(step == steps - 1)(finish)


def run_layer(packed, per_device, place, images, cotangent, vectors, qv_bias, expand_bias, bias, weights):
    order_np = window_order()
    onehot = (order_np[:, None] == np.arange(TOK)[None, :]).astype(np.float32)
    order = jnp.asarray(onehot, low)
    order_back = jnp.asarray(onehot.T, low)
    any_spec = pl.BlockSpec(memory_space=pl.ANY)

    def whole(shape):
        return pl.BlockSpec(shape, lambda i, s: (0,) * len(shape), pipeline_mode=pl.Buffered(1))

    batch = 2 if per_device % 2 == 0 else 1
    span = batch * ROWS
    image_spec = pl.BlockSpec((batch, TOK, C), lambda i, s: (i, 0, 0))
    out_spec = any_spec if packed else image_spec
    images_out = IMG_DEV if packed else per_device
    exchange = [
        pltpu.VMEM((per_device, TOK, C), low),
        pltpu.SemaphoreType.DMA((per_device,)),
        pltpu.SemaphoreType.DMA((3, per_device)),
        pltpu.SemaphoreType.DMA((3, per_device)),
    ]
    limit = 60 * 1024 * 1024
    if packed:
        params = pltpu.CompilerParams(collective_id=3, has_side_effects=True, vmem_limit_bytes=limit)
    else:
        params = pltpu.CompilerParams(vmem_limit_bytes=limit)
    if packed:
        weights = (weights,) * 4
        grad_shapes = [(16, 2, 192, C)]
        weight_shapes = [(32, 48, C), (32, 16, C), (32, 64, C), (32, 64, C)]
    else:
        weights = (weights[0], weights[1], weights[2].reshape(FF // 64, 64, C), weights[3].reshape(FF // 64, 64, C))
        grad_shapes = [(HEADS, 3, HD, C), (C, C), (FF, C), (FF, C)]
        weight_shapes = [w.shape for w in weights]
    outs = pl.pallas_call(
        functools.partial(layer_kernel, packed, batch),
        out_shape=[
            jax.ShapeDtypeStruct((images_out, TOK, C), low),
            jax.ShapeDtypeStruct((per_device, TOK, C), low),
            *[jax.ShapeDtypeStruct(shape, low) for shape in grad_shapes],
            jax.ShapeDtypeStruct((16, C), wide),
            jax.ShapeDtypeStruct((4, GROUP * PAIR, PAIR), wide),
        ],
        grid_spec=pltpu.PrefetchScalarGridSpec(
            num_scalar_prefetch=1,
            grid=(per_device // batch,),
            in_specs=[
                image_spec, image_spec, whole((ROWS, TOK)), whole((TOK, ROWS)), whole((6, C)), whole((2, C)),
                whole((4, 1, C)), whole((2, 4, GROUP * PAIR, PAIR)), any_spec, any_spec, any_spec, any_spec,
            ],
            out_specs=[out_spec, image_spec]
            + [whole(shape) for shape in grad_shapes]
            + [whole((16, C)), whole((4, GROUP * PAIR, PAIR))],
            scratch_shapes=[pltpu.VMEM(shape, low) for shape in weight_shapes[:1]]
            + [pltpu.VMEM((3, C, C), low)]
            + [pltpu.VMEM(shape, low) for shape in weight_shapes[1:]]
            + [
                pltpu.VMEM((3, C, C), wide),
                pltpu.VMEM((C, C), wide),
                pltpu.VMEM((FF, C), wide),
                pltpu.VMEM((FF, C), wide),
                pltpu.VMEM((12, span, 128), low),
                pltpu.VMEM((4, span, 128), low),
                pltpu.VMEM((12, span, 128), low),
                pltpu.VMEM((batch, 8, GROUP * PAIR, PAIR), wide),
                pltpu.VMEM((span, C), wide),
                pltpu.VMEM((span, C), low),
                pltpu.VMEM((span, C), wide),
                pltpu.VMEM((span, C), wide),
                pltpu.VMEM((span, C), low),
                pltpu.VMEM((span, C), low),
                pltpu.VMEM((span, C), wide),
                pltpu.VMEM((span, C), wide),
                pltpu.SemaphoreType.DMA((4,)),
            ]
            + (exchange if packed else []),
        ),
        compiler_params=params,
        name="window_layer",
    )(place, images, cotangent, order, order_back, vectors, qv_bias, expand_bias.reshape(4, 1, C), bias, *weights)
    grads = outs[2 : 2 + len(grad_shapes)]
    grads = grads[0].reshape(32, 192, C) if packed else [g.reshape(-1, C) for g in grads]
    return outs[0], outs[1], grads, outs[-2], outs[-1]


def pair_bias(pos_bias, window_mask):
    heads = pos_bias.shape[0]
    scores = pos_bias[None] + window_mask[:, None]
    scores = scores.reshape(2, 2, heads, SPAN, SPAN)
    first = jnp.pad(scores[:, 0], ((0, 0), (0, 0), (0, 0), (0, PAIR - SPAN)), constant_values=away)
    second = jnp.pad(scores[:, 1], ((0, 0), (0, 0), (0, 0), (SPAN, PAIR - 2 * SPAN)), constant_values=away)
    rest = jnp.broadcast_to(
        jnp.where(jnp.arange(PAIR) < SPAN, 0.0, away).astype(wide), (2, heads, PAIR - 2 * SPAN, PAIR)
    )
    return jnp.concatenate([first, second, rest], axis=2).reshape(2, heads // GROUP, GROUP * PAIR, PAIR)


MESH = pl.DeviceIdType.MESH
DEPTH = 4


class Place:
    def __init__(self):
        dp_index, mp_index = lax.axis_index("dp"), lax.axis_index("mp")
        self.z, self.x = dp_index // 2, dp_index % 2
        self.y, self.core = mp_index // 2, mp_index % 2
        self.dp_index, self.mp_index = dp_index, mp_index
        self.x_side = self.device(self.z, 1 - self.x, self.y, self.core)
        self.y_side = self.device(self.z, self.x, 1 - self.y, self.core)
        self.partner = self.device(self.z, self.x, self.y, 1 - self.core)
        self.above = self.device(self.z + 1, self.x, self.y, self.core)
        self.below = self.device(self.z - 1, self.x, self.y, self.core)
        self.z_near = self.device(self.z + 1 - 2 * lax.rem(self.z, 2), self.x, self.y, self.core)
        self.z_far = self.device(lax.rem(self.z + 2, DEPTH), self.x, self.y, self.core)

    @staticmethod
    def device(z, x, y, core):
        return {"dp": z * 2 + x, "mp": y * 2 + core}

    @staticmethod
    def owner(z, x, y, core):
        return (y * 2 + core) * 8 + z * 2 + x

    def greet(self):
        barrier = pltpu.get_barrier_semaphore()

        def signal(device):
            pl.semaphore_signal(barrier, inc=1, device_id=device, device_id_type=MESH)

        signal(self.x_side)
        signal(self.y_side)
        signal(self.partner)
        pl.when(self.z > 0)(lambda: signal(self.below))
        pl.when(self.z < DEPTH - 1)(lambda: signal(self.above))
        ends = (self.z == 0).astype(jnp.int32) + (self.z == DEPTH - 1).astype(jnp.int32)
        pl.semaphore_wait(barrier, 5 - ends)


def remote(src, dst, send_sem, recv_sem, device):
    return pltpu.make_async_remote_copy(
        src_ref=src,
        dst_ref=dst,
        send_sem=send_sem,
        recv_sem=recv_sem,
        device_id=device,
        device_id_type=MESH,
    )


def spread(at, own_ref, out_ref, own_sem, z_send, z_recv, side_send, side_recv, pair_send, pair_recv):
    rows = own_ref.shape[0]
    half = rows // 2
    z, x, y, core = at.z, at.x, at.y, at.core
    low, high = pl.ds(0, half), pl.ds(half, rows - half)

    def slot(source_z, other_x, other_y):
        return out_ref.at[
            at.owner(source_z, 1 - x if other_x else x, 1 - y if other_y else y, core)
        ]

    def up(source_z, src=None):
        dst = slot(source_z, False, False)
        return remote(dst if src is None else src, dst, z_send.at[0, source_z], z_recv.at[0, source_z], at.above)

    def down(source_z, src=None):
        dst = slot(source_z, False, False)
        return remote(dst if src is None else src, dst, z_send.at[1, source_z], z_recv.at[1, source_z], at.below)

    def side(kind, source_z, src=None):
        if kind == 0 or kind == 1:
            dst = slot(source_z, False, False)
        elif kind == 2:
            dst = slot(source_z, True, False).at[low]
        else:
            dst = slot(source_z, False, True).at[high]
        device = at.x_side if kind in (0, 3) else at.y_side
        return remote(
            dst if src is None else src, dst, side_send.at[kind, source_z], side_recv.at[kind, source_z], device
        )

    def side_arrival(kind, source_z):
        if kind == 0:
            dst = slot(source_z, True, False)
        elif kind == 1:
            dst = slot(source_z, False, True)
        elif kind == 2:
            dst = slot(source_z, True, True).at[low]
        else:
            dst = slot(source_z, True, True).at[high]
        device = at.x_side if kind in (0, 3) else at.y_side
        return remote(dst, dst, side_send.at[kind, source_z], side_recv.at[kind, source_z], device)

    def pair_region(kind, source_z, of_core):
        other_x, other_y = ((False, False), (True, False), (False, True), (True, True), (True, True))[kind]
        ref = out_ref.at[at.owner(source_z, 1 - x if other_x else x, 1 - y if other_y else y, of_core)]
        if kind == 3:
            ref = ref.at[low]
        elif kind == 4:
            ref = ref.at[high]
        return ref

    def pair(kind, source_z, src=None):
        dst = pair_region(kind, source_z, core)
        return remote(
            dst if src is None else src, dst, pair_send.at[kind, source_z], pair_recv.at[kind, source_z], at.partner
        )

    def pair_arrival(kind, source_z):
        dst = pair_region(kind, source_z, 1 - core)
        return remote(dst, dst, pair_send.at[kind, source_z], pair_recv.at[kind, source_z], at.partner)

    keep = pltpu.make_async_copy(own_ref, slot(z, False, False), own_sem)
    pl.when(z < DEPTH - 1)(lambda: up(z, own_ref).start())
    pl.when(z > 0)(lambda: down(z, own_ref).start())
    side(0, z, own_ref).start()
    side(1, z, own_ref).start()
    pair(0, z, own_ref).start()
    keep.start()

    def plane(source_z):
        side_arrival(0, source_z).wait_recv()
        side(2, source_z).start()
        pair(1, source_z).start()
        side_arrival(1, source_z).wait_recv()
        side(3, source_z).start()
        pair(2, source_z).start()

    def column(source_z):
        side(0, source_z).start()
        side(1, source_z).start()
        pair(0, source_z).start()

    for distance in range(1, DEPTH + 1):

        def from_below(source_z=z - distance):
            up(source_z).wait_recv()
            pl.when(z < DEPTH - 1)(lambda: up(source_z).start())
            column(source_z)

        def from_above(source_z=z + distance):
            down(source_z).wait_recv()
            pl.when(z > 0)(lambda: down(source_z).start())
            column(source_z)

        pl.when(z - distance >= 0)(from_below)
        pl.when(z + distance <= DEPTH - 1)(from_above)
        past = distance - 1
        if past == 0:
            plane(z)
        else:
            pl.when(z - past >= 0)(functools.partial(plane, z - past))
            pl.when(z + past <= DEPTH - 1)(functools.partial(plane, z + past))

    def corner(source_z):
        side_arrival(2, source_z).wait_recv()
        pair(3, source_z).start()
        side_arrival(3, source_z).wait_recv()
        pair(4, source_z).start()

    for distance in range(DEPTH):
        if distance == 0:
            corner(z)
        else:
            pl.when(z - distance >= 0)(functools.partial(corner, z - distance))
            pl.when(z + distance <= DEPTH - 1)(functools.partial(corner, z + distance))
    keep.wait()
    for source_z in range(DEPTH):
        for kind in range(5):
            pair_arrival(kind, source_z).wait_recv()
            pair(kind, source_z).wait_send()
        for kind in range(4):
            side(kind, source_z).wait_send()
        pl.when((z < DEPTH - 1) & (source_z <= z))(lambda: up(source_z).wait_send())
        pl.when((z > 0) & (source_z >= z))(lambda: down(source_z).wait_send())


SPREAD_SEMS = [
    pltpu.SemaphoreType.DMA,
    pltpu.SemaphoreType.DMA((2, DEPTH)),
    pltpu.SemaphoreType.DMA((2, DEPTH)),
    pltpu.SemaphoreType.DMA((4, DEPTH)),
    pltpu.SemaphoreType.DMA((4, DEPTH)),
    pltpu.SemaphoreType.DMA((5, DEPTH)),
    pltpu.SemaphoreType.DMA((5, DEPTH)),
]


def gather_kernel(qkv_ref, proj_ref, expand_ref, contract_ref, misc_ref, out_ref, expand_bias, qv_bias, table,
                  own_ref, misc_out, misc_send, misc_recv, *sems):
    at = Place()
    start = 0
    for weight in (qkv_ref, proj_ref, expand_ref, contract_ref):
        own_ref[pl.ds(start, weight.shape[0])] = weight[...].astype(own_ref.dtype)
        start += weight.shape[0]
    at.greet()
    to_pair = remote(misc_ref, misc_out.at[at.mp_index], misc_send.at[0], misc_recv.at[0], at.partner)
    to_side = remote(misc_ref, misc_out.at[at.mp_index], misc_send.at[1], misc_recv.at[1], at.y_side)
    to_pair.start()
    to_side.start()
    misc_out[at.mp_index] = misc_ref[...]
    over = (1 - at.y) * 2 + at.core
    from_side = remote(misc_ref, misc_out.at[over], misc_send.at[1], misc_recv.at[1], at.y_side)
    relay = remote(misc_out.at[over], misc_out.at[over], misc_send.at[2], misc_recv.at[2], at.partner)
    spread(at, own_ref, out_ref, *sems)
    from_side.wait_recv()
    relay.start()
    beside = at.y * 2 + 1 - at.core
    remote(misc_ref, misc_out.at[beside], misc_send.at[0], misc_recv.at[0], at.partner).wait_recv()
    across = (1 - at.y) * 2 + 1 - at.core
    remote(misc_ref, misc_out.at[across], misc_send.at[2], misc_recv.at[2], at.partner).wait_recv()
    to_pair.wait_send()
    to_side.wait_send()
    relay.wait_send()
    for which in range(4):
        expand_bias[which] = misc_out[which, 0:1]
        for kind in range(2):
            qv_bias[kind : kind + 1, pl.ds(128 * which, 128)] = misc_out[which, 1:2, pl.ds(128 * kind, 128)]
        table[pl.ds(4 * which, 4)] = misc_out[which, 2:6, 0:256]


def gather_all(weights, misc):
    rows, columns = sum(weight.shape[0] for weight in weights), C
    vmem = pl.BlockSpec(memory_space=pltpu.VMEM)
    return pl.pallas_call(
        gather_kernel,
        out_shape=(
            jax.ShapeDtypeStruct((32, rows, columns), low),
            jax.ShapeDtypeStruct((4, 1, columns), wide),
            jax.ShapeDtypeStruct((2, columns), wide),
            jax.ShapeDtypeStruct((HEADS, 256), wide),
        ),
        in_specs=[vmem] * 5,
        out_specs=(pl.BlockSpec(memory_space=pl.ANY), vmem, vmem, vmem),
        scratch_shapes=[
            pltpu.VMEM((rows, columns), low),
            pltpu.VMEM((4,) + misc.shape, wide),
            pltpu.SemaphoreType.DMA((3,)),
            pltpu.SemaphoreType.DMA((3,)),
        ]
        + SPREAD_SEMS,
        compiler_params=pltpu.CompilerParams(collective_id=0, has_side_effects=True),
        name="gather_weights",
    )(*weights, misc)


def collect(at, grads, total_ref, mine, pair_buf, corner_x, corner_y, full_x, full_y, z_up, z_down, z_out,
            load_sem, pair_send, pair_recv, side_send, side_recv, z_send, z_recv):
    rows = total_ref.shape[0]
    half = rows // 2
    z, x, y, core = at.z, at.x, at.y, at.core
    low, high = pl.ds(0, half), pl.ds(half, rows - half)
    orders = ((3, 2, 1, 0), (3, 0, 2, 1), (0, 3, 1, 2), (0, 1, 2, 3))

    def turn(step):
        choice = jnp.int32(orders[3][step])
        for which in range(3):
            choice = jnp.where(z == which, jnp.int32(orders[which][step]), choice)
        return choice

    turns = [turn(step) for step in range(DEPTH)]

    def load(target, y_of):
        return pltpu.make_async_copy(
            grads.at[y_of * 2 + core, target], mine.at[y_of, target], load_sem.at[y_of, target]
        )

    def pair(target, y_of):
        return remote(
            grads.at[y_of * 2 + 1 - core, target], pair_buf.at[y_of, target],
            pair_send.at[y_of, target], pair_recv.at[y_of, target], at.partner,
        )

    def corner(kind, target):
        part = mine.at[1 - y, target, 1 - x]
        if kind == 0:
            return remote(part.at[low], corner_y.at[target], side_send.at[0, target], side_recv.at[0, target], at.y_side)
        return remote(part.at[high], corner_x.at[target], side_send.at[1, target], side_recv.at[1, target], at.x_side)

    def full(kind, target):
        if kind == 2:
            return remote(mine.at[y, target, 1 - x], full_x.at[target], side_send.at[2, target], side_recv.at[2, target], at.x_side)
        return remote(mine.at[1 - y, target, x], full_y.at[target], side_send.at[3, target], side_recv.at[3, target], at.y_side)

    def up(target):
        return remote(z_out.at[target], z_up.at[target], z_send.at[target], z_recv.at[0, target], at.above)

    def down(target):
        return remote(z_out.at[target], z_down.at[target], z_send.at[target], z_recv.at[1, target], at.below)

    wide = jnp.float32
    for target in turns:
        for y_of in (0, 1):
            pair(target, y_of).start()
            load(target, y_of).start()

    def first(target):
        for y_of in (0, 1):
            load(target, y_of).wait()
            pair(target, y_of).wait_recv()

        def add(which, carry):
            y_of, x_of = which // 2, which % 2
            mine[y_of, target, x_of] = (
                mine[y_of, target, x_of].astype(wide) + pair_buf[y_of, target, x_of].astype(wide)
            ).astype(mine.dtype)
            return carry

        lax.fori_loop(0, 4, add, 0)
        corner(0, target).start()
        corner(1, target).start()

    def second(target):
        corner(0, target).wait_recv()
        mine[y, target, 1 - x, low] = (
            mine[y, target, 1 - x, low].astype(wide) + corner_y[target].astype(wide)
        ).astype(mine.dtype)
        full(2, target).start()
        corner(1, target).wait_recv()
        mine[1 - y, target, x, high] = (
            mine[1 - y, target, x, high].astype(wide) + corner_x[target].astype(wide)
        ).astype(mine.dtype)
        full(3, target).start()

    def third(target, last):
        full(2, target).wait_recv()
        full(3, target).wait_recv()
        total_ref[...] = mine[y, target, x].astype(wide) + (
            full_x[target].astype(wide) + full_y[target].astype(wide)
        )

        def add_below():
            up(target).wait_recv()
            total_ref[...] += z_up[target].astype(wide)

        def add_above():
            down(target).wait_recv()
            total_ref[...] += z_down[target].astype(wide)

        pl.when((target >= z) & (z > 0))(add_below)
        pl.when((target <= z) & (z < DEPTH - 1))(add_above)
        if not last:
            z_out[target] = total_ref[...].astype(z_out.dtype)
            pl.when(target > z)(lambda: up(target).start())
            pl.when(target < z)(lambda: down(target).start())

    for step in range(DEPTH + 2):
        if step < DEPTH:
            first(turns[step])
        if 1 <= step <= DEPTH:
            second(turns[step - 1])
        if step >= 2:
            third(turns[step - 2], step - 2 == DEPTH - 1)
    for target in range(DEPTH):
        for y_of in (0, 1):
            pair(target, y_of).wait_send()
        for kind in (0, 1):
            corner(kind, target).wait_send()
        for kind in (2, 3):
            full(kind, target).wait_send()
        pl.when(target != z)(lambda: up(target).wait_send())


def collect_scratch(rows, columns, dtype):
    return [
        pltpu.VMEM((2, DEPTH, 2, rows, columns), dtype),
        pltpu.VMEM((2, DEPTH, 2, rows, columns), dtype),
        pltpu.VMEM((DEPTH, rows // 2, columns), dtype),
        pltpu.VMEM((DEPTH, rows // 2, columns), dtype),
        pltpu.VMEM((DEPTH, rows, columns), dtype),
        pltpu.VMEM((DEPTH, rows, columns), dtype),
        pltpu.VMEM((DEPTH, rows, columns), dtype),
        pltpu.VMEM((DEPTH, rows, columns), dtype),
        pltpu.VMEM((DEPTH, rows, columns), dtype),
        pltpu.SemaphoreType.DMA((2, DEPTH)),
        pltpu.SemaphoreType.DMA((2, DEPTH)),
        pltpu.SemaphoreType.DMA((2, DEPTH)),
        pltpu.SemaphoreType.DMA((4, DEPTH)),
        pltpu.SemaphoreType.DMA((4, DEPTH)),
        pltpu.SemaphoreType.DMA((DEPTH,)),
        pltpu.SemaphoreType.DMA((2, DEPTH)),
    ]


N_COLLECT = 16


def muon_kernel(grads, qkv_ref, proj_ref, expand_ref, contract_ref, grad_out, moment_out, next_all,
                own_next, *scratch):
    at = Place()
    at.greet()
    collect(at, grads, grad_out, *scratch[:N_COLLECT])
    start = 0
    for moment_ref in (qkv_ref, proj_ref, expand_ref, contract_ref):
        rows = pl.ds(start, moment_ref.shape[0])
        grad = grad_out[rows]
        moment = muon_beta * moment_ref[...] + grad
        moment_out[rows] = moment
        own_next[rows] = (grad + muon_beta * moment).astype(own_next.dtype)
        start += moment_ref.shape[0]
    spread(at, own_next, next_all, *scratch[N_COLLECT:])


def muon_exchange(grads, moments):
    rows, columns = sum(moment.shape[0] for moment in moments), C
    shape = jax.ShapeDtypeStruct((rows, columns), jnp.float32)
    vmem = pl.BlockSpec(memory_space=pltpu.VMEM)
    hbm = pl.BlockSpec(memory_space=pl.ANY)
    return pl.pallas_call(
        muon_kernel,
        out_shape=(shape, shape, jax.ShapeDtypeStruct((32, rows, columns), jnp.bfloat16)),
        in_specs=[hbm] + [vmem] * 4,
        out_specs=(vmem, vmem, hbm),
        scratch_shapes=[pltpu.VMEM((rows, columns), jnp.bfloat16)]
        + collect_scratch(rows, columns, jnp.bfloat16)
        + SPREAD_SEMS,
        compiler_params=pltpu.CompilerParams(
            collective_id=1, has_side_effects=True, vmem_limit_bytes=40 * 1024 * 1024
        ),
        name="muon_exchange",
    )(grads.reshape(4, DEPTH, 2, rows, columns), *moments)


def ns_kernel(next_all, own_images, small_ref, swapped, images_all, small_out,
              products, rows_buf, map_buf, small_parts, small_in, sem, keep_sem,
              act_send, act_recv, small_send, small_recv, swap_send, swap_recv):
    at = Place()
    mp_index, dp_index = at.mp_index, at.dp_index
    counts = (48, 16, 64, 64)
    pieces = own_images.shape[0]
    over = (1 - at.y) * 2 + at.core
    across = (1 - at.y) * 2 + 1 - at.core
    beside = at.y * 2 + 1 - at.core
    mp_peers = [{"dp": dp_index, "mp": lax.rem(mp_index + shift, 4)} for shift in (1, 2, 3)]
    small_peers = (at.y_side, at.partner, at.x_side, at.z_near, at.z_far)
    barrier = pltpu.get_barrier_semaphore()
    for device in (*mp_peers, at.x_side, at.z_near, at.z_far):
        pl.semaphore_signal(barrier, inc=1, device_id=device, device_id_type=MESH)

    def fetch(which):
        count = counts[which]
        copy = pltpu.make_async_copy(
            next_all.at[:, pl.ds(sum(counts[:which]), count)], rows_buf.at[:, pl.ds(0, count)], sem
        )
        copy.start()
        if count < 64:
            rows_buf[:, pl.ds(count, 64 - count)] = jnp.zeros((32, 64 - count, C), rows_buf.dtype)
        copy.wait()

    for which in range(4):
        pl.when(mp_index == which)(functools.partial(fetch, which))
    pl.semaphore_wait(barrier, 6)

    def slot(of_mp, image):
        return images_all.at[of_mp * pieces + image]

    def keep_copy(image):
        return pltpu.make_async_copy(own_images.at[image], slot(mp_index, image), keep_sem.at[image])

    def own_copy(which, image):
        device = (at.partner, at.y_side)[which]
        return remote(
            own_images.at[image], slot(mp_index, image), act_send.at[which, image], act_recv.at[which, image], device
        )

    def own_arrival(which, image):
        source, device = ((beside, at.partner), (over, at.y_side))[which]
        return remote(
            own_images.at[image], slot(source, image), act_send.at[which, image], act_recv.at[which, image], device
        )

    def relay(image):
        return remote(slot(over, image), slot(over, image), act_send.at[2, image], act_recv.at[2, image], at.partner)

    def relay_arrival(image):
        return remote(
            slot(across, image), slot(across, image), act_send.at[2, image], act_recv.at[2, image], at.partner
        )

    def small_copy(stage):
        source = small_ref if stage == 0 else small_parts.at[stage - 1]
        return remote(source, small_in.at[stage], small_send.at[stage], small_recv.at[stage], small_peers[stage])

    def small_step(stage):
        small_copy(stage).wait_recv()
        held = small_ref[...] if stage == 0 else small_parts[stage - 1]
        held = held + small_in[stage]
        if stage < 4:
            small_parts[stage] = held
            small_copy(stage + 1).start()
        else:
            small_out[...] = held

    small_copy(0).start()
    for image in range(pieces):
        own_copy(1, image).start()
    for image in range(pieces):
        own_copy(0, image).start()
        keep_copy(image).start()

    gram = None
    for part in range(4):
        block = rows_buf[8 * part : 8 * (part + 1)].reshape(512, C)
        term = dot_tn(block, block)
        gram = term if gram is None else gram + term
    eye = (
        lax.broadcasted_iota(jnp.int32, (C, C), 0) == lax.broadcasted_iota(jnp.int32, (C, C), 1)
    ).astype(wide)
    norm_value = jnp.sqrt(jnp.sum(jnp.sum(gram * eye, axis=1, keepdims=True), axis=0, keepdims=True)) + ns_eps
    gram = gram / (norm_value * norm_value)

    def dot_high(a, b):
        return jnp.dot(a, b, precision=lax.Precision.HIGH, preferred_element_type=wide)

    def pass_on(image):
        own_arrival(1, image).wait_recv()
        relay(image).start()

    total = None
    for iteration in range(NS_ITERS):
        square = dot_high(gram, gram)
        poly = coef_a * eye + (coef_b * gram + coef_c * square)
        total = poly if total is None else dot_high(total, poly)
        if iteration + 1 < NS_ITERS:
            gram = dot_high(dot_high(gram, poly), poly)
        pl.when(at.z >= 0)(functools.partial(small_step, iteration))
    map_buf[...] = total / norm_value

    def swap_copy(which):
        return remote(
            products.at[lax.rem(mp_index + which + 1, 4)], swapped.at[mp_index],
            swap_send.at[which], swap_recv.at[which], mp_peers[which],
        )

    for group in range(4):
        rows = rows_buf[group * 8 + dp_index].astype(wide)
        products[group] = dot_high(rows, map_buf[...]).astype(products.dtype)
    for which in (1, 2, 0):
        swap_copy(which).start()
    swapped[mp_index] = products[mp_index]
    for image in range(pieces):
        pass_on(image)
    for image in range(pieces):
        own_arrival(0, image).wait_recv()
        relay_arrival(image).wait_recv()
        own_copy(0, image).wait_send()
        own_copy(1, image).wait_send()
        relay(image).wait_send()
        keep_copy(image).wait()
    for which in range(3):
        source = lax.rem(mp_index + 3 - which, 4)
        remote(
            products.at[source], swapped.at[source], swap_send.at[which], swap_recv.at[which],
            {"dp": dp_index, "mp": source},
        ).wait_recv()
        swap_copy(which).wait_send()
    for stage in range(5):
        small_copy(stage).wait_send()


def newton_schulz_rows(next_all, own_images, small):
    vmem = pl.BlockSpec(memory_space=pltpu.VMEM)
    hbm = pl.BlockSpec(memory_space=pl.ANY)
    pieces = own_images.shape[0]
    return pl.pallas_call(
        ns_kernel,
        out_shape=(
            jax.ShapeDtypeStruct((4, 64, C), low),
            jax.ShapeDtypeStruct((4 * pieces,) + own_images.shape[1:], low),
            jax.ShapeDtypeStruct(small.shape, wide),
        ),
        in_specs=[hbm, vmem, vmem],
        out_specs=(vmem, hbm, vmem),
        scratch_shapes=[
            pltpu.VMEM((4, 64, C), low),
            pltpu.VMEM((32, 64, C), low),
            pltpu.VMEM((C, C), wide),
            pltpu.VMEM((4,) + small.shape, wide),
            pltpu.VMEM((5,) + small.shape, wide),
            pltpu.SemaphoreType.DMA,
            pltpu.SemaphoreType.DMA((pieces,)),
            pltpu.SemaphoreType.DMA((3, pieces)),
            pltpu.SemaphoreType.DMA((3, pieces)),
            pltpu.SemaphoreType.DMA((5,)),
            pltpu.SemaphoreType.DMA((5,)),
            pltpu.SemaphoreType.DMA((3,)),
            pltpu.SemaphoreType.DMA((3,)),
        ],
        compiler_params=pltpu.CompilerParams(
            collective_id=2, has_side_effects=True, vmem_limit_bytes=40 * 1024 * 1024
        ),
        name="newton_schulz",
    )(next_all, own_images, small)


def update_kernel(grads, moments, swapped, *refs):
    weights, outs = refs[:4], refs[4:]
    factors = (math.sqrt(3.0), 1.0, math.sqrt(max(1.0, FF / C)), 1.0)
    start = 0
    for which in range(4):
        count = weights[which].shape[0]
        rows = pl.ds(start, count)
        outs[which][...] = grads[rows]
        outs[4 + which][...] = moments[rows]
        part = swapped[which, pl.ds(0, count)].astype(wide)
        outs[8 + which][...] = -muon_rate * (muon_decay * weights[which][...] + factors[which] * part)
        start += count


def update_shards(grads, moments, swapped, weights):
    vmem = pl.BlockSpec(memory_space=pltpu.VMEM)
    shapes = [jax.ShapeDtypeStruct(weight.shape, wide) for weight in weights] * 3
    return pl.pallas_call(
        update_kernel,
        out_shape=shapes,
        in_specs=[vmem] * 7,
        out_specs=[vmem] * 12,
        name="update_shards",
    )(grads, moments, swapped, *weights)


def split_low(values):
    high = lax.reduce_precision(values, exponent_bits=8, mantissa_bits=7)
    return high.astype(jnp.bfloat16), (values - high).astype(jnp.bfloat16)


def dot_three(left, right):
    left_high, left_rest = left
    right_high, right_rest = right
    wide = dict(preferred_element_type=jnp.float32)
    return (
        jnp.dot(left_rest, right_high, **wide)
        + jnp.dot(left_high, right_rest, **wide)
        + jnp.dot(left_high, right_high, **wide)
    )


def newton_schulz(gram):
    width = gram.shape[0]
    eye = jnp.eye(width, dtype=jnp.float32)
    norm_value = jnp.sqrt(jnp.sum(gram * eye)) + ns_eps
    gram = gram / (norm_value * norm_value)
    total = None
    for iteration in range(NS_ITERS):
        parts = split_low(gram)
        square = dot_three(parts, parts)
        poly = coef_a * eye + (coef_b * gram + coef_c * square)
        poly_parts = split_low(poly)
        total = poly if total is None else dot_three(split_low(total), poly_parts)
        if iteration + 1 < NS_ITERS:
            half = dot_three(parts, poly_parts)
            gram = dot_three(split_low(half), poly_parts)
    return total / norm_value


def adam_update(grad_sum, first_moment, second_moment):
    first_new = adam_one * first_moment + (1.0 - adam_one) * grad_sum
    second_new = adam_two * second_moment + (1.0 - adam_two) * grad_sum * grad_sum
    first_hat = first_new / (1.0 - adam_one**adam_step)
    second_hat = second_new / (1.0 - adam_two**adam_step)
    return (-adam_rate * first_hat / (jnp.sqrt(second_hat) + adam_eps), first_new, second_new)


def exchange_plain(own_low, own_moments, rows):
    everyone = ("mp", "dp")
    starts = [sum(rows[:which]) for which in range(4)]

    def cut(stacked):
        return [stacked[:, start : start + count] for start, count in zip(starts, rows)]

    gathered = [
        part.reshape(-1, C) for part in cut(lax.all_gather(own_low, everyone, axis=0, tiled=False))
    ]

    def finish(big_local):
        mp_size, dp_size = lax.axis_size("mp"), lax.axis_size("dp")
        mp_index, dp_index = lax.axis_index("mp"), lax.axis_index("dp")
        devices = mp_size * dp_size
        stacked_grads = jnp.concatenate(
            [grad.reshape(devices, count, C) for grad, count in zip(big_local, rows)], axis=1
        )
        own_grads = lax.psum_scatter(
            stacked_grads.reshape(devices * sum(rows), C), everyone, scatter_dimension=0, tiled=True
        ).astype(wide)
        own_buffers = muon_beta * own_moments + own_grads
        own_nesterov = own_grads + muon_beta * own_buffers
        iterate_all = lax.all_gather(own_nesterov.astype(low), everyone, axis=0, tiled=False)
        grams = jnp.stack([dot_tn(part.reshape(-1, C), part.reshape(-1, C)) for part in cut(iterate_all)])
        ortho_map = newton_schulz(lax.dynamic_index_in_dim(grams, mp_index, 0, keepdims=False))
        most = max(rows)
        picked = lax.dynamic_slice(
            iterate_all.reshape(mp_size, dp_size, sum(rows), C),
            (
                jnp.int32(0),
                dp_index.astype(jnp.int32),
                jnp.array(starts, jnp.int32)[mp_index],
                jnp.int32(0),
            ),
            (mp_size, 1, most, C),
        ).reshape(mp_size * most, C)
        map_parts = split_low(ortho_map)
        products = dot(picked, map_parts[0]) + dot(picked, map_parts[1])
        swapped = lax.all_to_all(products.reshape(mp_size, most, C), "mp", 0, 0, tiled=False)
        return own_grads, own_buffers, swapped

    return gathered, finish


def shards(
    images,
    cotangent,
    qkv_weight,
    proj_weight,
    expand_weight,
    contract_weight,
    qkv_moment,
    proj_moment,
    expand_moment,
    contract_moment,
    vectors,
    qv_bias,
    expand_bias,
    rel_table,
    vectors_first,
    vectors_second,
    qv_first,
    qv_second,
    expand_bias_first,
    expand_bias_second,
    table_first,
    table_second,
    region_ids,
    pos_index,
    image_counts,
):
    everyone = ("mp", "dp")
    mp_size, dp_size = lax.axis_size("mp"), lax.axis_size("dp")
    mp_index = lax.axis_index("mp")
    linked = mp_size == 4 and dp_size == 8
    per_device = IMG_DEV // mp_size
    first_image = (mp_index * per_device).astype(jnp.int32)
    place = jnp.stack([first_image, image_counts[0]])
    own_images = lax.dynamic_slice_in_dim(images, first_image, per_device, 0)
    own_cotangent = lax.dynamic_slice_in_dim(cotangent, first_image, per_device, 0)
    weights_all = (qkv_weight, proj_weight, expand_weight, contract_weight)
    rows = [weight.shape[0] for weight in weights_all]
    starts = [sum(rows[:which]) for which in range(4)]
    moments = (qkv_moment, proj_moment, expand_moment, contract_moment)
    if linked:
        misc = jnp.concatenate(
            [
                expand_bias[None],
                jnp.pad(qv_bias.reshape(1, -1), ((0, 0), (0, C - qv_bias.size))),
                jnp.pad(rel_table.T, ((0, 2), (0, C - TABLE))),
            ],
            axis=0,
        )
        gathered, expand_full, qv_full, table_wide = gather_all(weights_all, misc)
        table_full = table_wide[:, :TABLE]
    else:
        own_low = jnp.concatenate([weight.astype(low) for weight in weights_all], axis=0)
        own_moments = jnp.concatenate(moments, axis=0)
        gathered, finish_plain = exchange_plain(own_low, own_moments, rows)
        qv_full = lax.all_gather(qv_bias, "mp", axis=1, tiled=True)
        expand_full = lax.all_gather(expand_bias, "mp", axis=0, tiled=True).reshape(4, C)
        table_full = lax.all_gather(rel_table.T, "mp", axis=0, tiled=True)
    onehot = (
        jnp.arange(TABLE, dtype=jnp.int32)[:, None] == pos_index.reshape(1, SPAN * SPAN)
    ).astype(wide)
    pos_bias = jnp.dot(table_full, onehot, precision=highest).reshape(HEADS, SPAN, SPAN)
    window_regions = to_windows(region_ids.reshape(1, TOK, 1))[:, :, 0]
    window_mask = jnp.where(
        window_regions[:, :, None] != window_regions[:, None, :], mask_value, 0.0
    ).astype(wide)
    bias = pair_bias(pos_bias, window_mask)
    block_low, input_low, big_local, small_rows, table_pairs = run_layer(
        linked, per_device, place, own_images, own_cotangent, vectors, qv_full, expand_full, bias, gathered
    )
    if linked:
        block_out = block_low
    else:
        block_out = lax.all_gather(block_low, "mp", axis=0, tiled=True)
        input_grad = lax.all_gather(input_low, "mp", axis=0, tiled=True)
    pairs = table_pairs.reshape(HEADS, PAIR, PAIR)
    bias_heads = pairs[:, :SPAN, :SPAN] + pairs[:, SPAN : 2 * SPAN, SPAN : 2 * SPAN]
    table_local = lax.dot_general(
        bias_heads.reshape(HEADS, SPAN * SPAN),
        onehot,
        (((1,), (1,)), ((), ())),
        precision=highest,
        preferred_element_type=wide,
    )
    if linked:
        small_own = jnp.concatenate(
            [small_rows, jnp.pad(table_local, ((0, 0), (0, C - TABLE)))], axis=0
        )
        own_grads, own_buffers, next_all = muon_exchange(big_local, moments)
        swapped, input_grad, small_all = newton_schulz_rows(next_all, input_low, small_own)
        small_full, table_all = small_all[:HEADS], small_all[HEADS:, :TABLE]
    else:
        small_full, table_all = lax.psum((small_rows, table_local), everyone)
        own_grads, own_buffers, swapped = finish_plain(big_local)
    updated = update_shards(own_grads, own_buffers, swapped, weights_all)
    shares, buffers, new_steps = updated[:4], updated[4:8], updated[8:]

    def own_columns(full, width):
        return lax.dynamic_slice_in_dim(full, mp_index * width, width, full.ndim - 1)

    small_sums = (
        small_full[:6],
        own_columns(small_full[6:8], qv_bias.shape[1]),
        own_columns(small_full[8:12].reshape(FF), expand_bias.shape[0]),
        lax.dynamic_slice_in_dim(table_all, mp_index * rel_table.shape[1], rel_table.shape[1], 0).T,
    )
    vectors_step, vectors_first_new, vectors_second_new = adam_update(
        small_sums[0], vectors_first, vectors_second
    )
    qv_step, qv_first_new, qv_second_new = adam_update(small_sums[1], qv_first, qv_second)
    expand_bias_step, expand_bias_first_new, expand_bias_second_new = adam_update(
        small_sums[2], expand_bias_first, expand_bias_second
    )
    table_step, table_first_new, table_second_new = adam_update(
        small_sums[3], table_first, table_second
    )
    return (
        block_out,
        input_grad,
        shares[0],
        shares[1],
        shares[2],
        shares[3],
        small_sums[0],
        small_sums[1],
        small_sums[2],
        small_sums[3],
        new_steps[0],
        new_steps[1],
        new_steps[2],
        new_steps[3],
        buffers[0],
        buffers[1],
        buffers[2],
        buffers[3],
        vectors_step,
        qv_step,
        expand_bias_step,
        table_step,
        vectors_first_new,
        vectors_second_new,
        qv_first_new,
        qv_second_new,
        expand_bias_first_new,
        expand_bias_second_new,
        table_first_new,
        table_second_new,
    )


def solution(mesh):
    return jax.shard_map(
        shards,
        mesh=mesh,
        in_specs=(
            P("dp", None, None),
            P("dp", None, None),
            P(("mp", "dp"), None),
            P(("mp", "dp"), None),
            P(("mp", "dp"), None),
            P(("mp", "dp"), None),
            P(("mp", "dp"), None),
            P(("mp", "dp"), None),
            P(("mp", "dp"), None),
            P(("mp", "dp"), None),
            P(),
            P(None, "mp"),
            P("mp"),
            P(None, "mp"),
            P(),
            P(),
            P(None, "mp"),
            P(None, "mp"),
            P("mp"),
            P("mp"),
            P(None, "mp"),
            P(None, "mp"),
            P(),
            P(),
            P("dp"),
        ),
        out_specs=(
            P("dp", None, None),
            P("dp", None, None),
            P(("mp", "dp"), None),
            P(("mp", "dp"), None),
            P(("mp", "dp"), None),
            P(("mp", "dp"), None),
            P(),
            P(None, "mp"),
            P("mp"),
            P(None, "mp"),
            P(("mp", "dp"), None),
            P(("mp", "dp"), None),
            P(("mp", "dp"), None),
            P(("mp", "dp"), None),
            P(("mp", "dp"), None),
            P(("mp", "dp"), None),
            P(("mp", "dp"), None),
            P(("mp", "dp"), None),
            P(),
            P(None, "mp"),
            P("mp"),
            P(None, "mp"),
            P(),
            P(),
            P(None, "mp"),
            P(None, "mp"),
            P("mp"),
            P("mp"),
            P(None, "mp"),
            P(None, "mp"),
        ),
        check_vma=False,
    )
```

```python
import functools
import math

import jax
import jax.numpy as jnp
import numpy as np
from jax import lax
from jax.experimental import pallas as pl
from jax.experimental.pallas import tpu as pltpu
from jax.sharding import PartitionSpec as P

C = 512
HEADS = 16
HD = 32
FF = 2048
WIN = 7
SIDE = 14
SHIFT = 3
SPAN = WIN * WIN
TOK = SIDE * SIDE
NS_ITERS = 5
IMG_DEV = 16
TABLE = 169
PAIR = 112
ROWS = 2 * PAIR
GROUP = 4

norm_eps = 1e-05
ns_eps = 1e-07
coef_a = 3.4445
coef_b = -4.775
coef_c = 2.0315
muon_rate = 0.3
muon_decay = 0.1
muon_beta = 0.95
adam_rate = 0.1
adam_one = 0.9
adam_two = 0.999
adam_eps = 1e-08
adam_step = 4
mask_value = -100.0
away = -1e30
wide = jnp.float32
low = jnp.bfloat16
highest = lax.Precision.HIGHEST


def to_windows(field_values):
    image_total = field_values.shape[0]
    channels = field_values.shape[-1]
    blocks = SIDE // WIN
    grid_values = field_values.reshape(image_total, SIDE, SIDE, channels)
    grid_values = jnp.roll(grid_values, (-SHIFT, -SHIFT), axis=(1, 2))
    grid_values = grid_values.reshape(image_total, blocks, WIN, blocks, WIN, channels)
    grid_values = grid_values.transpose(0, 1, 3, 2, 4, 5)
    return grid_values.reshape(image_total * blocks * blocks, WIN * WIN, channels)


def window_order():
    order = np.full((ROWS,), -1, np.int64)
    for window in range(4):
        top, left = window // 2, window % 2
        for token in range(SPAN):
            row = (top * WIN + token // WIN + SHIFT) % SIDE
            column = (left * WIN + token % WIN + SHIFT) % SIDE
            order[(window // 2) * PAIR + (window % 2) * SPAN + token] = row * SIDE + column
    return order


def dot(a, b):
    return jnp.dot(a, b, preferred_element_type=wide)


def dot_nt(a, b):
    return lax.dot_general(a, b, (((1,), (1,)), ((), ())), preferred_element_type=wide)


def dot_tn(a, b):
    return lax.dot_general(a, b, (((0,), (0,)), ((), ())), preferred_element_type=wide)


def mean_of(values):
    return jnp.sum(values, axis=-1, keepdims=True) * (1.0 / C)


def normalize(values):
    centered = values - mean_of(values)
    inv_scale = lax.rsqrt(mean_of(centered * centered) + norm_eps)
    return centered * inv_scale, inv_scale


def normalize_back(grad_norm, normed, inv_scale, gain):
    scaled = grad_norm * gain
    return inv_scale * (scaled - mean_of(scaled) - normed * mean_of(scaled * normed))


def column_sum(values):
    return jnp.sum(values, axis=0, keepdims=True)


def head_masks():
    lane = lax.broadcasted_iota(jnp.int32, (1, 128), 1) // HD
    return [(lane == head).astype(wide).astype(low) for head in range(GROUP)]


def stack_heads(block, masks):
    return jnp.concatenate([block * mask for mask in masks], axis=0)


def pick_heads(stacked):
    lane = lax.broadcasted_iota(jnp.int32, (PAIR, 128), 1)
    parts = [stacked[PAIR * head : PAIR * (head + 1)] for head in range(GROUP)]
    return jnp.where(
        lane < 2 * HD,
        jnp.where(lane < HD, parts[0], parts[1]),
        jnp.where(lane < 3 * HD, parts[2], parts[3]),
    )


def layer_kernel(
    packed, batch, place, images, cotangent, order, order_back, vectors, qv_bias, expand_bias, bias,
    qkv_hbm, proj_hbm, expand_hbm, contract_hbm,
    block_out, input_grad, *rest,
):
    n_grads = 1 if packed else 4
    grad_outs = rest[:n_grads]
    (small, table_sum, qkv_nat, qkv_w, proj_w, expand_w, contract_w,
     qkv_acc, proj_acc, expand_acc, contract_acc,
     qkv_s, att_s, back_s, probs_s, normed_s, first_s, middle_s, normed2_s, second_s,
     out_low_s, mlp_s, second_grad_s, sems) = rest[n_grads : n_grads + 24]
    step = pl.program_id(0)
    steps = pl.num_programs(0)
    masks = head_masks()
    if packed:
        staged, keep_sem, act_send, act_recv = rest[n_grads + 24 :]
        at = Place()
        per_device = staged.shape[0]
        over = (1 - at.y) * 2 + at.core
        across = (1 - at.y) * 2 + 1 - at.core
        beside = at.y * 2 + 1 - at.core

        def slot(mp_index, image):
            return block_out.at[mp_index * per_device + image]

        def keep_copy(image):
            return pltpu.make_async_copy(staged.at[image], slot(at.mp_index, image), keep_sem.at[image])

        def own_copy(which, image):
            device = (at.partner, at.y_side)[which]
            return remote(
                staged.at[image], slot(at.mp_index, image),
                act_send.at[which, image], act_recv.at[which, image], device,
            )

        def own_arrival(which, image):
            source, device = ((beside, at.partner), (over, at.y_side))[which]
            return remote(
                staged.at[image], slot(source, image),
                act_send.at[which, image], act_recv.at[which, image], device,
            )

        def relay(image):
            return remote(
                slot(over, image), slot(over, image), act_send.at[2, image], act_recv.at[2, image], at.partner
            )

        def relay_arrival(image):
            return remote(
                slot(across, image), slot(across, image), act_send.at[2, image], act_recv.at[2, image], at.partner
            )

        def pass_on(of_step):
            for slice_ in range(batch):
                image = of_step * batch + slice_
                own_arrival(1, image).wait_recv()
                relay(image).start()

        def greet():
            barrier = pltpu.get_barrier_semaphore()
            for device in (at.partner, at.y_side):
                pl.semaphore_signal(barrier, inc=1, device_id=device, device_id_type=MESH)
            pl.semaphore_wait(barrier, 2)

        pl.when(step == 0)(greet)

    def put_block(slice_, value):
        if packed:
            image = step * batch + slice_
            staged[image] = value
            own_copy(1, image).start()
            own_copy(0, image).start()
            keep_copy(image).start()
        else:
            block_out[slice_] = value

    def put_grad(slice_, value):
        input_grad[slice_] = value

    row = lax.broadcasted_iota(jnp.int32, (batch * ROWS, 1), 0) // ROWS
    live_scale = jnp.zeros((batch * ROWS, 1), wide)
    for slice_ in range(batch):
        is_live = (place[1] > place[0] + step * batch + slice_).astype(wide)
        live_scale = jnp.where(row == slice_, is_live, live_scale)

    def fetch(which):
        if packed:
            counts = (48, 16, 64, 64)
            source = qkv_hbm.at[:, pl.ds(sum(counts[:which]), counts[which])]
            target = (qkv_nat, proj_w, expand_w, contract_w)[which]
        else:
            source = (qkv_hbm, proj_hbm, expand_hbm, contract_hbm)[which]
            target = (qkv_nat, proj_w, expand_w, contract_w)[which]
        return pltpu.make_async_copy(source, target, sems.at[which])

    def rows_of(ref, count):
        return ref[...].reshape(count, C)

    def begin():
        for which in range(4):
            fetch(which).start()
        for ref in (qkv_acc, proj_acc, expand_acc, contract_acc, small, table_sum):
            ref[...] = jnp.zeros_like(ref)
        for which in range(4):
            fetch(which).wait()
        natural = rows_of(qkv_nat, 3 * C).reshape(HEADS, 3, HD, C)
        for kind in range(3):
            qkv_w[kind] = natural[:, kind].reshape(C, C)

    pl.when(step == 0)(begin)

    tokens = jnp.concatenate([dot(order[...], images[slice_]) for slice_ in range(batch)], axis=0)
    normed, inv_one = normalize(tokens)
    normed_s[...] = normed
    first_in = (normed * vectors[0:1] + vectors[1:2]).astype(low)
    first_s[...] = first_in
    for kind in range(3):
        projected = dot_nt(first_in, qkv_w[kind])
        if kind != 1:
            projected = projected + qv_bias[kind // 2 : kind // 2 + 1]
        projected = projected.astype(low)
        for group in range(4):
            qkv_s[kind * 4 + group] = projected[:, 128 * group : 128 * (group + 1)]
    score_scale = 1.0 / math.sqrt(HD)

    def attend(which, carry):
        pair, group = which // 4, which % 4
        pair_scores = bias[pair, group]
        for slice_ in range(batch):
            rows = pl.ds(pl.multiple_of(slice_ * ROWS + pair * PAIR, 16), PAIR)
            queries = stack_heads(qkv_s[group, rows], masks)
            scores = dot_nt(queries, qkv_s[4 + group, rows]) * score_scale + pair_scores
            top = jnp.max(scores, axis=-1, keepdims=True)
            exponent = jnp.exp(scores - top)
            attention = exponent / jnp.sum(exponent, axis=-1, keepdims=True)
            probs_s[slice_, which] = attention
            att_s[group, rows] = pick_heads(dot(attention.astype(low), qkv_s[8 + group, rows])).astype(low)
        return carry

    lax.fori_loop(0, 8, attend, 0)
    attended = jnp.concatenate([att_s[group] for group in range(4)], axis=1)
    middle = tokens + (dot(attended, rows_of(proj_w, C)) + vectors[4:5])
    middle_s[...] = middle
    normed_two, inv_two = normalize(middle)
    normed2_s[...] = normed_two
    second_in = (normed_two * vectors[2:3] + vectors[3:4]).astype(low)
    second_s[...] = second_in

    grad_tokens = jnp.concatenate([dot(order[...], cotangent[slice_]) for slice_ in range(batch)], axis=0)
    out_low = (grad_tokens * live_scale).astype(low)
    out_low_s[...] = out_low
    mlp_s[...] = jnp.zeros_like(mlp_s)
    second_grad_s[...] = jnp.zeros_like(second_grad_s)
    chunk = 512
    owners = expand_w.shape[0] // (FF // chunk)

    def feed(which, carry):
        units = pl.ds(pl.multiple_of(which * owners, owners), owners)
        expand_part = expand_w[units].reshape(chunk, C)
        contract_part = contract_w[units].reshape(chunk, C)
        second = second_s[...]
        grad_rows = out_low_s[...]
        hidden = dot_nt(second, expand_part) + expand_bias[which]
        cumulative = 0.5 * (1.0 + lax.erf(hidden * (1.0 / math.sqrt(2.0))))
        acted = (hidden * cumulative).astype(low)
        slope = cumulative + hidden * jnp.exp(-0.5 * hidden * hidden) * (1.0 / math.sqrt(2.0 * math.pi))
        mlp_s[...] += dot(acted, contract_part)
        hidden_grad32 = dot_nt(grad_rows, contract_part) * slope
        hidden_grad = hidden_grad32.astype(low)
        small[pl.ds(8 + which, 1)] += column_sum(hidden_grad.astype(wide))
        second_grad_s[...] += dot(hidden_grad, expand_part)
        units_wide = pl.ds(pl.multiple_of(which * chunk, chunk), chunk)
        contract_acc[units_wide] += dot_tn(acted, grad_rows)
        expand_acc[units_wide] += dot_tn(hidden_grad, second)
        return carry

    lax.fori_loop(0, FF // chunk, feed, 0)
    result = middle_s[...] + (mlp_s[...] + vectors[5:6])
    result = jnp.where(live_scale > 0.0, result, 0.0).astype(low)
    if packed:
        pl.when(step > 0)(lambda: pass_on(step - 1))
    for slice_ in range(batch):
        put_block(slice_, dot(order_back[...], result[ROWS * slice_ : ROWS * (slice_ + 1)]).astype(low))

    grad_out = out_low_s[...].astype(wide)
    second_grad = second_grad_s[...]
    normed_two = normed2_s[...]
    small[5:6] += column_sum(grad_out)
    small[3:4] += column_sum(second_grad)
    small[2:3] += column_sum(second_grad * normed_two)
    middle_grad = grad_out + normalize_back(second_grad, normed_two, inv_two, vectors[2:3])
    small[4:5] += column_sum(middle_grad)
    middle_s[...] = middle_grad
    attn_low = middle_grad.astype(low)
    attended = jnp.concatenate([att_s[group] for group in range(4)], axis=1)
    proj_acc[...] += dot_tn(attended, attn_low)
    attended_grad = dot_nt(attn_low, rows_of(proj_w, C)).astype(low)
    for group in range(4):
        att_s[group] = attended_grad[:, 128 * group : 128 * (group + 1)]

    def attend_back(which, carry):
        pair, group = which // 4, which % 4
        bias_grad = None
        for slice_ in range(batch):
            rows = pl.ds(pl.multiple_of(slice_ * ROWS + pair * PAIR, 16), PAIR)
            attention = probs_s[slice_, which]
            keys, values = qkv_s[4 + group, rows], qkv_s[8 + group, rows]
            grads = stack_heads(att_s[group, rows], masks)
            queries = stack_heads(qkv_s[group, rows], masks)
            probs_grad = dot_nt(grads, values)
            row_term = jnp.sum(attention * probs_grad, axis=-1, keepdims=True)
            score_grad = (attention * (probs_grad - row_term)).astype(low)
            wide_grad = score_grad.astype(wide)
            bias_grad = wide_grad if bias_grad is None else bias_grad + wide_grad
            back_s[group, rows] = (pick_heads(dot(score_grad, keys)) * score_scale).astype(low)
            back_s[4 + group, rows] = (dot_tn(score_grad, queries) * score_scale).astype(low)
            back_s[8 + group, rows] = dot_tn(attention.astype(low), grads).astype(low)
        table_sum[group] += bias_grad
        return carry

    lax.fori_loop(0, 8, attend_back, 0)
    first_in = first_s[...]
    first_grad = None
    for kind in range(3):
        back = jnp.concatenate([back_s[kind * 4 + group] for group in range(4)], axis=1)
        if kind != 1:
            row = 6 + kind // 2
            small[row : row + 1] += column_sum(back.astype(wide))
        qkv_acc[kind] += dot_tn(back, first_in)
        part = dot(back, qkv_w[kind])
        first_grad = part if first_grad is None else first_grad + part
    normed = normed_s[...]
    small[1:2] += column_sum(first_grad)
    small[0:1] += column_sum(first_grad * normed)
    token_grad = middle_s[...] + normalize_back(first_grad, normed, inv_one, vectors[0:1])
    token_low = token_grad.astype(low)
    for slice_ in range(batch):
        put_grad(slice_, dot(order_back[...], token_low[ROWS * slice_ : ROWS * (slice_ + 1)]).astype(low))

    def finish():
        if packed:
            pass_on(steps - 1)
        for kind in range(3):
            part = qkv_acc[kind].astype(low).reshape(HEADS, HD, C)
            if packed:
                out = grad_outs[0]
                for piece in range(2):
                    block = kind * 2 + piece
                    out[:, block // 3, pl.ds(16 * (block % 3), 16)] = part[:, 16 * piece : 16 * (piece + 1)]
            else:
                grad_outs[0][:, kind] = part
        if packed:
            out = grad_outs[0]
            out[:, :, pl.ds(48, 16)] = proj_acc[...].astype(low).reshape(16, 2, 16, C)
            out[:, :, pl.ds(64, 64)] = expand_acc[...].astype(low).reshape(16, 2, 64, C)
            out[:, :, pl.ds(128, 64)] = contract_acc[...].astype(low).reshape(16, 2, 64, C)
        else:
            grad_outs[1][...] = proj_acc[...].astype(low)
            grad_outs[2][...] = expand_acc[...].astype(low)
            grad_outs[3][...] = contract_acc[...].astype(low)
        if packed:

            def settle(image, carry):
                own_arrival(0, image).wait_recv()
                relay_arrival(image).wait_recv()
                own_copy(0, image).wait_send()
                own_copy(1, image).wait_send()
                relay(image).wait_send()
                keep_copy(image).wait()
                return carry

            lax.fori_loop(0, per_device, settle, 0)

    pl.when(step == steps - 1)(finish)


def run_layer(packed, per_device, place, images, cotangent, vectors, qv_bias, expand_bias, bias, weights):
    order_np = window_order()
    onehot = (order_np[:, None] == np.arange(TOK)[None, :]).astype(np.float32)
    order = jnp.asarray(onehot, low)
    order_back = jnp.asarray(onehot.T, low)
    any_spec = pl.BlockSpec(memory_space=pl.ANY)

    def whole(shape):
        return pl.BlockSpec(shape, lambda i, s: (0,) * len(shape), pipeline_mode=pl.Buffered(1))

    batch = 2 if per_device % 2 == 0 else 1
    span = batch * ROWS
    image_spec = pl.BlockSpec((batch, TOK, C), lambda i, s: (i, 0, 0))
    out_spec = any_spec if packed else image_spec
    images_out = IMG_DEV if packed else per_device
    exchange = [
        pltpu.VMEM((per_device, TOK, C), low),
        pltpu.SemaphoreType.DMA((per_device,)),
        pltpu.SemaphoreType.DMA((3, per_device)),
        pltpu.SemaphoreType.DMA((3, per_device)),
    ]
    limit = 60 * 1024 * 1024
    if packed:
        params = pltpu.CompilerParams(collective_id=3, has_side_effects=True, vmem_limit_bytes=limit)
    else:
        params = pltpu.CompilerParams(vmem_limit_bytes=limit)
    if packed:
        weights = (weights,) * 4
        grad_shapes = [(16, 2, 192, C)]
        weight_shapes = [(32, 48, C), (32, 16, C), (32, 64, C), (32, 64, C)]
    else:
        weights = (weights[0], weights[1], weights[2].reshape(FF // 64, 64, C), weights[3].reshape(FF // 64, 64, C))
        grad_shapes = [(HEADS, 3, HD, C), (C, C), (FF, C), (FF, C)]
        weight_shapes = [w.shape for w in weights]
    outs = pl.pallas_call(
        functools.partial(layer_kernel, packed, batch),
        out_shape=[
            jax.ShapeDtypeStruct((images_out, TOK, C), low),
            jax.ShapeDtypeStruct((per_device, TOK, C), low),
            *[jax.ShapeDtypeStruct(shape, low) for shape in grad_shapes],
            jax.ShapeDtypeStruct((16, C), wide),
            jax.ShapeDtypeStruct((4, GROUP * PAIR, PAIR), wide),
        ],
        grid_spec=pltpu.PrefetchScalarGridSpec(
            num_scalar_prefetch=1,
            grid=(per_device // batch,),
            in_specs=[
                image_spec, image_spec, whole((ROWS, TOK)), whole((TOK, ROWS)), whole((6, C)), whole((2, C)),
                whole((4, 1, C)), whole((2, 4, GROUP * PAIR, PAIR)), any_spec, any_spec, any_spec, any_spec,
            ],
            out_specs=[out_spec, image_spec]
            + [whole(shape) for shape in grad_shapes]
            + [whole((16, C)), whole((4, GROUP * PAIR, PAIR))],
            scratch_shapes=[pltpu.VMEM(shape, low) for shape in weight_shapes[:1]]
            + [pltpu.VMEM((3, C, C), low)]
            + [pltpu.VMEM(shape, low) for shape in weight_shapes[1:]]
            + [
                pltpu.VMEM((3, C, C), wide),
                pltpu.VMEM((C, C), wide),
                pltpu.VMEM((FF, C), wide),
                pltpu.VMEM((FF, C), wide),
                pltpu.VMEM((12, span, 128), low),
                pltpu.VMEM((4, span, 128), low),
                pltpu.VMEM((12, span, 128), low),
                pltpu.VMEM((batch, 8, GROUP * PAIR, PAIR), wide),
                pltpu.VMEM((span, C), wide),
                pltpu.VMEM((span, C), low),
                pltpu.VMEM((span, C), wide),
                pltpu.VMEM((span, C), wide),
                pltpu.VMEM((span, C), low),
                pltpu.VMEM((span, C), low),
                pltpu.VMEM((span, C), wide),
                pltpu.VMEM((span, C), wide),
                pltpu.SemaphoreType.DMA((4,)),
            ]
            + (exchange if packed else []),
        ),
        compiler_params=params,
        name="window_layer",
    )(place, images, cotangent, order, order_back, vectors, qv_bias, expand_bias.reshape(4, 1, C), bias, *weights)
    grads = outs[2 : 2 + len(grad_shapes)]
    grads = grads[0].reshape(32, 192, C) if packed else [g.reshape(-1, C) for g in grads]
    return outs[0], outs[1], grads, outs[-2], outs[-1]


def pair_bias(pos_bias, window_mask):
    heads = pos_bias.shape[0]
    scores = pos_bias[None] + window_mask[:, None]
    scores = scores.reshape(2, 2, heads, SPAN, SPAN)
    first = jnp.pad(scores[:, 0], ((0, 0), (0, 0), (0, 0), (0, PAIR - SPAN)), constant_values=away)
    second = jnp.pad(scores[:, 1], ((0, 0), (0, 0), (0, 0), (SPAN, PAIR - 2 * SPAN)), constant_values=away)
    rest = jnp.broadcast_to(
        jnp.where(jnp.arange(PAIR) < SPAN, 0.0, away).astype(wide), (2, heads, PAIR - 2 * SPAN, PAIR)
    )
    return jnp.concatenate([first, second, rest], axis=2).reshape(2, heads // GROUP, GROUP * PAIR, PAIR)


MESH = pl.DeviceIdType.MESH
DEPTH = 4


class Place:
    def __init__(self):
        dp_index, mp_index = lax.axis_index("dp"), lax.axis_index("mp")
        self.z, self.x = dp_index // 2, dp_index % 2
        self.y, self.core = mp_index // 2, mp_index % 2
        self.dp_index, self.mp_index = dp_index, mp_index
        self.x_side = self.device(self.z, 1 - self.x, self.y, self.core)
        self.y_side = self.device(self.z, self.x, 1 - self.y, self.core)
        self.partner = self.device(self.z, self.x, self.y, 1 - self.core)
        self.above = self.device(self.z + 1, self.x, self.y, self.core)
        self.below = self.device(self.z - 1, self.x, self.y, self.core)
        self.z_near = self.device(self.z + 1 - 2 * lax.rem(self.z, 2), self.x, self.y, self.core)
        self.z_far = self.device(lax.rem(self.z + 2, DEPTH), self.x, self.y, self.core)

    @staticmethod
    def device(z, x, y, core):
        return {"dp": z * 2 + x, "mp": y * 2 + core}

    @staticmethod
    def owner(z, x, y, core):
        return (y * 2 + core) * 8 + z * 2 + x

    def greet(self):
        barrier = pltpu.get_barrier_semaphore()

        def signal(device):
            pl.semaphore_signal(barrier, inc=1, device_id=device, device_id_type=MESH)

        signal(self.x_side)
        signal(self.y_side)
        signal(self.partner)
        pl.when(self.z > 0)(lambda: signal(self.below))
        pl.when(self.z < DEPTH - 1)(lambda: signal(self.above))
        ends = (self.z == 0).astype(jnp.int32) + (self.z == DEPTH - 1).astype(jnp.int32)
        pl.semaphore_wait(barrier, 5 - ends)


def remote(src, dst, send_sem, recv_sem, device):
    return pltpu.make_async_remote_copy(
        src_ref=src,
        dst_ref=dst,
        send_sem=send_sem,
        recv_sem=recv_sem,
        device_id=device,
        device_id_type=MESH,
    )


def spread(at, own_ref, out_ref, own_sem, z_send, z_recv, side_send, side_recv, pair_send, pair_recv):
    rows = own_ref.shape[0]
    half = rows // 2
    z, x, y, core = at.z, at.x, at.y, at.core
    low, high = pl.ds(0, half), pl.ds(half, rows - half)

    def slot(source_z, other_x, other_y):
        return out_ref.at[
            at.owner(source_z, 1 - x if other_x else x, 1 - y if other_y else y, core)
        ]

    def up(source_z, src=None):
        dst = slot(source_z, False, False)
        return remote(dst if src is None else src, dst, z_send.at[0, source_z], z_recv.at[0, source_z], at.above)

    def down(source_z, src=None):
        dst = slot(source_z, False, False)
        return remote(dst if src is None else src, dst, z_send.at[1, source_z], z_recv.at[1, source_z], at.below)

    def side(kind, source_z, src=None):
        if kind == 0 or kind == 1:
            dst = slot(source_z, False, False)
        elif kind == 2:
            dst = slot(source_z, True, False).at[low]
        else:
            dst = slot(source_z, False, True).at[high]
        device = at.x_side if kind in (0, 3) else at.y_side
        return remote(
            dst if src is None else src, dst, side_send.at[kind, source_z], side_recv.at[kind, source_z], device
        )

    def side_arrival(kind, source_z):
        if kind == 0:
            dst = slot(source_z, True, False)
        elif kind == 1:
            dst = slot(source_z, False, True)
        elif kind == 2:
            dst = slot(source_z, True, True).at[low]
        else:
            dst = slot(source_z, True, True).at[high]
        device = at.x_side if kind in (0, 3) else at.y_side
        return remote(dst, dst, side_send.at[kind, source_z], side_recv.at[kind, source_z], device)

    def pair_region(kind, source_z, of_core):
        other_x, other_y = ((False, False), (True, False), (False, True), (True, True), (True, True))[kind]
        ref = out_ref.at[at.owner(source_z, 1 - x if other_x else x, 1 - y if other_y else y, of_core)]
        if kind == 3:
            ref = ref.at[low]
        elif kind == 4:
            ref = ref.at[high]
        return ref

    def pair(kind, source_z, src=None):
        dst = pair_region(kind, source_z, core)
        return remote(
            dst if src is None else src, dst, pair_send.at[kind, source_z], pair_recv.at[kind, source_z], at.partner
        )

    def pair_arrival(kind, source_z):
        dst = pair_region(kind, source_z, 1 - core)
        return remote(dst, dst, pair_send.at[kind, source_z], pair_recv.at[kind, source_z], at.partner)

    keep = pltpu.make_async_copy(own_ref, slot(z, False, False), own_sem)
    pl.when(z < DEPTH - 1)(lambda: up(z, own_ref).start())
    pl.when(z > 0)(lambda: down(z, own_ref).start())
    side(0, z, own_ref).start()
    side(1, z, own_ref).start()
    pair(0, z, own_ref).start()
    keep.start()

    def plane(source_z):
        side_arrival(0, source_z).wait_recv()
        side(2, source_z).start()
        pair(1, source_z).start()
        side_arrival(1, source_z).wait_recv()
        side(3, source_z).start()
        pair(2, source_z).start()

    def column(source_z):
        side(0, source_z).start()
        side(1, source_z).start()
        pair(0, source_z).start()

    for distance in range(1, DEPTH + 1):

        def from_below(source_z=z - distance):
            up(source_z).wait_recv()
            pl.when(z < DEPTH - 1)(lambda: up(source_z).start())
            column(source_z)

        def from_above(source_z=z + distance):
            down(source_z).wait_recv()
            pl.when(z > 0)(lambda: down(source_z).start())
            column(source_z)

        pl.when(z - distance >= 0)(from_below)
        pl.when(z + distance <= DEPTH - 1)(from_above)
        past = distance - 1
        if past == 0:
            plane(z)
        else:
            pl.when(z - past >= 0)(functools.partial(plane, z - past))
            pl.when(z + past <= DEPTH - 1)(functools.partial(plane, z + past))

    def corner(source_z):
        side_arrival(2, source_z).wait_recv()
        pair(3, source_z).start()
        side_arrival(3, source_z).wait_recv()
        pair(4, source_z).start()

    for distance in range(DEPTH):
        if distance == 0:
            corner(z)
        else:
            pl.when(z - distance >= 0)(functools.partial(corner, z - distance))
            pl.when(z + distance <= DEPTH - 1)(functools.partial(corner, z + distance))
    keep.wait()
    for source_z in range(DEPTH):
        for kind in range(5):
            pair_arrival(kind, source_z).wait_recv()
            pair(kind, source_z).wait_send()
        for kind in range(4):
            side(kind, source_z).wait_send()
        pl.when((z < DEPTH - 1) & (source_z <= z))(lambda: up(source_z).wait_send())
        pl.when((z > 0) & (source_z >= z))(lambda: down(source_z).wait_send())


SPREAD_SEMS = [
    pltpu.SemaphoreType.DMA,
    pltpu.SemaphoreType.DMA((2, DEPTH)),
    pltpu.SemaphoreType.DMA((2, DEPTH)),
    pltpu.SemaphoreType.DMA((4, DEPTH)),
    pltpu.SemaphoreType.DMA((4, DEPTH)),
    pltpu.SemaphoreType.DMA((5, DEPTH)),
    pltpu.SemaphoreType.DMA((5, DEPTH)),
]


def gather_kernel(qkv_ref, proj_ref, expand_ref, contract_ref, misc_ref, out_ref, expand_bias, qv_bias, table,
                  own_ref, misc_out, misc_send, misc_recv, *sems):
    at = Place()
    start = 0
    for weight in (qkv_ref, proj_ref, expand_ref, contract_ref):
        own_ref[pl.ds(start, weight.shape[0])] = weight[...].astype(own_ref.dtype)
        start += weight.shape[0]
    at.greet()
    to_pair = remote(misc_ref, misc_out.at[at.mp_index], misc_send.at[0], misc_recv.at[0], at.partner)
    to_side = remote(misc_ref, misc_out.at[at.mp_index], misc_send.at[1], misc_recv.at[1], at.y_side)
    to_pair.start()
    to_side.start()
    misc_out[at.mp_index] = misc_ref[...]
    over = (1 - at.y) * 2 + at.core
    from_side = remote(misc_ref, misc_out.at[over], misc_send.at[1], misc_recv.at[1], at.y_side)
    relay = remote(misc_out.at[over], misc_out.at[over], misc_send.at[2], misc_recv.at[2], at.partner)
    spread(at, own_ref, out_ref, *sems)
    from_side.wait_recv()
    relay.start()
    beside = at.y * 2 + 1 - at.core
    remote(misc_ref, misc_out.at[beside], misc_send.at[0], misc_recv.at[0], at.partner).wait_recv()
    across = (1 - at.y) * 2 + 1 - at.core
    remote(misc_ref, misc_out.at[across], misc_send.at[2], misc_recv.at[2], at.partner).wait_recv()
    to_pair.wait_send()
    to_side.wait_send()
    relay.wait_send()
    for which in range(4):
        expand_bias[which] = misc_out[which, 0:1]
        for kind in range(2):
            qv_bias[kind : kind + 1, pl.ds(128 * which, 128)] = misc_out[which, 1:2, pl.ds(128 * kind, 128)]
        table[pl.ds(4 * which, 4)] = misc_out[which, 2:6, 0:256]


def gather_all(weights, misc):
    rows, columns = sum(weight.shape[0] for weight in weights), C
    vmem = pl.BlockSpec(memory_space=pltpu.VMEM)
    return pl.pallas_call(
        gather_kernel,
        out_shape=(
            jax.ShapeDtypeStruct((32, rows, columns), low),
            jax.ShapeDtypeStruct((4, 1, columns), wide),
            jax.ShapeDtypeStruct((2, columns), wide),
            jax.ShapeDtypeStruct((HEADS, 256), wide),
        ),
        in_specs=[vmem] * 5,
        out_specs=(pl.BlockSpec(memory_space=pl.ANY), vmem, vmem, vmem),
        scratch_shapes=[
            pltpu.VMEM((rows, columns), low),
            pltpu.VMEM((4,) + misc.shape, wide),
            pltpu.SemaphoreType.DMA((3,)),
            pltpu.SemaphoreType.DMA((3,)),
        ]
        + SPREAD_SEMS,
        compiler_params=pltpu.CompilerParams(collective_id=0, has_side_effects=True),
        name="gather_weights",
    )(*weights, misc)


def collect(at, grads, total_ref, mine, pair_buf, corner_x, corner_y, full_x, full_y, z_up, z_down, z_out,
            load_sem, pair_send, pair_recv, side_send, side_recv, z_send, z_recv):
    rows = total_ref.shape[0]
    half = rows // 2
    z, x, y, core = at.z, at.x, at.y, at.core
    low, high = pl.ds(0, half), pl.ds(half, rows - half)
    orders = ((3, 2, 1, 0), (3, 0, 2, 1), (0, 3, 1, 2), (0, 1, 2, 3))

    def turn(step):
        choice = jnp.int32(orders[3][step])
        for which in range(3):
            choice = jnp.where(z == which, jnp.int32(orders[which][step]), choice)
        return choice

    turns = [turn(step) for step in range(DEPTH)]

    def load(target, y_of):
        return pltpu.make_async_copy(
            grads.at[y_of * 2 + core, target], mine.at[y_of, target], load_sem.at[y_of, target]
        )

    def pair(target, y_of):
        return remote(
            grads.at[y_of * 2 + 1 - core, target], pair_buf.at[y_of, target],
            pair_send.at[y_of, target], pair_recv.at[y_of, target], at.partner,
        )

    def corner(kind, target):
        part = mine.at[1 - y, target, 1 - x]
        if kind == 0:
            return remote(part.at[low], corner_y.at[target], side_send.at[0, target], side_recv.at[0, target], at.y_side)
        return remote(part.at[high], corner_x.at[target], side_send.at[1, target], side_recv.at[1, target], at.x_side)

    def full(kind, target):
        if kind == 2:
            return remote(mine.at[y, target, 1 - x], full_x.at[target], side_send.at[2, target], side_recv.at[2, target], at.x_side)
        return remote(mine.at[1 - y, target, x], full_y.at[target], side_send.at[3, target], side_recv.at[3, target], at.y_side)

    def up(target):
        return remote(z_out.at[target], z_up.at[target], z_send.at[target], z_recv.at[0, target], at.above)

    def down(target):
        return remote(z_out.at[target], z_down.at[target], z_send.at[target], z_recv.at[1, target], at.below)

    wide = jnp.float32
    for target in turns:
        for y_of in (0, 1):
            pair(target, y_of).start()
            load(target, y_of).start()

    def first(target):
        for y_of in (0, 1):
            load(target, y_of).wait()
            pair(target, y_of).wait_recv()

        def add(which, carry):
            y_of, x_of = which // 2, which % 2
            mine[y_of, target, x_of] = (
                mine[y_of, target, x_of].astype(wide) + pair_buf[y_of, target, x_of].astype(wide)
            ).astype(mine.dtype)
            return carry

        lax.fori_loop(0, 4, add, 0)
        corner(0, target).start()
        corner(1, target).start()

    def second(target):
        corner(0, target).wait_recv()
        mine[y, target, 1 - x, low] = (
            mine[y, target, 1 - x, low].astype(wide) + corner_y[target].astype(wide)
        ).astype(mine.dtype)
        full(2, target).start()
        corner(1, target).wait_recv()
        mine[1 - y, target, x, high] = (
            mine[1 - y, target, x, high].astype(wide) + corner_x[target].astype(wide)
        ).astype(mine.dtype)
        full(3, target).start()

    def third(target, last):
        full(2, target).wait_recv()
        full(3, target).wait_recv()
        total_ref[...] = mine[y, target, x].astype(wide) + (
            full_x[target].astype(wide) + full_y[target].astype(wide)
        )

        def add_below():
            up(target).wait_recv()
            total_ref[...] += z_up[target].astype(wide)

        def add_above():
            down(target).wait_recv()
            total_ref[...] += z_down[target].astype(wide)

        pl.when((target >= z) & (z > 0))(add_below)
        pl.when((target <= z) & (z < DEPTH - 1))(add_above)
        if not last:
            z_out[target] = total_ref[...].astype(z_out.dtype)
            pl.when(target > z)(lambda: up(target).start())
            pl.when(target < z)(lambda: down(target).start())

    for step in range(DEPTH + 2):
        if step < DEPTH:
            first(turns[step])
        if 1 <= step <= DEPTH:
            second(turns[step - 1])
        if step >= 2:
            third(turns[step - 2], step - 2 == DEPTH - 1)
    for target in range(DEPTH):
        for y_of in (0, 1):
            pair(target, y_of).wait_send()
        for kind in (0, 1):
            corner(kind, target).wait_send()
        for kind in (2, 3):
            full(kind, target).wait_send()
        pl.when(target != z)(lambda: up(target).wait_send())


def collect_scratch(rows, columns, dtype):
    return [
        pltpu.VMEM((2, DEPTH, 2, rows, columns), dtype),
        pltpu.VMEM((2, DEPTH, 2, rows, columns), dtype),
        pltpu.VMEM((DEPTH, rows // 2, columns), dtype),
        pltpu.VMEM((DEPTH, rows // 2, columns), dtype),
        pltpu.VMEM((DEPTH, rows, columns), dtype),
        pltpu.VMEM((DEPTH, rows, columns), dtype),
        pltpu.VMEM((DEPTH, rows, columns), dtype),
        pltpu.VMEM((DEPTH, rows, columns), dtype),
        pltpu.VMEM((DEPTH, rows, columns), dtype),
        pltpu.SemaphoreType.DMA((2, DEPTH)),
        pltpu.SemaphoreType.DMA((2, DEPTH)),
        pltpu.SemaphoreType.DMA((2, DEPTH)),
        pltpu.SemaphoreType.DMA((4, DEPTH)),
        pltpu.SemaphoreType.DMA((4, DEPTH)),
        pltpu.SemaphoreType.DMA((DEPTH,)),
        pltpu.SemaphoreType.DMA((2, DEPTH)),
    ]


N_COLLECT = 16


def muon_kernel(grads, qkv_ref, proj_ref, expand_ref, contract_ref, grad_out, moment_out, next_all,
                own_next, *scratch):
    at = Place()
    at.greet()
    collect(at, grads, grad_out, *scratch[:N_COLLECT])
    start = 0
    for moment_ref in (qkv_ref, proj_ref, expand_ref, contract_ref):
        rows = pl.ds(start, moment_ref.shape[0])
        grad = grad_out[rows]
        moment = muon_beta * moment_ref[...] + grad
        moment_out[rows] = moment
        own_next[rows] = (grad + muon_beta * moment).astype(own_next.dtype)
        start += moment_ref.shape[0]
    spread(at, own_next, next_all, *scratch[N_COLLECT:])


def muon_exchange(grads, moments):
    rows, columns = sum(moment.shape[0] for moment in moments), C
    shape = jax.ShapeDtypeStruct((rows, columns), jnp.float32)
    vmem = pl.BlockSpec(memory_space=pltpu.VMEM)
    hbm = pl.BlockSpec(memory_space=pl.ANY)
    return pl.pallas_call(
        muon_kernel,
        out_shape=(shape, shape, jax.ShapeDtypeStruct((32, rows, columns), jnp.bfloat16)),
        in_specs=[hbm] + [vmem] * 4,
        out_specs=(vmem, vmem, hbm),
        scratch_shapes=[pltpu.VMEM((rows, columns), jnp.bfloat16)]
        + collect_scratch(rows, columns, jnp.bfloat16)
        + SPREAD_SEMS,
        compiler_params=pltpu.CompilerParams(
            collective_id=1, has_side_effects=True, vmem_limit_bytes=40 * 1024 * 1024
        ),
        name="muon_exchange",
    )(grads.reshape(4, DEPTH, 2, rows, columns), *moments)


def ns_kernel(next_all, own_images, small_ref, swapped, images_all, small_out,
              products, rows_buf, map_buf, gram_buf, total_buf, small_parts, small_in, sem, keep_sem,
              act_send, act_recv, small_send, small_recv, swap_send, swap_recv):
    at = Place()
    mp_index, dp_index = at.mp_index, at.dp_index
    counts = (48, 16, 64, 64)
    pieces = own_images.shape[0]
    over = (1 - at.y) * 2 + at.core
    across = (1 - at.y) * 2 + 1 - at.core
    beside = at.y * 2 + 1 - at.core
    mp_peers = [{"dp": dp_index, "mp": lax.rem(mp_index + shift, 4)} for shift in (1, 2, 3)]
    small_peers = (at.y_side, at.partner, at.x_side, at.z_near, at.z_far)
    barrier = pltpu.get_barrier_semaphore()
    for device in (*mp_peers, at.x_side, at.z_near, at.z_far):
        pl.semaphore_signal(barrier, inc=1, device_id=device, device_id_type=MESH)

    def fetch(which):
        count = counts[which]
        copy = pltpu.make_async_copy(
            next_all.at[:, pl.ds(sum(counts[:which]), count)], rows_buf.at[:, pl.ds(0, count)], sem
        )
        copy.start()
        if count < 64:
            rows_buf[:, pl.ds(count, 64 - count)] = jnp.zeros((32, 64 - count, C), rows_buf.dtype)
        copy.wait()

    pl.semaphore_wait(barrier, 6)

    def slot(of_mp, image):
        return images_all.at[of_mp * pieces + image]

    def keep_copy(image):
        return pltpu.make_async_copy(own_images.at[image], slot(mp_index, image), keep_sem.at[image])

    def own_copy(which, image):
        device = (at.partner, at.y_side)[which]
        return remote(
            own_images.at[image], slot(mp_index, image), act_send.at[which, image], act_recv.at[which, image], device
        )

    def own_arrival(which, image):
        source, device = ((beside, at.partner), (over, at.y_side))[which]
        return remote(
            own_images.at[image], slot(source, image), act_send.at[which, image], act_recv.at[which, image], device
        )

    def relay(image):
        return remote(slot(over, image), slot(over, image), act_send.at[2, image], act_recv.at[2, image], at.partner)

    def relay_arrival(image):
        return remote(
            slot(across, image), slot(across, image), act_send.at[2, image], act_recv.at[2, image], at.partner
        )

    def small_copy(stage):
        source = small_ref if stage == 0 else small_parts.at[stage - 1]
        return remote(source, small_in.at[stage], small_send.at[stage], small_recv.at[stage], small_peers[stage])

    def small_step(stage):
        small_copy(stage).wait_recv()
        held = small_ref[...] if stage == 0 else small_parts[stage - 1]
        held = held + small_in[stage]
        if stage < 4:
            small_parts[stage] = held
            small_copy(stage + 1).start()
        else:
            small_out[...] = held

    small_copy(0).start()
    for image in range(pieces):
        own_copy(1, image).start()
    for image in range(pieces):
        own_copy(0, image).start()
        keep_copy(image).start()

    for which in range(4):
        pl.when(mp_index == which)(functools.partial(fetch, which))

    gram = None
    for part in range(4):
        block = rows_buf[8 * part : 8 * (part + 1)].reshape(512, C)
        term = dot_tn(block, block)
        gram = term if gram is None else gram + term
    eye = (
        lax.broadcasted_iota(jnp.int32, (C, C), 0) == lax.broadcasted_iota(jnp.int32, (C, C), 1)
    ).astype(wide)
    norm_value = jnp.sqrt(jnp.sum(jnp.sum(gram * eye, axis=1, keepdims=True), axis=0, keepdims=True)) + ns_eps
    gram = gram / (norm_value * norm_value)

    def dot_high(a, b):
        return jnp.dot(a, b, precision=lax.Precision.HIGH, preferred_element_type=wide)

    def pass_on(image):
        own_arrival(1, image).wait_recv()
        relay(image).start()

    def poly_of(gram):
        square = dot_high(gram, gram)
        return coef_a * eye + (coef_b * gram + coef_c * square)

    gram_buf[...] = gram
    poly = poly_of(gram)
    total_buf[...] = poly
    gram_buf[...] = dot_high(dot_high(gram, poly), poly)
    pl.when(at.z >= 0)(functools.partial(small_step, 0))

    def iterate(iteration, carry):
        gram = gram_buf[...]
        poly = poly_of(gram)
        total_buf[...] = dot_high(total_buf[...], poly)
        gram_buf[...] = dot_high(dot_high(gram, poly), poly)
        for which in range(1, NS_ITERS - 1):
            pl.when(iteration == which)(functools.partial(small_step, which))
        return carry

    lax.fori_loop(1, NS_ITERS - 1, iterate, 0)
    total = dot_high(total_buf[...], poly_of(gram_buf[...]))
    pl.when(at.z >= 0)(functools.partial(small_step, NS_ITERS - 1))
    map_buf[...] = total / norm_value

    def swap_copy(which):
        return remote(
            products.at[lax.rem(mp_index + which + 1, 4)], swapped.at[mp_index],
            swap_send.at[which], swap_recv.at[which], mp_peers[which],
        )

    for group in range(4):
        rows = rows_buf[group * 8 + dp_index].astype(wide)
        products[group] = dot_high(rows, map_buf[...]).astype(products.dtype)
    for which in (1, 2, 0):
        swap_copy(which).start()
    swapped[mp_index] = products[mp_index]
    for image in range(pieces):
        pass_on(image)
    for image in range(pieces):
        own_arrival(0, image).wait_recv()
        relay_arrival(image).wait_recv()
        own_copy(0, image).wait_send()
        own_copy(1, image).wait_send()
        relay(image).wait_send()
        keep_copy(image).wait()
    for which in range(3):
        source = lax.rem(mp_index + 3 - which, 4)
        remote(
            products.at[source], swapped.at[source], swap_send.at[which], swap_recv.at[which],
            {"dp": dp_index, "mp": source},
        ).wait_recv()
        swap_copy(which).wait_send()
    for stage in range(5):
        small_copy(stage).wait_send()


def newton_schulz_rows(next_all, own_images, small):
    vmem = pl.BlockSpec(memory_space=pltpu.VMEM)
    hbm = pl.BlockSpec(memory_space=pl.ANY)
    pieces = own_images.shape[0]
    return pl.pallas_call(
        ns_kernel,
        out_shape=(
            jax.ShapeDtypeStruct((4, 64, C), low),
            jax.ShapeDtypeStruct((4 * pieces,) + own_images.shape[1:], low),
            jax.ShapeDtypeStruct(small.shape, wide),
        ),
        in_specs=[hbm, vmem, vmem],
        out_specs=(vmem, hbm, vmem),
        scratch_shapes=[
            pltpu.VMEM((4, 64, C), low),
            pltpu.VMEM((32, 64, C), low),
            pltpu.VMEM((C, C), wide),
            pltpu.VMEM((C, C), wide),
            pltpu.VMEM((C, C), wide),
            pltpu.VMEM((4,) + small.shape, wide),
            pltpu.VMEM((5,) + small.shape, wide),
            pltpu.SemaphoreType.DMA,
            pltpu.SemaphoreType.DMA((pieces,)),
            pltpu.SemaphoreType.DMA((3, pieces)),
            pltpu.SemaphoreType.DMA((3, pieces)),
            pltpu.SemaphoreType.DMA((5,)),
            pltpu.SemaphoreType.DMA((5,)),
            pltpu.SemaphoreType.DMA((3,)),
            pltpu.SemaphoreType.DMA((3,)),
        ],
        compiler_params=pltpu.CompilerParams(
            collective_id=2, has_side_effects=True, vmem_limit_bytes=40 * 1024 * 1024
        ),
        name="newton_schulz",
    )(next_all, own_images, small)


def update_kernel(grads, moments, swapped, *refs):
    weights, outs = refs[:4], refs[4:]
    factors = (math.sqrt(3.0), 1.0, math.sqrt(max(1.0, FF / C)), 1.0)
    start = 0
    for which in range(4):
        count = weights[which].shape[0]
        rows = pl.ds(start, count)
        outs[which][...] = grads[rows]
        outs[4 + which][...] = moments[rows]
        part = swapped[which, pl.ds(0, count)].astype(wide)
        outs[8 + which][...] = -muon_rate * (muon_decay * weights[which][...] + factors[which] * part)
        start += count


def update_shards(grads, moments, swapped, weights):
    vmem = pl.BlockSpec(memory_space=pltpu.VMEM)
    shapes = [jax.ShapeDtypeStruct(weight.shape, wide) for weight in weights] * 3
    return pl.pallas_call(
        update_kernel,
        out_shape=shapes,
        in_specs=[vmem] * 7,
        out_specs=[vmem] * 12,
        name="update_shards",
    )(grads, moments, swapped, *weights)


def split_low(values):
    high = lax.reduce_precision(values, exponent_bits=8, mantissa_bits=7)
    return high.astype(jnp.bfloat16), (values - high).astype(jnp.bfloat16)


def dot_three(left, right):
    left_high, left_rest = left
    right_high, right_rest = right
    wide = dict(preferred_element_type=jnp.float32)
    return (
        jnp.dot(left_rest, right_high, **wide)
        + jnp.dot(left_high, right_rest, **wide)
        + jnp.dot(left_high, right_high, **wide)
    )


def newton_schulz(gram):
    width = gram.shape[0]
    eye = jnp.eye(width, dtype=jnp.float32)
    norm_value = jnp.sqrt(jnp.sum(gram * eye)) + ns_eps
    gram = gram / (norm_value * norm_value)
    total = None
    for iteration in range(NS_ITERS):
        parts = split_low(gram)
        square = dot_three(parts, parts)
        poly = coef_a * eye + (coef_b * gram + coef_c * square)
        poly_parts = split_low(poly)
        total = poly if total is None else dot_three(split_low(total), poly_parts)
        if iteration + 1 < NS_ITERS:
            half = dot_three(parts, poly_parts)
            gram = dot_three(split_low(half), poly_parts)
    return total / norm_value


def adam_update(grad_sum, first_moment, second_moment):
    first_new = adam_one * first_moment + (1.0 - adam_one) * grad_sum
    second_new = adam_two * second_moment + (1.0 - adam_two) * grad_sum * grad_sum
    first_hat = first_new / (1.0 - adam_one**adam_step)
    second_hat = second_new / (1.0 - adam_two**adam_step)
    return (-adam_rate * first_hat / (jnp.sqrt(second_hat) + adam_eps), first_new, second_new)


def exchange_plain(own_low, own_moments, rows):
    everyone = ("mp", "dp")
    starts = [sum(rows[:which]) for which in range(4)]

    def cut(stacked):
        return [stacked[:, start : start + count] for start, count in zip(starts, rows)]

    gathered = [
        part.reshape(-1, C) for part in cut(lax.all_gather(own_low, everyone, axis=0, tiled=False))
    ]

    def finish(big_local):
        mp_size, dp_size = lax.axis_size("mp"), lax.axis_size("dp")
        mp_index, dp_index = lax.axis_index("mp"), lax.axis_index("dp")
        devices = mp_size * dp_size
        stacked_grads = jnp.concatenate(
            [grad.reshape(devices, count, C) for grad, count in zip(big_local, rows)], axis=1
        )
        own_grads = lax.psum_scatter(
            stacked_grads.reshape(devices * sum(rows), C), everyone, scatter_dimension=0, tiled=True
        ).astype(wide)
        own_buffers = muon_beta * own_moments + own_grads
        own_nesterov = own_grads + muon_beta * own_buffers
        iterate_all = lax.all_gather(own_nesterov.astype(low), everyone, axis=0, tiled=False)
        grams = jnp.stack([dot_tn(part.reshape(-1, C), part.reshape(-1, C)) for part in cut(iterate_all)])
        ortho_map = newton_schulz(lax.dynamic_index_in_dim(grams, mp_index, 0, keepdims=False))
        most = max(rows)
        picked = lax.dynamic_slice(
            iterate_all.reshape(mp_size, dp_size, sum(rows), C),
            (
                jnp.int32(0),
                dp_index.astype(jnp.int32),
                jnp.array(starts, jnp.int32)[mp_index],
                jnp.int32(0),
            ),
            (mp_size, 1, most, C),
        ).reshape(mp_size * most, C)
        map_parts = split_low(ortho_map)
        products = dot(picked, map_parts[0]) + dot(picked, map_parts[1])
        swapped = lax.all_to_all(products.reshape(mp_size, most, C), "mp", 0, 0, tiled=False)
        return own_grads, own_buffers, swapped

    return gathered, finish


def shards(
    images,
    cotangent,
    qkv_weight,
    proj_weight,
    expand_weight,
    contract_weight,
    qkv_moment,
    proj_moment,
    expand_moment,
    contract_moment,
    vectors,
    qv_bias,
    expand_bias,
    rel_table,
    vectors_first,
    vectors_second,
    qv_first,
    qv_second,
    expand_bias_first,
    expand_bias_second,
    table_first,
    table_second,
    region_ids,
    pos_index,
    image_counts,
):
    everyone = ("mp", "dp")
    mp_size, dp_size = lax.axis_size("mp"), lax.axis_size("dp")
    mp_index = lax.axis_index("mp")
    linked = mp_size == 4 and dp_size == 8
    per_device = IMG_DEV // mp_size
    first_image = (mp_index * per_device).astype(jnp.int32)
    place = jnp.stack([first_image, image_counts[0]])
    own_images = lax.dynamic_slice_in_dim(images, first_image, per_device, 0)
    own_cotangent = lax.dynamic_slice_in_dim(cotangent, first_image, per_device, 0)
    weights_all = (qkv_weight, proj_weight, expand_weight, contract_weight)
    rows = [weight.shape[0] for weight in weights_all]
    starts = [sum(rows[:which]) for which in range(4)]
    moments = (qkv_moment, proj_moment, expand_moment, contract_moment)
    if linked:
        misc = jnp.concatenate(
            [
                expand_bias[None],
                jnp.pad(qv_bias.reshape(1, -1), ((0, 0), (0, C - qv_bias.size))),
                jnp.pad(rel_table.T, ((0, 2), (0, C - TABLE))),
            ],
            axis=0,
        )
        gathered, expand_full, qv_full, table_wide = gather_all(weights_all, misc)
        table_full = table_wide[:, :TABLE]
    else:
        own_low = jnp.concatenate([weight.astype(low) for weight in weights_all], axis=0)
        own_moments = jnp.concatenate(moments, axis=0)
        gathered, finish_plain = exchange_plain(own_low, own_moments, rows)
        qv_full = lax.all_gather(qv_bias, "mp", axis=1, tiled=True)
        expand_full = lax.all_gather(expand_bias, "mp", axis=0, tiled=True).reshape(4, C)
        table_full = lax.all_gather(rel_table.T, "mp", axis=0, tiled=True)
    onehot = (
        jnp.arange(TABLE, dtype=jnp.int32)[:, None] == pos_index.reshape(1, SPAN * SPAN)
    ).astype(wide)
    pos_bias = jnp.dot(table_full, onehot, precision=highest).reshape(HEADS, SPAN, SPAN)
    window_regions = to_windows(region_ids.reshape(1, TOK, 1))[:, :, 0]
    window_mask = jnp.where(
        window_regions[:, :, None] != window_regions[:, None, :], mask_value, 0.0
    ).astype(wide)
    bias = pair_bias(pos_bias, window_mask)
    block_low, input_low, big_local, small_rows, table_pairs = run_layer(
        linked, per_device, place, own_images, own_cotangent, vectors, qv_full, expand_full, bias, gathered
    )
    if linked:
        block_out = block_low
    else:
        block_out = lax.all_gather(block_low, "mp", axis=0, tiled=True)
        input_grad = lax.all_gather(input_low, "mp", axis=0, tiled=True)
    pairs = table_pairs.reshape(HEADS, PAIR, PAIR)
    bias_heads = pairs[:, :SPAN, :SPAN] + pairs[:, SPAN : 2 * SPAN, SPAN : 2 * SPAN]
    table_local = lax.dot_general(
        bias_heads.reshape(HEADS, SPAN * SPAN),
        onehot,
        (((1,), (1,)), ((), ())),
        precision=highest,
        preferred_element_type=wide,
    )
    if linked:
        small_own = jnp.concatenate(
            [small_rows, jnp.pad(table_local, ((0, 0), (0, C - TABLE)))], axis=0
        )
        own_grads, own_buffers, next_all = muon_exchange(big_local, moments)
        swapped, input_grad, small_all = newton_schulz_rows(next_all, input_low, small_own)
        small_full, table_all = small_all[:HEADS], small_all[HEADS:, :TABLE]
    else:
        small_full, table_all = lax.psum((small_rows, table_local), everyone)
        own_grads, own_buffers, swapped = finish_plain(big_local)
    updated = update_shards(own_grads, own_buffers, swapped, weights_all)
    shares, buffers, new_steps = updated[:4], updated[4:8], updated[8:]

    def own_columns(full, width):
        return lax.dynamic_slice_in_dim(full, mp_index * width, width, full.ndim - 1)

    small_sums = (
        small_full[:6],
        own_columns(small_full[6:8], qv_bias.shape[1]),
        own_columns(small_full[8:12].reshape(FF), expand_bias.shape[0]),
        lax.dynamic_slice_in_dim(table_all, mp_index * rel_table.shape[1], rel_table.shape[1], 0).T,
    )
    vectors_step, vectors_first_new, vectors_second_new = adam_update(
        small_sums[0], vectors_first, vectors_second
    )
    qv_step, qv_first_new, qv_second_new = adam_update(small_sums[1], qv_first, qv_second)
    expand_bias_step, expand_bias_first_new, expand_bias_second_new = adam_update(
        small_sums[2], expand_bias_first, expand_bias_second
    )
    table_step, table_first_new, table_second_new = adam_update(
        small_sums[3], table_first, table_second
    )
    return (
        block_out,
        input_grad,
        shares[0],
        shares[1],
        shares[2],
        shares[3],
        small_sums[0],
        small_sums[1],
        small_sums[2],
        small_sums[3],
        new_steps[0],
        new_steps[1],
        new_steps[2],
        new_steps[3],
        buffers[0],
        buffers[1],
        buffers[2],
        buffers[3],
        vectors_step,
        qv_step,
        expand_bias_step,
        table_step,
        vectors_first_new,
        vectors_second_new,
        qv_first_new,
        qv_second_new,
        expand_bias_first_new,
        expand_bias_second_new,
        table_first_new,
        table_second_new,
    )


def solution(mesh):
    return jax.shard_map(
        shards,
        mesh=mesh,
        in_specs=(
            P("dp", None, None),
            P("dp", None, None),
            P(("mp", "dp"), None),
            P(("mp", "dp"), None),
            P(("mp", "dp"), None),
            P(("mp", "dp"), None),
            P(("mp", "dp"), None),
            P(("mp", "dp"), None),
            P(("mp", "dp"), None),
            P(("mp", "dp"), None),
            P(),
            P(None, "mp"),
            P("mp"),
            P(None, "mp"),
            P(),
            P(),
            P(None, "mp"),
            P(None, "mp"),
            P("mp"),
            P("mp"),
            P(None, "mp"),
            P(None, "mp"),
            P(),
            P(),
            P("dp"),
        ),
        out_specs=(
            P("dp", None, None),
            P("dp", None, None),
            P(("mp", "dp"), None),
            P(("mp", "dp"), None),
            P(("mp", "dp"), None),
            P(("mp", "dp"), None),
            P(),
            P(None, "mp"),
            P("mp"),
            P(None, "mp"),
            P(("mp", "dp"), None),
            P(("mp", "dp"), None),
            P(("mp", "dp"), None),
            P(("mp", "dp"), None),
            P(("mp", "dp"), None),
            P(("mp", "dp"), None),
            P(("mp", "dp"), None),
            P(("mp", "dp"), None),
            P(),
            P(None, "mp"),
            P("mp"),
            P(None, "mp"),
            P(),
            P(),
            P(None, "mp"),
            P(None, "mp"),
            P("mp"),
            P("mp"),
            P(None, "mp"),
            P(None, "mp"),
        ),
        check_vma=False,
    )
```

```python
import functools
import math

import jax
import jax.numpy as jnp
import numpy as np
from jax import lax
from jax.experimental import pallas as pl
from jax.experimental.pallas import tpu as pltpu
from jax.sharding import PartitionSpec as P

C = 512
HEADS = 16
HD = 32
FF = 2048
WIN = 7
SIDE = 14
SHIFT = 3
SPAN = WIN * WIN
TOK = SIDE * SIDE
NS_ITERS = 5
IMG_DEV = 16
TABLE = 169
PAIR = 112
ROWS = 2 * PAIR
GROUP = 4

norm_eps = 1e-05
ns_eps = 1e-07
coef_a = 3.4445
coef_b = -4.775
coef_c = 2.0315
muon_rate = 0.3
muon_decay = 0.1
muon_beta = 0.95
adam_rate = 0.1
adam_one = 0.9
adam_two = 0.999
adam_eps = 1e-08
adam_step = 4
mask_value = -100.0
away = -1e30
wide = jnp.float32
low = jnp.bfloat16
highest = lax.Precision.HIGHEST


def to_windows(field_values):
    image_total = field_values.shape[0]
    channels = field_values.shape[-1]
    blocks = SIDE // WIN
    grid_values = field_values.reshape(image_total, SIDE, SIDE, channels)
    grid_values = jnp.roll(grid_values, (-SHIFT, -SHIFT), axis=(1, 2))
    grid_values = grid_values.reshape(image_total, blocks, WIN, blocks, WIN, channels)
    grid_values = grid_values.transpose(0, 1, 3, 2, 4, 5)
    return grid_values.reshape(image_total * blocks * blocks, WIN * WIN, channels)


def window_order():
    order = np.full((ROWS,), -1, np.int64)
    for window in range(4):
        top, left = window // 2, window % 2
        for token in range(SPAN):
            row = (top * WIN + token // WIN + SHIFT) % SIDE
            column = (left * WIN + token % WIN + SHIFT) % SIDE
            order[(window // 2) * PAIR + (window % 2) * SPAN + token] = row * SIDE + column
    return order


def dot(a, b):
    return jnp.dot(a, b, preferred_element_type=wide)


def dot_nt(a, b):
    return lax.dot_general(a, b, (((1,), (1,)), ((), ())), preferred_element_type=wide)


def dot_tn(a, b):
    return lax.dot_general(a, b, (((0,), (0,)), ((), ())), preferred_element_type=wide)


def mean_of(values):
    return jnp.sum(values, axis=-1, keepdims=True) * (1.0 / C)


def normalize(values):
    centered = values - mean_of(values)
    inv_scale = lax.rsqrt(mean_of(centered * centered) + norm_eps)
    return centered * inv_scale, inv_scale


def normalize_back(grad_norm, normed, inv_scale, gain):
    scaled = grad_norm * gain
    return inv_scale * (scaled - mean_of(scaled) - normed * mean_of(scaled * normed))


def column_sum(values):
    return jnp.sum(values, axis=0, keepdims=True)


def head_masks():
    lane = lax.broadcasted_iota(jnp.int32, (1, 128), 1) // HD
    return [(lane == head).astype(wide).astype(low) for head in range(GROUP)]


def stack_heads(block, masks):
    return jnp.concatenate([block * mask for mask in masks], axis=0)


def pick_heads(stacked):
    lane = lax.broadcasted_iota(jnp.int32, (PAIR, 128), 1)
    parts = [stacked[PAIR * head : PAIR * (head + 1)] for head in range(GROUP)]
    return jnp.where(
        lane < 2 * HD,
        jnp.where(lane < HD, parts[0], parts[1]),
        jnp.where(lane < 3 * HD, parts[2], parts[3]),
    )


def layer_kernel(
    packed, batch, place, images, cotangent, order, order_back, vectors, qv_bias, expand_bias, bias,
    qkv_hbm, proj_hbm, expand_hbm, contract_hbm,
    block_out, input_grad, *rest,
):
    n_grads = 1 if packed else 4
    grad_outs = rest[:n_grads]
    (small, table_sum, qkv_nat, qkv_w, proj_w, expand_w, contract_w,
     qkv_acc, proj_acc, expand_acc, contract_acc,
     qkv_s, att_s, back_s, probs_s, normed_s, first_s, middle_s, normed2_s, second_s,
     out_low_s, mlp_s, second_grad_s, sems) = rest[n_grads : n_grads + 24]
    step = pl.program_id(0)
    steps = pl.num_programs(0)
    masks = head_masks()
    if packed:
        staged, keep_sem, act_send, act_recv = rest[n_grads + 24 :]
        at = Place()
        per_device = staged.shape[0]
        over = (1 - at.y) * 2 + at.core
        across = (1 - at.y) * 2 + 1 - at.core
        beside = at.y * 2 + 1 - at.core

        def slot(mp_index, image):
            return block_out.at[mp_index * per_device + image]

        def keep_copy(image):
            return pltpu.make_async_copy(staged.at[image], slot(at.mp_index, image), keep_sem.at[image])

        def own_copy(which, image):
            device = (at.partner, at.y_side)[which]
            return remote(
                staged.at[image], slot(at.mp_index, image),
                act_send.at[which, image], act_recv.at[which, image], device,
            )

        def own_arrival(which, image):
            source, device = ((beside, at.partner), (over, at.y_side))[which]
            return remote(
                staged.at[image], slot(source, image),
                act_send.at[which, image], act_recv.at[which, image], device,
            )

        def relay(image):
            return remote(
                slot(over, image), slot(over, image), act_send.at[2, image], act_recv.at[2, image], at.partner
            )

        def relay_arrival(image):
            return remote(
                slot(across, image), slot(across, image), act_send.at[2, image], act_recv.at[2, image], at.partner
            )

        def pass_on(of_step):
            for slice_ in range(batch):
                image = of_step * batch + slice_
                own_arrival(1, image).wait_recv()
                relay(image).start()

        def greet():
            barrier = pltpu.get_barrier_semaphore()
            for device in (at.partner, at.y_side):
                pl.semaphore_signal(barrier, inc=1, device_id=device, device_id_type=MESH)
            pl.semaphore_wait(barrier, 2)

        pl.when(step == 0)(greet)

    def put_block(slice_, value):
        if packed:
            image = step * batch + slice_
            staged[image] = value
            own_copy(1, image).start()
            own_copy(0, image).start()
            keep_copy(image).start()
        else:
            block_out[slice_] = value

    def put_grad(slice_, value):
        input_grad[slice_] = value

    def two_of(body):
        return lambda index, carry: body(2 * index + 1, body(2 * index, carry))

    row = lax.broadcasted_iota(jnp.int32, (batch * ROWS, 1), 0) // ROWS
    live_scale = jnp.zeros((batch * ROWS, 1), wide)
    for slice_ in range(batch):
        is_live = (place[1] > place[0] + step * batch + slice_).astype(wide)
        live_scale = jnp.where(row == slice_, is_live, live_scale)

    def fetch(which):
        if packed:
            counts = (48, 16, 64, 64)
            source = qkv_hbm.at[:, pl.ds(sum(counts[:which]), counts[which])]
            target = (qkv_nat, proj_w, expand_w, contract_w)[which]
        else:
            source = (qkv_hbm, proj_hbm, expand_hbm, contract_hbm)[which]
            target = (qkv_nat, proj_w, expand_w, contract_w)[which]
        return pltpu.make_async_copy(source, target, sems.at[which])

    def rows_of(ref, count):
        return ref[...].reshape(count, C)

    def begin():
        for which in range(4):
            fetch(which).start()
        for ref in (qkv_acc, proj_acc, expand_acc, contract_acc, small, table_sum):
            ref[...] = jnp.zeros_like(ref)
        for which in range(4):
            fetch(which).wait()
        natural = rows_of(qkv_nat, 3 * C).reshape(HEADS, 3, HD, C)
        for kind in range(3):
            qkv_w[kind] = natural[:, kind].reshape(C, C)

    pl.when(step == 0)(begin)

    tokens = jnp.concatenate([dot(order[...], images[slice_]) for slice_ in range(batch)], axis=0)
    normed, inv_one = normalize(tokens)
    normed_s[...] = normed
    first_in = (normed * vectors[0:1] + vectors[1:2]).astype(low)
    first_s[...] = first_in
    for kind in range(3):
        projected = dot_nt(first_in, qkv_w[kind])
        if kind != 1:
            projected = projected + qv_bias[kind // 2 : kind // 2 + 1]
        projected = projected.astype(low)
        for group in range(4):
            qkv_s[kind * 4 + group] = projected[:, 128 * group : 128 * (group + 1)]
    score_scale = 1.0 / math.sqrt(HD)

    def attend(which, carry):
        pair, group = which // 4, which % 4
        pair_scores = bias[pair, group]
        for slice_ in range(batch):
            rows = pl.ds(pl.multiple_of(slice_ * ROWS + pair * PAIR, 16), PAIR)
            queries = stack_heads(qkv_s[group, rows], masks)
            scores = dot_nt(queries, qkv_s[4 + group, rows]) * score_scale + pair_scores
            top = jnp.max(scores, axis=-1, keepdims=True)
            exponent = jnp.exp(scores - top)
            attention = exponent / jnp.sum(exponent, axis=-1, keepdims=True)
            probs_s[slice_, which] = attention
            att_s[group, rows] = pick_heads(dot(attention.astype(low), qkv_s[8 + group, rows])).astype(low)
        return carry

    lax.fori_loop(0, 2, two_of(two_of(attend)), 0)
    attended = jnp.concatenate([att_s[group] for group in range(4)], axis=1)
    middle = tokens + (dot(attended, rows_of(proj_w, C)) + vectors[4:5])
    middle_s[...] = middle
    normed_two, inv_two = normalize(middle)
    normed2_s[...] = normed_two
    second_in = (normed_two * vectors[2:3] + vectors[3:4]).astype(low)
    second_s[...] = second_in

    grad_tokens = jnp.concatenate([dot(order[...], cotangent[slice_]) for slice_ in range(batch)], axis=0)
    out_low = (grad_tokens * live_scale).astype(low)
    out_low_s[...] = out_low
    mlp_s[...] = jnp.zeros_like(mlp_s)
    second_grad_s[...] = jnp.zeros_like(second_grad_s)
    chunk = 512
    owners = expand_w.shape[0] // (FF // chunk)

    def feed(which, carry):
        units = pl.ds(pl.multiple_of(which * owners, owners), owners)
        expand_part = expand_w[units].reshape(chunk, C)
        contract_part = contract_w[units].reshape(chunk, C)
        second = second_s[...]
        grad_rows = out_low_s[...]
        hidden = dot_nt(second, expand_part) + expand_bias[which]
        cumulative = 0.5 * (1.0 + lax.erf(hidden * (1.0 / math.sqrt(2.0))))
        acted = (hidden * cumulative).astype(low)
        slope = cumulative + hidden * jnp.exp(-0.5 * hidden * hidden) * (1.0 / math.sqrt(2.0 * math.pi))
        mlp_s[...] += dot(acted, contract_part)
        hidden_grad32 = dot_nt(grad_rows, contract_part) * slope
        hidden_grad = hidden_grad32.astype(low)
        small[pl.ds(8 + which, 1)] += column_sum(hidden_grad.astype(wide))
        second_grad_s[...] += dot(hidden_grad, expand_part)
        units_wide = pl.ds(pl.multiple_of(which * chunk, chunk), chunk)
        contract_acc[units_wide] += dot_tn(acted, grad_rows)
        expand_acc[units_wide] += dot_tn(hidden_grad, second)
        return carry

    lax.fori_loop(0, FF // chunk, feed, 0)
    result = middle_s[...] + (mlp_s[...] + vectors[5:6])
    result = jnp.where(live_scale > 0.0, result, 0.0).astype(low)
    if packed:
        pl.when(step > 0)(lambda: pass_on(step - 1))
    for slice_ in range(batch):
        put_block(slice_, dot(order_back[...], result[ROWS * slice_ : ROWS * (slice_ + 1)]).astype(low))

    grad_out = out_low_s[...].astype(wide)
    second_grad = second_grad_s[...]
    normed_two = normed2_s[...]
    small[5:6] += column_sum(grad_out)
    small[3:4] += column_sum(second_grad)
    small[2:3] += column_sum(second_grad * normed_two)
    middle_grad = grad_out + normalize_back(second_grad, normed_two, inv_two, vectors[2:3])
    small[4:5] += column_sum(middle_grad)
    middle_s[...] = middle_grad
    attn_low = middle_grad.astype(low)
    attended = jnp.concatenate([att_s[group] for group in range(4)], axis=1)
    proj_acc[...] += dot_tn(attended, attn_low)
    attended_grad = dot_nt(attn_low, rows_of(proj_w, C)).astype(low)
    for group in range(4):
        att_s[group] = attended_grad[:, 128 * group : 128 * (group + 1)]

    def attend_back(which, carry):
        pair, group = which // 4, which % 4
        bias_grad = None
        for slice_ in range(batch):
            rows = pl.ds(pl.multiple_of(slice_ * ROWS + pair * PAIR, 16), PAIR)
            attention = probs_s[slice_, which]
            keys, values = qkv_s[4 + group, rows], qkv_s[8 + group, rows]
            grads = stack_heads(att_s[group, rows], masks)
            queries = stack_heads(qkv_s[group, rows], masks)
            probs_grad = dot_nt(grads, values)
            row_term = jnp.sum(attention * probs_grad, axis=-1, keepdims=True)
            score_grad = (attention * (probs_grad - row_term)).astype(low)
            wide_grad = score_grad.astype(wide)
            bias_grad = wide_grad if bias_grad is None else bias_grad + wide_grad
            back_s[group, rows] = (pick_heads(dot(score_grad, keys)) * score_scale).astype(low)
            back_s[4 + group, rows] = (dot_tn(score_grad, queries) * score_scale).astype(low)
            back_s[8 + group, rows] = dot_tn(attention.astype(low), grads).astype(low)
        table_sum[group] += bias_grad
        return carry

    lax.fori_loop(0, 2, two_of(two_of(attend_back)), 0)
    first_in = first_s[...]
    first_grad = None
    for kind in range(3):
        back = jnp.concatenate([back_s[kind * 4 + group] for group in range(4)], axis=1)
        if kind != 1:
            row = 6 + kind // 2
            small[row : row + 1] += column_sum(back.astype(wide))
        qkv_acc[kind] += dot_tn(back, first_in)
        part = dot(back, qkv_w[kind])
        first_grad = part if first_grad is None else first_grad + part
    normed = normed_s[...]
    small[1:2] += column_sum(first_grad)
    small[0:1] += column_sum(first_grad * normed)
    token_grad = middle_s[...] + normalize_back(first_grad, normed, inv_one, vectors[0:1])
    token_low = token_grad.astype(low)
    for slice_ in range(batch):
        put_grad(slice_, dot(order_back[...], token_low[ROWS * slice_ : ROWS * (slice_ + 1)]).astype(low))

    def finish():
        if packed:
            pass_on(steps - 1)
        for kind in range(3):
            part = qkv_acc[kind].astype(low).reshape(HEADS, HD, C)
            if packed:
                out = grad_outs[0]
                for piece in range(2):
                    block = kind * 2 + piece
                    out[:, block // 3, pl.ds(16 * (block % 3), 16)] = part[:, 16 * piece : 16 * (piece + 1)]
            else:
                grad_outs[0][:, kind] = part
        if packed:
            out = grad_outs[0]
            out[:, :, pl.ds(48, 16)] = proj_acc[...].astype(low).reshape(16, 2, 16, C)
            out[:, :, pl.ds(64, 64)] = expand_acc[...].astype(low).reshape(16, 2, 64, C)
            out[:, :, pl.ds(128, 64)] = contract_acc[...].astype(low).reshape(16, 2, 64, C)
        else:
            grad_outs[1][...] = proj_acc[...].astype(low)
            grad_outs[2][...] = expand_acc[...].astype(low)
            grad_outs[3][...] = contract_acc[...].astype(low)
        if packed:

            def settle(image, carry):
                own_arrival(0, image).wait_recv()
                relay_arrival(image).wait_recv()
                own_copy(0, image).wait_send()
                own_copy(1, image).wait_send()
                relay(image).wait_send()
                keep_copy(image).wait()
                return carry

            lax.fori_loop(0, per_device, settle, 0)

    pl.when(step == steps - 1)(finish)


def run_layer(packed, per_device, place, images, cotangent, vectors, qv_bias, expand_bias, bias, weights):
    order_np = window_order()
    onehot = (order_np[:, None] == np.arange(TOK)[None, :]).astype(np.float32)
    order = jnp.asarray(onehot, low)
    order_back = jnp.asarray(onehot.T, low)
    any_spec = pl.BlockSpec(memory_space=pl.ANY)

    def whole(shape):
        return pl.BlockSpec(shape, lambda i, s: (0,) * len(shape), pipeline_mode=pl.Buffered(1))

    batch = 2 if per_device % 2 == 0 else 1
    span = batch * ROWS
    image_spec = pl.BlockSpec((batch, TOK, C), lambda i, s: (i, 0, 0))
    out_spec = any_spec if packed else image_spec
    images_out = IMG_DEV if packed else per_device
    exchange = [
        pltpu.VMEM((per_device, TOK, C), low),
        pltpu.SemaphoreType.DMA((per_device,)),
        pltpu.SemaphoreType.DMA((3, per_device)),
        pltpu.SemaphoreType.DMA((3, per_device)),
    ]
    limit = 60 * 1024 * 1024
    if packed:
        params = pltpu.CompilerParams(collective_id=3, has_side_effects=True, vmem_limit_bytes=limit)
    else:
        params = pltpu.CompilerParams(vmem_limit_bytes=limit)
    if packed:
        weights = (weights,) * 4
        grad_shapes = [(16, 2, 192, C)]
        weight_shapes = [(32, 48, C), (32, 16, C), (32, 64, C), (32, 64, C)]
    else:
        weights = (weights[0], weights[1], weights[2].reshape(FF // 64, 64, C), weights[3].reshape(FF // 64, 64, C))
        grad_shapes = [(HEADS, 3, HD, C), (C, C), (FF, C), (FF, C)]
        weight_shapes = [w.shape for w in weights]
    outs = pl.pallas_call(
        functools.partial(layer_kernel, packed, batch),
        out_shape=[
            jax.ShapeDtypeStruct((images_out, TOK, C), low),
            jax.ShapeDtypeStruct((per_device, TOK, C), low),
            *[jax.ShapeDtypeStruct(shape, low) for shape in grad_shapes],
            jax.ShapeDtypeStruct((16, C), wide),
            jax.ShapeDtypeStruct((4, GROUP * PAIR, PAIR), wide),
        ],
        grid_spec=pltpu.PrefetchScalarGridSpec(
            num_scalar_prefetch=1,
            grid=(per_device // batch,),
            in_specs=[
                image_spec, image_spec, whole((ROWS, TOK)), whole((TOK, ROWS)), whole((6, C)), whole((2, C)),
                whole((4, 1, C)), whole((2, 4, GROUP * PAIR, PAIR)), any_spec, any_spec, any_spec, any_spec,
            ],
            out_specs=[out_spec, image_spec]
            + [whole(shape) for shape in grad_shapes]
            + [whole((16, C)), whole((4, GROUP * PAIR, PAIR))],
            scratch_shapes=[pltpu.VMEM(shape, low) for shape in weight_shapes[:1]]
            + [pltpu.VMEM((3, C, C), low)]
            + [pltpu.VMEM(shape, low) for shape in weight_shapes[1:]]
            + [
                pltpu.VMEM((3, C, C), wide),
                pltpu.VMEM((C, C), wide),
                pltpu.VMEM((FF, C), wide),
                pltpu.VMEM((FF, C), wide),
                pltpu.VMEM((12, span, 128), low),
                pltpu.VMEM((4, span, 128), low),
                pltpu.VMEM((12, span, 128), low),
                pltpu.VMEM((batch, 8, GROUP * PAIR, PAIR), wide),
                pltpu.VMEM((span, C), wide),
                pltpu.VMEM((span, C), low),
                pltpu.VMEM((span, C), wide),
                pltpu.VMEM((span, C), wide),
                pltpu.VMEM((span, C), low),
                pltpu.VMEM((span, C), low),
                pltpu.VMEM((span, C), wide),
                pltpu.VMEM((span, C), wide),
                pltpu.SemaphoreType.DMA((4,)),
            ]
            + (exchange if packed else []),
        ),
        compiler_params=params,
        name="window_layer",
    )(place, images, cotangent, order, order_back, vectors, qv_bias, expand_bias.reshape(4, 1, C), bias, *weights)
    grads = outs[2 : 2 + len(grad_shapes)]
    grads = grads[0].reshape(32, 192, C) if packed else [g.reshape(-1, C) for g in grads]
    return outs[0], outs[1], grads, outs[-2], outs[-1]


def pair_bias(pos_bias, window_mask):
    heads = pos_bias.shape[0]
    scores = pos_bias[None] + window_mask[:, None]
    scores = scores.reshape(2, 2, heads, SPAN, SPAN)
    first = jnp.pad(scores[:, 0], ((0, 0), (0, 0), (0, 0), (0, PAIR - SPAN)), constant_values=away)
    second = jnp.pad(scores[:, 1], ((0, 0), (0, 0), (0, 0), (SPAN, PAIR - 2 * SPAN)), constant_values=away)
    rest = jnp.broadcast_to(
        jnp.where(jnp.arange(PAIR) < SPAN, 0.0, away).astype(wide), (2, heads, PAIR - 2 * SPAN, PAIR)
    )
    return jnp.concatenate([first, second, rest], axis=2).reshape(2, heads // GROUP, GROUP * PAIR, PAIR)


MESH = pl.DeviceIdType.MESH
DEPTH = 4


class Place:
    def __init__(self):
        dp_index, mp_index = lax.axis_index("dp"), lax.axis_index("mp")
        self.z, self.x = dp_index // 2, dp_index % 2
        self.y, self.core = mp_index // 2, mp_index % 2
        self.dp_index, self.mp_index = dp_index, mp_index
        self.x_side = self.device(self.z, 1 - self.x, self.y, self.core)
        self.y_side = self.device(self.z, self.x, 1 - self.y, self.core)
        self.partner = self.device(self.z, self.x, self.y, 1 - self.core)
        self.above = self.device(self.z + 1, self.x, self.y, self.core)
        self.below = self.device(self.z - 1, self.x, self.y, self.core)
        self.z_near = self.device(self.z + 1 - 2 * lax.rem(self.z, 2), self.x, self.y, self.core)
        self.z_far = self.device(lax.rem(self.z + 2, DEPTH), self.x, self.y, self.core)

    @staticmethod
    def device(z, x, y, core):
        return {"dp": z * 2 + x, "mp": y * 2 + core}

    @staticmethod
    def owner(z, x, y, core):
        return (y * 2 + core) * 8 + z * 2 + x

    def greet(self):
        barrier = pltpu.get_barrier_semaphore()

        def signal(device):
            pl.semaphore_signal(barrier, inc=1, device_id=device, device_id_type=MESH)

        signal(self.x_side)
        signal(self.y_side)
        signal(self.partner)
        pl.when(self.z > 0)(lambda: signal(self.below))
        pl.when(self.z < DEPTH - 1)(lambda: signal(self.above))
        ends = (self.z == 0).astype(jnp.int32) + (self.z == DEPTH - 1).astype(jnp.int32)
        pl.semaphore_wait(barrier, 5 - ends)


def remote(src, dst, send_sem, recv_sem, device):
    return pltpu.make_async_remote_copy(
        src_ref=src,
        dst_ref=dst,
        send_sem=send_sem,
        recv_sem=recv_sem,
        device_id=device,
        device_id_type=MESH,
    )


def spread(at, own_ref, out_ref, own_sem, z_send, z_recv, side_send, side_recv, pair_send, pair_recv):
    rows = own_ref.shape[0]
    half = rows // 2
    z, x, y, core = at.z, at.x, at.y, at.core
    low, high = pl.ds(0, half), pl.ds(half, rows - half)

    def slot(source_z, other_x, other_y):
        return out_ref.at[
            at.owner(source_z, 1 - x if other_x else x, 1 - y if other_y else y, core)
        ]

    def up(source_z, src=None):
        dst = slot(source_z, False, False)
        return remote(dst if src is None else src, dst, z_send.at[0, source_z], z_recv.at[0, source_z], at.above)

    def down(source_z, src=None):
        dst = slot(source_z, False, False)
        return remote(dst if src is None else src, dst, z_send.at[1, source_z], z_recv.at[1, source_z], at.below)

    def side(kind, source_z, src=None):
        if kind == 0 or kind == 1:
            dst = slot(source_z, False, False)
        elif kind == 2:
            dst = slot(source_z, True, False).at[low]
        else:
            dst = slot(source_z, False, True).at[high]
        device = at.x_side if kind in (0, 3) else at.y_side
        return remote(
            dst if src is None else src, dst, side_send.at[kind, source_z], side_recv.at[kind, source_z], device
        )

    def side_arrival(kind, source_z):
        if kind == 0:
            dst = slot(source_z, True, False)
        elif kind == 1:
            dst = slot(source_z, False, True)
        elif kind == 2:
            dst = slot(source_z, True, True).at[low]
        else:
            dst = slot(source_z, True, True).at[high]
        device = at.x_side if kind in (0, 3) else at.y_side
        return remote(dst, dst, side_send.at[kind, source_z], side_recv.at[kind, source_z], device)

    def pair_region(kind, source_z, of_core):
        other_x, other_y = ((False, False), (True, False), (False, True), (True, True), (True, True))[kind]
        ref = out_ref.at[at.owner(source_z, 1 - x if other_x else x, 1 - y if other_y else y, of_core)]
        if kind == 3:
            ref = ref.at[low]
        elif kind == 4:
            ref = ref.at[high]
        return ref

    def pair(kind, source_z, src=None):
        dst = pair_region(kind, source_z, core)
        return remote(
            dst if src is None else src, dst, pair_send.at[kind, source_z], pair_recv.at[kind, source_z], at.partner
        )

    def pair_arrival(kind, source_z):
        dst = pair_region(kind, source_z, 1 - core)
        return remote(dst, dst, pair_send.at[kind, source_z], pair_recv.at[kind, source_z], at.partner)

    keep = pltpu.make_async_copy(own_ref, slot(z, False, False), own_sem)
    pl.when(z < DEPTH - 1)(lambda: up(z, own_ref).start())
    pl.when(z > 0)(lambda: down(z, own_ref).start())
    side(0, z, own_ref).start()
    side(1, z, own_ref).start()
    pair(0, z, own_ref).start()
    keep.start()

    def plane(source_z):
        side_arrival(0, source_z).wait_recv()
        side(2, source_z).start()
        pair(1, source_z).start()
        side_arrival(1, source_z).wait_recv()
        side(3, source_z).start()
        pair(2, source_z).start()

    def column(source_z):
        side(0, source_z).start()
        side(1, source_z).start()
        pair(0, source_z).start()

    for distance in range(1, DEPTH + 1):

        def from_below(source_z=z - distance):
            up(source_z).wait_recv()
            pl.when(z < DEPTH - 1)(lambda: up(source_z).start())
            column(source_z)

        def from_above(source_z=z + distance):
            down(source_z).wait_recv()
            pl.when(z > 0)(lambda: down(source_z).start())
            column(source_z)

        pl.when(z - distance >= 0)(from_below)
        pl.when(z + distance <= DEPTH - 1)(from_above)
        past = distance - 1
        if past == 0:
            plane(z)
        else:
            pl.when(z - past >= 0)(functools.partial(plane, z - past))
            pl.when(z + past <= DEPTH - 1)(functools.partial(plane, z + past))

    def corner(source_z):
        side_arrival(2, source_z).wait_recv()
        pair(3, source_z).start()
        side_arrival(3, source_z).wait_recv()
        pair(4, source_z).start()

    for distance in range(DEPTH):
        if distance == 0:
            corner(z)
        else:
            pl.when(z - distance >= 0)(functools.partial(corner, z - distance))
            pl.when(z + distance <= DEPTH - 1)(functools.partial(corner, z + distance))
    keep.wait()
    for source_z in range(DEPTH):
        for kind in range(5):
            pair_arrival(kind, source_z).wait_recv()
            pair(kind, source_z).wait_send()
        for kind in range(4):
            side(kind, source_z).wait_send()
        pl.when((z < DEPTH - 1) & (source_z <= z))(lambda: up(source_z).wait_send())
        pl.when((z > 0) & (source_z >= z))(lambda: down(source_z).wait_send())


SPREAD_SEMS = [
    pltpu.SemaphoreType.DMA,
    pltpu.SemaphoreType.DMA((2, DEPTH)),
    pltpu.SemaphoreType.DMA((2, DEPTH)),
    pltpu.SemaphoreType.DMA((4, DEPTH)),
    pltpu.SemaphoreType.DMA((4, DEPTH)),
    pltpu.SemaphoreType.DMA((5, DEPTH)),
    pltpu.SemaphoreType.DMA((5, DEPTH)),
]


def gather_kernel(qkv_ref, proj_ref, expand_ref, contract_ref, misc_ref, out_ref, expand_bias, qv_bias, table,
                  own_ref, misc_out, misc_send, misc_recv, *sems):
    at = Place()
    start = 0
    for weight in (qkv_ref, proj_ref, expand_ref, contract_ref):
        own_ref[pl.ds(start, weight.shape[0])] = weight[...].astype(own_ref.dtype)
        start += weight.shape[0]
    at.greet()
    to_pair = remote(misc_ref, misc_out.at[at.mp_index], misc_send.at[0], misc_recv.at[0], at.partner)
    to_side = remote(misc_ref, misc_out.at[at.mp_index], misc_send.at[1], misc_recv.at[1], at.y_side)
    to_pair.start()
    to_side.start()
    misc_out[at.mp_index] = misc_ref[...]
    over = (1 - at.y) * 2 + at.core
    from_side = remote(misc_ref, misc_out.at[over], misc_send.at[1], misc_recv.at[1], at.y_side)
    relay = remote(misc_out.at[over], misc_out.at[over], misc_send.at[2], misc_recv.at[2], at.partner)
    spread(at, own_ref, out_ref, *sems)
    from_side.wait_recv()
    relay.start()
    beside = at.y * 2 + 1 - at.core
    remote(misc_ref, misc_out.at[beside], misc_send.at[0], misc_recv.at[0], at.partner).wait_recv()
    across = (1 - at.y) * 2 + 1 - at.core
    remote(misc_ref, misc_out.at[across], misc_send.at[2], misc_recv.at[2], at.partner).wait_recv()
    to_pair.wait_send()
    to_side.wait_send()
    relay.wait_send()
    for which in range(4):
        expand_bias[which] = misc_out[which, 0:1]
        for kind in range(2):
            qv_bias[kind : kind + 1, pl.ds(128 * which, 128)] = misc_out[which, 1:2, pl.ds(128 * kind, 128)]
        table[pl.ds(4 * which, 4)] = misc_out[which, 2:6, 0:256]


def gather_all(weights, misc):
    rows, columns = sum(weight.shape[0] for weight in weights), C
    vmem = pl.BlockSpec(memory_space=pltpu.VMEM)
    return pl.pallas_call(
        gather_kernel,
        out_shape=(
            jax.ShapeDtypeStruct((32, rows, columns), low),
            jax.ShapeDtypeStruct((4, 1, columns), wide),
            jax.ShapeDtypeStruct((2, columns), wide),
            jax.ShapeDtypeStruct((HEADS, 256), wide),
        ),
        in_specs=[vmem] * 5,
        out_specs=(pl.BlockSpec(memory_space=pl.ANY), vmem, vmem, vmem),
        scratch_shapes=[
            pltpu.VMEM((rows, columns), low),
            pltpu.VMEM((4,) + misc.shape, wide),
            pltpu.SemaphoreType.DMA((3,)),
            pltpu.SemaphoreType.DMA((3,)),
        ]
        + SPREAD_SEMS,
        compiler_params=pltpu.CompilerParams(collective_id=0, has_side_effects=True),
        name="gather_weights",
    )(*weights, misc)


def collect(at, grads, total_ref, mine, pair_buf, corner_x, corner_y, full_x, full_y, z_up, z_down, z_out,
            load_sem, pair_send, pair_recv, side_send, side_recv, z_send, z_recv):
    rows = total_ref.shape[0]
    half = rows // 2
    z, x, y, core = at.z, at.x, at.y, at.core
    low, high = pl.ds(0, half), pl.ds(half, rows - half)
    orders = ((3, 2, 1, 0), (3, 0, 2, 1), (0, 3, 1, 2), (0, 1, 2, 3))

    def turn(step):
        choice = jnp.int32(orders[3][step])
        for which in range(3):
            choice = jnp.where(z == which, jnp.int32(orders[which][step]), choice)
        return choice

    turns = [turn(step) for step in range(DEPTH)]

    def load(target, y_of):
        return pltpu.make_async_copy(
            grads.at[y_of * 2 + core, target], mine.at[y_of, target], load_sem.at[y_of, target]
        )

    def pair(target, y_of):
        return remote(
            grads.at[y_of * 2 + 1 - core, target], pair_buf.at[y_of, target],
            pair_send.at[y_of, target], pair_recv.at[y_of, target], at.partner,
        )

    def corner(kind, target):
        part = mine.at[1 - y, target, 1 - x]
        if kind == 0:
            return remote(part.at[low], corner_y.at[target], side_send.at[0, target], side_recv.at[0, target], at.y_side)
        return remote(part.at[high], corner_x.at[target], side_send.at[1, target], side_recv.at[1, target], at.x_side)

    def full(kind, target):
        if kind == 2:
            return remote(mine.at[y, target, 1 - x], full_x.at[target], side_send.at[2, target], side_recv.at[2, target], at.x_side)
        return remote(mine.at[1 - y, target, x], full_y.at[target], side_send.at[3, target], side_recv.at[3, target], at.y_side)

    def up(target):
        return remote(z_out.at[target], z_up.at[target], z_send.at[target], z_recv.at[0, target], at.above)

    def down(target):
        return remote(z_out.at[target], z_down.at[target], z_send.at[target], z_recv.at[1, target], at.below)

    wide = jnp.float32
    for target in turns:
        for y_of in (0, 1):
            pair(target, y_of).start()
            load(target, y_of).start()

    def first(target):
        for y_of in (0, 1):
            load(target, y_of).wait()
            pair(target, y_of).wait_recv()

        def add(which, carry):
            y_of, x_of = which // 2, which % 2
            mine[y_of, target, x_of] = (
                mine[y_of, target, x_of].astype(wide) + pair_buf[y_of, target, x_of].astype(wide)
            ).astype(mine.dtype)
            return carry

        lax.fori_loop(0, 4, add, 0)
        corner(0, target).start()
        corner(1, target).start()

    def second(target):
        corner(0, target).wait_recv()
        mine[y, target, 1 - x, low] = (
            mine[y, target, 1 - x, low].astype(wide) + corner_y[target].astype(wide)
        ).astype(mine.dtype)
        full(2, target).start()
        corner(1, target).wait_recv()
        mine[1 - y, target, x, high] = (
            mine[1 - y, target, x, high].astype(wide) + corner_x[target].astype(wide)
        ).astype(mine.dtype)
        full(3, target).start()

    def third(target, last):
        full(2, target).wait_recv()
        full(3, target).wait_recv()
        total_ref[...] = mine[y, target, x].astype(wide) + (
            full_x[target].astype(wide) + full_y[target].astype(wide)
        )

        def add_below():
            up(target).wait_recv()
            total_ref[...] += z_up[target].astype(wide)

        def add_above():
            down(target).wait_recv()
            total_ref[...] += z_down[target].astype(wide)

        pl.when((target >= z) & (z > 0))(add_below)
        pl.when((target <= z) & (z < DEPTH - 1))(add_above)
        if not last:
            z_out[target] = total_ref[...].astype(z_out.dtype)
            pl.when(target > z)(lambda: up(target).start())
            pl.when(target < z)(lambda: down(target).start())

    for step in range(DEPTH + 2):
        if step < DEPTH:
            first(turns[step])
        if 1 <= step <= DEPTH:
            second(turns[step - 1])
        if step >= 2:
            third(turns[step - 2], step - 2 == DEPTH - 1)
    for target in range(DEPTH):
        for y_of in (0, 1):
            pair(target, y_of).wait_send()
        for kind in (0, 1):
            corner(kind, target).wait_send()
        for kind in (2, 3):
            full(kind, target).wait_send()
        pl.when(target != z)(lambda: up(target).wait_send())


def collect_scratch(rows, columns, dtype):
    return [
        pltpu.VMEM((2, DEPTH, 2, rows, columns), dtype),
        pltpu.VMEM((2, DEPTH, 2, rows, columns), dtype),
        pltpu.VMEM((DEPTH, rows // 2, columns), dtype),
        pltpu.VMEM((DEPTH, rows // 2, columns), dtype),
        pltpu.VMEM((DEPTH, rows, columns), dtype),
        pltpu.VMEM((DEPTH, rows, columns), dtype),
        pltpu.VMEM((DEPTH, rows, columns), dtype),
        pltpu.VMEM((DEPTH, rows, columns), dtype),
        pltpu.VMEM((DEPTH, rows, columns), dtype),
        pltpu.SemaphoreType.DMA((2, DEPTH)),
        pltpu.SemaphoreType.DMA((2, DEPTH)),
        pltpu.SemaphoreType.DMA((2, DEPTH)),
        pltpu.SemaphoreType.DMA((4, DEPTH)),
        pltpu.SemaphoreType.DMA((4, DEPTH)),
        pltpu.SemaphoreType.DMA((DEPTH,)),
        pltpu.SemaphoreType.DMA((2, DEPTH)),
    ]


N_COLLECT = 16


def muon_kernel(grads, qkv_ref, proj_ref, expand_ref, contract_ref, grad_out, moment_out, next_all,
                own_next, *scratch):
    at = Place()
    at.greet()
    collect(at, grads, grad_out, *scratch[:N_COLLECT])
    start = 0
    for moment_ref in (qkv_ref, proj_ref, expand_ref, contract_ref):
        rows = pl.ds(start, moment_ref.shape[0])
        grad = grad_out[rows]
        moment = muon_beta * moment_ref[...] + grad
        moment_out[rows] = moment
        own_next[rows] = (grad + muon_beta * moment).astype(own_next.dtype)
        start += moment_ref.shape[0]
    spread(at, own_next, next_all, *scratch[N_COLLECT:])


def muon_exchange(grads, moments):
    rows, columns = sum(moment.shape[0] for moment in moments), C
    shape = jax.ShapeDtypeStruct((rows, columns), jnp.float32)
    vmem = pl.BlockSpec(memory_space=pltpu.VMEM)
    hbm = pl.BlockSpec(memory_space=pl.ANY)
    return pl.pallas_call(
        muon_kernel,
        out_shape=(shape, shape, jax.ShapeDtypeStruct((32, rows, columns), jnp.bfloat16)),
        in_specs=[hbm] + [vmem] * 4,
        out_specs=(vmem, vmem, hbm),
        scratch_shapes=[pltpu.VMEM((rows, columns), jnp.bfloat16)]
        + collect_scratch(rows, columns, jnp.bfloat16)
        + SPREAD_SEMS,
        compiler_params=pltpu.CompilerParams(
            collective_id=1, has_side_effects=True, vmem_limit_bytes=40 * 1024 * 1024
        ),
        name="muon_exchange",
    )(grads.reshape(4, DEPTH, 2, rows, columns), *moments)


def ns_kernel(next_all, own_images, small_ref, swapped, images_all, small_out,
              products, rows_buf, map_buf, gram_buf, total_buf, small_parts, small_in, sem, keep_sem,
              act_send, act_recv, small_send, small_recv, swap_send, swap_recv):
    at = Place()
    mp_index, dp_index = at.mp_index, at.dp_index
    counts = (48, 16, 64, 64)
    pieces = own_images.shape[0]
    over = (1 - at.y) * 2 + at.core
    across = (1 - at.y) * 2 + 1 - at.core
    beside = at.y * 2 + 1 - at.core
    mp_peers = [{"dp": dp_index, "mp": lax.rem(mp_index + shift, 4)} for shift in (1, 2, 3)]
    small_peers = (at.y_side, at.partner, at.x_side, at.z_near, at.z_far)
    barrier = pltpu.get_barrier_semaphore()
    for device in (*mp_peers, at.x_side, at.z_near, at.z_far):
        pl.semaphore_signal(barrier, inc=1, device_id=device, device_id_type=MESH)

    def fetch(which):
        count = counts[which]
        copy = pltpu.make_async_copy(
            next_all.at[:, pl.ds(sum(counts[:which]), count)], rows_buf.at[:, pl.ds(0, count)], sem
        )
        copy.start()
        if count < 64:
            rows_buf[:, pl.ds(count, 64 - count)] = jnp.zeros((32, 64 - count, C), rows_buf.dtype)
        copy.wait()

    pl.semaphore_wait(barrier, 6)

    def slot(of_mp, image):
        return images_all.at[of_mp * pieces + image]

    def keep_copy(image):
        return pltpu.make_async_copy(own_images.at[image], slot(mp_index, image), keep_sem.at[image])

    def own_copy(which, image):
        device = (at.partner, at.y_side)[which]
        return remote(
            own_images.at[image], slot(mp_index, image), act_send.at[which, image], act_recv.at[which, image], device
        )

    def own_arrival(which, image):
        source, device = ((beside, at.partner), (over, at.y_side))[which]
        return remote(
            own_images.at[image], slot(source, image), act_send.at[which, image], act_recv.at[which, image], device
        )

    def relay(image):
        return remote(slot(over, image), slot(over, image), act_send.at[2, image], act_recv.at[2, image], at.partner)

    def relay_arrival(image):
        return remote(
            slot(across, image), slot(across, image), act_send.at[2, image], act_recv.at[2, image], at.partner
        )

    def small_copy(stage):
        source = small_ref if stage == 0 else small_parts.at[stage - 1]
        return remote(source, small_in.at[stage], small_send.at[stage], small_recv.at[stage], small_peers[stage])

    def small_step(stage):
        small_copy(stage).wait_recv()
        held = small_ref[...] if stage == 0 else small_parts[stage - 1]
        held = held + small_in[stage]
        if stage < 4:
            small_parts[stage] = held
            small_copy(stage + 1).start()
        else:
            small_out[...] = held

    small_copy(0).start()
    for image in range(pieces):
        own_copy(1, image).start()
    for image in range(pieces):
        own_copy(0, image).start()
        keep_copy(image).start()

    for which in range(4):
        pl.when(mp_index == which)(functools.partial(fetch, which))

    gram = None
    for part in range(4):
        block = rows_buf[8 * part : 8 * (part + 1)].reshape(512, C)
        term = dot_tn(block, block)
        gram = term if gram is None else gram + term
    eye = (
        lax.broadcasted_iota(jnp.int32, (C, C), 0) == lax.broadcasted_iota(jnp.int32, (C, C), 1)
    ).astype(wide)
    norm_value = jnp.sqrt(jnp.sum(jnp.sum(gram * eye, axis=1, keepdims=True), axis=0, keepdims=True)) + ns_eps
    gram = gram / (norm_value * norm_value)

    def dot_high(a, b):
        return jnp.dot(a, b, precision=lax.Precision.HIGH, preferred_element_type=wide)

    def pass_on(image):
        own_arrival(1, image).wait_recv()
        relay(image).start()

    def poly_of(gram):
        square = dot_high(gram, gram)
        return coef_a * eye + (coef_b * gram + coef_c * square)

    gram_buf[...] = gram
    poly = poly_of(gram)
    total_buf[...] = poly
    gram_buf[...] = dot_high(dot_high(gram, poly), poly)
    pl.when(at.z >= 0)(functools.partial(small_step, 0))

    def iterate(iteration, carry):
        gram = gram_buf[...]
        poly = poly_of(gram)
        total_buf[...] = dot_high(total_buf[...], poly)
        gram_buf[...] = dot_high(dot_high(gram, poly), poly)
        for which in range(1, NS_ITERS - 1):
            pl.when(iteration == which)(functools.partial(small_step, which))
        return carry

    lax.fori_loop(1, NS_ITERS - 1, iterate, 0)
    total = dot_high(total_buf[...], poly_of(gram_buf[...]))
    pl.when(at.z >= 0)(functools.partial(small_step, NS_ITERS - 1))
    map_buf[...] = total / norm_value

    def swap_copy(which):
        return remote(
            products.at[lax.rem(mp_index + which + 1, 4)], swapped.at[mp_index],
            swap_send.at[which], swap_recv.at[which], mp_peers[which],
        )

    for group in range(4):
        rows = rows_buf[group * 8 + dp_index].astype(wide)
        products[group] = dot_high(rows, map_buf[...]).astype(products.dtype)
    for which in (1, 2, 0):
        swap_copy(which).start()
    swapped[mp_index] = products[mp_index]
    for image in range(pieces):
        pass_on(image)
    for image in range(pieces):
        own_arrival(0, image).wait_recv()
        relay_arrival(image).wait_recv()
        own_copy(0, image).wait_send()
        own_copy(1, image).wait_send()
        relay(image).wait_send()
        keep_copy(image).wait()
    for which in range(3):
        source = lax.rem(mp_index + 3 - which, 4)
        remote(
            products.at[source], swapped.at[source], swap_send.at[which], swap_recv.at[which],
            {"dp": dp_index, "mp": source},
        ).wait_recv()
        swap_copy(which).wait_send()
    for stage in range(5):
        small_copy(stage).wait_send()


def newton_schulz_rows(next_all, own_images, small):
    vmem = pl.BlockSpec(memory_space=pltpu.VMEM)
    hbm = pl.BlockSpec(memory_space=pl.ANY)
    pieces = own_images.shape[0]
    return pl.pallas_call(
        ns_kernel,
        out_shape=(
            jax.ShapeDtypeStruct((4, 64, C), low),
            jax.ShapeDtypeStruct((4 * pieces,) + own_images.shape[1:], low),
            jax.ShapeDtypeStruct(small.shape, wide),
        ),
        in_specs=[hbm, vmem, vmem],
        out_specs=(vmem, hbm, vmem),
        scratch_shapes=[
            pltpu.VMEM((4, 64, C), low),
            pltpu.VMEM((32, 64, C), low),
            pltpu.VMEM((C, C), wide),
            pltpu.VMEM((C, C), wide),
            pltpu.VMEM((C, C), wide),
            pltpu.VMEM((4,) + small.shape, wide),
            pltpu.VMEM((5,) + small.shape, wide),
            pltpu.SemaphoreType.DMA,
            pltpu.SemaphoreType.DMA((pieces,)),
            pltpu.SemaphoreType.DMA((3, pieces)),
            pltpu.SemaphoreType.DMA((3, pieces)),
            pltpu.SemaphoreType.DMA((5,)),
            pltpu.SemaphoreType.DMA((5,)),
            pltpu.SemaphoreType.DMA((3,)),
            pltpu.SemaphoreType.DMA((3,)),
        ],
        compiler_params=pltpu.CompilerParams(
            collective_id=2, has_side_effects=True, vmem_limit_bytes=40 * 1024 * 1024
        ),
        name="newton_schulz",
    )(next_all, own_images, small)


def update_kernel(grads, moments, swapped, *refs):
    weights, outs = refs[:4], refs[4:]
    factors = (math.sqrt(3.0), 1.0, math.sqrt(max(1.0, FF / C)), 1.0)
    start = 0
    for which in range(4):
        count = weights[which].shape[0]
        rows = pl.ds(start, count)
        outs[which][...] = grads[rows]
        outs[4 + which][...] = moments[rows]
        part = swapped[which, pl.ds(0, count)].astype(wide)
        outs[8 + which][...] = -muon_rate * (muon_decay * weights[which][...] + factors[which] * part)
        start += count


def update_shards(grads, moments, swapped, weights):
    vmem = pl.BlockSpec(memory_space=pltpu.VMEM)
    shapes = [jax.ShapeDtypeStruct(weight.shape, wide) for weight in weights] * 3
    return pl.pallas_call(
        update_kernel,
        out_shape=shapes,
        in_specs=[vmem] * 7,
        out_specs=[vmem] * 12,
        name="update_shards",
    )(grads, moments, swapped, *weights)


def split_low(values):
    high = lax.reduce_precision(values, exponent_bits=8, mantissa_bits=7)
    return high.astype(jnp.bfloat16), (values - high).astype(jnp.bfloat16)


def dot_three(left, right):
    left_high, left_rest = left
    right_high, right_rest = right
    wide = dict(preferred_element_type=jnp.float32)
    return (
        jnp.dot(left_rest, right_high, **wide)
        + jnp.dot(left_high, right_rest, **wide)
        + jnp.dot(left_high, right_high, **wide)
    )


def newton_schulz(gram):
    width = gram.shape[0]
    eye = jnp.eye(width, dtype=jnp.float32)
    norm_value = jnp.sqrt(jnp.sum(gram * eye)) + ns_eps
    gram = gram / (norm_value * norm_value)
    total = None
    for iteration in range(NS_ITERS):
        parts = split_low(gram)
        square = dot_three(parts, parts)
        poly = coef_a * eye + (coef_b * gram + coef_c * square)
        poly_parts = split_low(poly)
        total = poly if total is None else dot_three(split_low(total), poly_parts)
        if iteration + 1 < NS_ITERS:
            half = dot_three(parts, poly_parts)
            gram = dot_three(split_low(half), poly_parts)
    return total / norm_value


def adam_update(grad_sum, first_moment, second_moment):
    first_new = adam_one * first_moment + (1.0 - adam_one) * grad_sum
    second_new = adam_two * second_moment + (1.0 - adam_two) * grad_sum * grad_sum
    first_hat = first_new / (1.0 - adam_one**adam_step)
    second_hat = second_new / (1.0 - adam_two**adam_step)
    return (-adam_rate * first_hat / (jnp.sqrt(second_hat) + adam_eps), first_new, second_new)


def exchange_plain(own_low, own_moments, rows):
    everyone = ("mp", "dp")
    starts = [sum(rows[:which]) for which in range(4)]

    def cut(stacked):
        return [stacked[:, start : start + count] for start, count in zip(starts, rows)]

    gathered = [
        part.reshape(-1, C) for part in cut(lax.all_gather(own_low, everyone, axis=0, tiled=False))
    ]

    def finish(big_local):
        mp_size, dp_size = lax.axis_size("mp"), lax.axis_size("dp")
        mp_index, dp_index = lax.axis_index("mp"), lax.axis_index("dp")
        devices = mp_size * dp_size
        stacked_grads = jnp.concatenate(
            [grad.reshape(devices, count, C) for grad, count in zip(big_local, rows)], axis=1
        )
        own_grads = lax.psum_scatter(
            stacked_grads.reshape(devices * sum(rows), C), everyone, scatter_dimension=0, tiled=True
        ).astype(wide)
        own_buffers = muon_beta * own_moments + own_grads
        own_nesterov = own_grads + muon_beta * own_buffers
        iterate_all = lax.all_gather(own_nesterov.astype(low), everyone, axis=0, tiled=False)
        grams = jnp.stack([dot_tn(part.reshape(-1, C), part.reshape(-1, C)) for part in cut(iterate_all)])
        ortho_map = newton_schulz(lax.dynamic_index_in_dim(grams, mp_index, 0, keepdims=False))
        most = max(rows)
        picked = lax.dynamic_slice(
            iterate_all.reshape(mp_size, dp_size, sum(rows), C),
            (
                jnp.int32(0),
                dp_index.astype(jnp.int32),
                jnp.array(starts, jnp.int32)[mp_index],
                jnp.int32(0),
            ),
            (mp_size, 1, most, C),
        ).reshape(mp_size * most, C)
        map_parts = split_low(ortho_map)
        products = dot(picked, map_parts[0]) + dot(picked, map_parts[1])
        swapped = lax.all_to_all(products.reshape(mp_size, most, C), "mp", 0, 0, tiled=False)
        return own_grads, own_buffers, swapped

    return gathered, finish


def shards(
    images,
    cotangent,
    qkv_weight,
    proj_weight,
    expand_weight,
    contract_weight,
    qkv_moment,
    proj_moment,
    expand_moment,
    contract_moment,
    vectors,
    qv_bias,
    expand_bias,
    rel_table,
    vectors_first,
    vectors_second,
    qv_first,
    qv_second,
    expand_bias_first,
    expand_bias_second,
    table_first,
    table_second,
    region_ids,
    pos_index,
    image_counts,
):
    everyone = ("mp", "dp")
    mp_size, dp_size = lax.axis_size("mp"), lax.axis_size("dp")
    mp_index = lax.axis_index("mp")
    linked = mp_size == 4 and dp_size == 8
    per_device = IMG_DEV // mp_size
    first_image = (mp_index * per_device).astype(jnp.int32)
    place = jnp.stack([first_image, image_counts[0]])
    own_images = lax.dynamic_slice_in_dim(images, first_image, per_device, 0)
    own_cotangent = lax.dynamic_slice_in_dim(cotangent, first_image, per_device, 0)
    weights_all = (qkv_weight, proj_weight, expand_weight, contract_weight)
    rows = [weight.shape[0] for weight in weights_all]
    starts = [sum(rows[:which]) for which in range(4)]
    moments = (qkv_moment, proj_moment, expand_moment, contract_moment)
    if linked:
        misc = jnp.concatenate(
            [
                expand_bias[None],
                jnp.pad(qv_bias.reshape(1, -1), ((0, 0), (0, C - qv_bias.size))),
                jnp.pad(rel_table.T, ((0, 2), (0, C - TABLE))),
            ],
            axis=0,
        )
        gathered, expand_full, qv_full, table_wide = gather_all(weights_all, misc)
        table_full = table_wide[:, :TABLE]
    else:
        own_low = jnp.concatenate([weight.astype(low) for weight in weights_all], axis=0)
        own_moments = jnp.concatenate(moments, axis=0)
        gathered, finish_plain = exchange_plain(own_low, own_moments, rows)
        qv_full = lax.all_gather(qv_bias, "mp", axis=1, tiled=True)
        expand_full = lax.all_gather(expand_bias, "mp", axis=0, tiled=True).reshape(4, C)
        table_full = lax.all_gather(rel_table.T, "mp", axis=0, tiled=True)
    onehot = (
        jnp.arange(TABLE, dtype=jnp.int32)[:, None] == pos_index.reshape(1, SPAN * SPAN)
    ).astype(wide)
    pos_bias = jnp.dot(table_full, onehot, precision=highest).reshape(HEADS, SPAN, SPAN)
    window_regions = to_windows(region_ids.reshape(1, TOK, 1))[:, :, 0]
    window_mask = jnp.where(
        window_regions[:, :, None] != window_regions[:, None, :], mask_value, 0.0
    ).astype(wide)
    bias = pair_bias(pos_bias, window_mask)
    block_low, input_low, big_local, small_rows, table_pairs = run_layer(
        linked, per_device, place, own_images, own_cotangent, vectors, qv_full, expand_full, bias, gathered
    )
    if linked:
        block_out = block_low
    else:
        block_out = lax.all_gather(block_low, "mp", axis=0, tiled=True)
        input_grad = lax.all_gather(input_low, "mp", axis=0, tiled=True)
    pairs = table_pairs.reshape(HEADS, PAIR, PAIR)
    bias_heads = pairs[:, :SPAN, :SPAN] + pairs[:, SPAN : 2 * SPAN, SPAN : 2 * SPAN]
    table_local = lax.dot_general(
        bias_heads.reshape(HEADS, SPAN * SPAN),
        onehot,
        (((1,), (1,)), ((), ())),
        precision=highest,
        preferred_element_type=wide,
    )
    if linked:
        small_own = jnp.concatenate(
            [small_rows, jnp.pad(table_local, ((0, 0), (0, C - TABLE)))], axis=0
        )
        own_grads, own_buffers, next_all = muon_exchange(big_local, moments)
        swapped, input_grad, small_all = newton_schulz_rows(next_all, input_low, small_own)
        small_full, table_all = small_all[:HEADS], small_all[HEADS:, :TABLE]
    else:
        small_full, table_all = lax.psum((small_rows, table_local), everyone)
        own_grads, own_buffers, swapped = finish_plain(big_local)
    updated = update_shards(own_grads, own_buffers, swapped, weights_all)
    shares, buffers, new_steps = updated[:4], updated[4:8], updated[8:]

    def own_columns(full, width):
        return lax.dynamic_slice_in_dim(full, mp_index * width, width, full.ndim - 1)

    small_sums = (
        small_full[:6],
        own_columns(small_full[6:8], qv_bias.shape[1]),
        own_columns(small_full[8:12].reshape(FF), expand_bias.shape[0]),
        lax.dynamic_slice_in_dim(table_all, mp_index * rel_table.shape[1], rel_table.shape[1], 0).T,
    )
    vectors_step, vectors_first_new, vectors_second_new = adam_update(
        small_sums[0], vectors_first, vectors_second
    )
    qv_step, qv_first_new, qv_second_new = adam_update(small_sums[1], qv_first, qv_second)
    expand_bias_step, expand_bias_first_new, expand_bias_second_new = adam_update(
        small_sums[2], expand_bias_first, expand_bias_second
    )
    table_step, table_first_new, table_second_new = adam_update(
        small_sums[3], table_first, table_second
    )
    return (
        block_out,
        input_grad,
        shares[0],
        shares[1],
        shares[2],
        shares[3],
        small_sums[0],
        small_sums[1],
        small_sums[2],
        small_sums[3],
        new_steps[0],
        new_steps[1],
        new_steps[2],
        new_steps[3],
        buffers[0],
        buffers[1],
        buffers[2],
        buffers[3],
        vectors_step,
        qv_step,
        expand_bias_step,
        table_step,
        vectors_first_new,
        vectors_second_new,
        qv_first_new,
        qv_second_new,
        expand_bias_first_new,
        expand_bias_second_new,
        table_first_new,
        table_second_new,
    )


def solution(mesh):
    return jax.shard_map(
        shards,
        mesh=mesh,
        in_specs=(
            P("dp", None, None),
            P("dp", None, None),
            P(("mp", "dp"), None),
            P(("mp", "dp"), None),
            P(("mp", "dp"), None),
            P(("mp", "dp"), None),
            P(("mp", "dp"), None),
            P(("mp", "dp"), None),
            P(("mp", "dp"), None),
            P(("mp", "dp"), None),
            P(),
            P(None, "mp"),
            P("mp"),
            P(None, "mp"),
            P(),
            P(),
            P(None, "mp"),
            P(None, "mp"),
            P("mp"),
            P("mp"),
            P(None, "mp"),
            P(None, "mp"),
            P(),
            P(),
            P("dp"),
        ),
        out_specs=(
            P("dp", None, None),
            P("dp", None, None),
            P(("mp", "dp"), None),
            P(("mp", "dp"), None),
            P(("mp", "dp"), None),
            P(("mp", "dp"), None),
            P(),
            P(None, "mp"),
            P("mp"),
            P(None, "mp"),
            P(("mp", "dp"), None),
            P(("mp", "dp"), None),
            P(("mp", "dp"), None),
            P(("mp", "dp"), None),
            P(("mp", "dp"), None),
            P(("mp", "dp"), None),
            P(("mp", "dp"), None),
            P(("mp", "dp"), None),
            P(),
            P(None, "mp"),
            P("mp"),
            P(None, "mp"),
            P(),
            P(),
            P(None, "mp"),
            P(None, "mp"),
            P("mp"),
            P("mp"),
            P(None, "mp"),
            P(None, "mp"),
        ),
        check_vma=False,
    )
```
